32 devices in a mesh: aux: 8 (over y, x, core), orb: 4 (over z).
Axes of the slice: x: 2, y: 2, z: 4, core: 2. Of those that a mesh axis runs over, the one named last changes fastest.
Arguments:
- tiles: float32 [256, 64, 4096], P(('aux', 'orb')), may hold values from -6 to 6
- tile_list: int32 [4, 256], P(None, ('aux', 'orb')), may hold values from 0 to 255, as said below
- orb_factor: float32 [4096, 256], P('orb'), may hold values from -30 to 30
- nu_factor: float32 [512, 256], replicated, may hold values from -30 to 30
Outputs:
- aux_factor: float32 [16384, 256], P('aux')
- orb_updated: float32 [4096, 256], P('orb')
- nu_updated: float32 [512, 256], replicated
The draws below stay inside these ranges and needn't reach their ends.
Inputs may be any that keep to these rules, and one draw needn't show every extreme that they name: `tile_list`: slot s belongs to the device s // 8 along aux+orb; for that device with aux index a and orb index o, row 0 lies in [a * 32, (a + 1) * 32), row 1 in [o * 16, (o + 1) * 16), row 2 below 8. The coordinates of one device's slots are distinct. Row 3 is 0 or 1: 1 on a device's first slots and 0 on the rest; every device has at least one flagged slot and some device has all 8 flagged.
All inputs are finite; a program needn't handle non-finite values.
Results may differ from the reference program's by a relative error of at most 0.0003.
Values sent between devices are 32-bit elements; how exact they have to be, the bound alone decides.
A program may use at most 256 MiB of HBM per device.

```python
import jax
import jax.numpy as jnp
from jax import lax

P_SIZE = 16384
MU = 4096
NU = 512
R = 256
TILE = 64
TILES_DEV = 8
NTILES = 256
BLOCK_P = 32
BLOCK_M = 16


def factor_draw(key, row_count):
    key_list = jax.random.split(key, 4)
    noise_part = jnp.clip(jax.random.normal(key_list[0], (row_count, R), jnp.float32), -4.0, 4.0)
    shared = jnp.clip(jax.random.normal(key_list[1], (row_count, 12), jnp.float32), -4.0, 4.0)
    amplitudes = jax.random.uniform(key_list[2], (12, 1), jnp.float32, 0.3, 1.5)
    mixing = jax.random.normal(key_list[3], (12, R), jnp.float32) * amplitudes
    values = noise_part + jnp.dot(shared, mixing, preferred_element_type=jnp.float32)
    return jnp.clip(values, -30.0, 30.0)


def draw_orb_factor(key, part):
    return factor_draw(jax.random.fold_in(key, 11), MU)


def draw_nu_factor(key, part):
    return factor_draw(jax.random.fold_in(key, 13), NU)


def draw_tile_list(key, part):
    devices_all = NTILES // TILES_DEV
    orb_span = MU // TILE // BLOCK_M
    nu_tiles = NU // TILE
    region = BLOCK_P * BLOCK_M * nu_tiles
    key_list = jax.random.split(jax.random.fold_in(key, 7), 4)

    def pick_cells(device_key):
        return jax.random.permutation(device_key, region)[:TILES_DEV]
    cell_ids = jax.vmap(pick_cells)(jax.random.split(key_list[0], devices_all)).astype(jnp.int32)
    device_ids = jnp.arange(devices_all, dtype=jnp.int32)[:, None]
    shifted = (cell_ids + (region - 1 - cell_ids[:, :1])) % region
    is_last = device_ids == devices_all - 1
    cell_ids = jnp.where(is_last, shifted, cell_ids).astype(jnp.int32)
    first_tile = device_ids // orb_span * BLOCK_P + cell_ids // (BLOCK_M * nu_tiles)
    second_tile = device_ids % orb_span * BLOCK_M + cell_ids // nu_tiles % BLOCK_M
    third_tile = cell_ids % nu_tiles
    top_count = max(1, TILES_DEV // 2)
    counts = jax.random.randint(key_list[1], (devices_all, 1), 1, top_count + 1)
    picked_full = jax.random.randint(key_list[2], (devices_all, 1), 0, 8) == 0
    chosen = jax.random.randint(key_list[3], (), 0, devices_all)
    filled = picked_full | (device_ids == chosen)
    counts = jnp.where(filled, TILES_DEV, counts)
    slot_ids = jnp.arange(TILES_DEV, dtype=jnp.int32)[None, :]
    live_flags = (slot_ids < counts).astype(jnp.int32)
    stacked = jnp.stack([first_tile, second_tile, third_tile, live_flags])
    return stacked.reshape(4, NTILES).astype(jnp.int32)


def levels(stream_key, dims, pieces, least, top_value):
    gain, own = 1.0, jax.random.fold_in(stream_key, 6)
    for position, parts in pieces:
        draws = jnp.exp(jax.random.uniform(jax.random.fold_in(own, position), (parts,), jnp.float32, least / len(pieces), top_value / len(pieces)))
        gain = gain * jnp.repeat(draws, dims[position] // parts).reshape([-1 if axis == position else 1 for axis in range(len(dims))])
    return gain


def gaussian(key, dims, spread, limit, cuts=(), kind=jnp.bfloat16):
    factor_of = levels(key, dims, cuts, -0.22, 0.18) if cuts else 1.0
    result = jax.random.normal(key, dims, jnp.float32) * spread * factor_of
    return jnp.minimum(jnp.maximum(result, -limit), limit).astype(kind)


def setup_inputs(seed: int = 0) -> dict:
    key_of = jax.random.split(jax.random.key(seed), 5)
    tiles = gaussian(key_of[0], (NTILES, TILE, TILE * TILE), 1.0, 6.0, ((0, 32),), jnp.float32)
    tile_list = draw_tile_list(jax.random.fold_in(key_of[4], 71), 0)
    orb_factor = draw_orb_factor(jax.random.fold_in(key_of[4], 71), 0)
    nu_factor = draw_nu_factor(jax.random.fold_in(key_of[4], 71), 0)
    return {"tiles": tiles, "tile_list": tile_list, "orb_factor": orb_factor, "nu_factor": nu_factor}


ridge_weight = 0.5
epsilon = 1e-06
highest = lax.Precision.HIGHEST

def gram_of(matrix):
    return jnp.dot(matrix.T.astype(jnp.float32), matrix.astype(jnp.float32), precision=highest, preferred_element_type=jnp.float32)

def solve_rows(system, targets):
    factor_lower = jnp.linalg.cholesky(system)
    return jax.scipy.linalg.cho_solve((factor_lower, True), targets.T).T

def add_rows(running, addition, start):
    previous = lax.dynamic_slice_in_dim(running, start, addition.shape[0], 0)
    return lax.dynamic_update_slice_in_dim(running, previous + addition, start, 0)

def mode_first(tiles, tile_list, orb_factor, nu_factor):

    def tile_step(running, tile_item):
        tile_block, coords = tile_item
        nu_block = lax.dynamic_slice_in_dim(nu_factor, (coords[2] * TILE).astype(jnp.int32), TILE, 0)
        orb_block = lax.dynamic_slice_in_dim(orb_factor, (coords[1] * TILE).astype(jnp.int32), TILE, 0)
        contracted = jnp.dot(tile_block.reshape(TILE * TILE, TILE).astype(jnp.float32), nu_block.astype(jnp.float32), precision=highest, preferred_element_type=jnp.float32).reshape(TILE, TILE, R)
        addition = lax.optimization_barrier(jnp.sum(contracted * orb_block[None], axis=1)) * coords[3].astype(jnp.float32)
        return (add_rows(running, addition, (coords[0] * TILE).astype(jnp.int32)), None)
    running, _ = lax.scan(tile_step, jnp.zeros((P_SIZE, R), jnp.float32), (tiles, tile_list.T))
    return running

def mode_second(tiles, tile_list, aux_factor, nu_factor):

    def tile_step(running, tile_item):
        tile_block, coords = tile_item
        nu_block = lax.dynamic_slice_in_dim(nu_factor, (coords[2] * TILE).astype(jnp.int32), TILE, 0)
        aux_block = lax.dynamic_slice_in_dim(aux_factor, (coords[0] * TILE).astype(jnp.int32), TILE, 0)
        contracted = jnp.dot(tile_block.reshape(TILE * TILE, TILE).astype(jnp.float32), nu_block.astype(jnp.float32), precision=highest, preferred_element_type=jnp.float32).reshape(TILE, TILE, R)
        addition = lax.optimization_barrier(jnp.sum(contracted * aux_block[:, None, :], axis=0)) * coords[3].astype(jnp.float32)
        return (add_rows(running, addition, (coords[1] * TILE).astype(jnp.int32)), None)
    running, _ = lax.scan(tile_step, jnp.zeros((MU, R), jnp.float32), (tiles, tile_list.T))
    return running

def mode_third(tiles, tile_list, aux_factor, orb_factor):

    def tile_step(running, tile_item):
        tile_block, coords = tile_item
        aux_block = lax.dynamic_slice_in_dim(aux_factor, (coords[0] * TILE).astype(jnp.int32), TILE, 0)
        orb_block = lax.dynamic_slice_in_dim(orb_factor, (coords[1] * TILE).astype(jnp.int32), TILE, 0)
        contracted = lax.dot_general(tile_block.astype(jnp.float32), aux_block.astype(jnp.float32), (((0,), (0,)), ((), ())), precision=highest, preferred_element_type=jnp.float32).reshape(TILE, TILE, R)
        addition = lax.optimization_barrier(jnp.sum(contracted * orb_block[:, None, :], axis=0)) * coords[3].astype(jnp.float32)
        return (add_rows(running, addition, (coords[2] * TILE).astype(jnp.int32)), None)
    running, _ = lax.scan(tile_step, jnp.zeros((NU, R), jnp.float32), (tiles, tile_list.T))
    return running

def normalize(values, row_count):
    scales = jnp.sqrt(lax.optimization_barrier(jnp.sum(values * values, axis=0)) / row_count + epsilon)
    scaled = values / scales
    return (scaled, gram_of(scaled) / row_count)

def reference(tiles, tile_list, orb_factor, nu_factor):
    identity = jnp.eye(R, dtype=jnp.float32)
    s_orb = gram_of(orb_factor) / MU
    s_nu = gram_of(nu_factor) / NU
    first_terms = mode_first(tiles, tile_list, orb_factor, nu_factor)
    a_new = solve_rows(s_orb * s_nu + ridge_weight * identity, first_terms)
    aux_factor, s_first = normalize(a_new, P_SIZE)
    second_terms = mode_second(tiles, tile_list, aux_factor, nu_factor)
    b_new = solve_rows(s_first * s_nu + ridge_weight * identity, second_terms)
    orb_updated, s_second = normalize(b_new, MU)
    third_terms = mode_third(tiles, tile_list, aux_factor, orb_updated)
    c_new = solve_rows(s_first * s_second + ridge_weight * identity, third_terms)
    nu_updated, _ = normalize(c_new, NU)
    return (aux_factor, orb_updated, nu_updated)
```

```python
import functools

import jax
import jax.numpy as jnp
from jax import lax
from jax.experimental import pallas as pl
from jax.experimental.pallas import tpu as pltpu
from jax.sharding import PartitionSpec as P

P_SIZE = 16384
MU = 4096
NU = 512

ridge_weight = 0.5
epsilon = 1e-06
highest = lax.Precision.HIGHEST
f32 = jnp.float32
bf16 = jnp.bfloat16
PANEL = 32


MESH = pl.DeviceIdType.MESH


def reduce_kernel(steps, x_ref, out_ref, sum_ref, all_ref, *scratch):
    count = len(steps)
    landing = scratch[:count]
    send_sem, recv_sem = scratch[count:]
    bits, partners = [], []
    for axis, bit in steps:
        here = lax.axis_index(axis)
        value = (here // (1 << bit)) % 2
        bits.append(value)
        partners.append({axis: here + (1 - 2 * value) * (1 << bit)})
    barrier = pltpu.get_barrier_semaphore()
    for partner in partners:
        pl.semaphore_signal(barrier, inc=1, device_id=partner, device_id_type=MESH)
    pl.semaphore_wait(barrier, count)
    sum_ref[...] = x_ref[...]
    length = sum_ref.shape[0]
    start = jnp.int32(0)
    kept = []
    for step in range(count):
        length //= 2
        mine = pl.multiple_of(start + bits[step] * length, 8)
        other = pl.multiple_of(start + (1 - bits[step]) * length, 8)
        copy = pltpu.make_async_remote_copy(
            src_ref=sum_ref.at[pl.ds(other, length), :],
            dst_ref=landing[step],
            send_sem=send_sem.at[step],
            recv_sem=recv_sem.at[step],
            device_id=partners[step],
            device_id_type=MESH,
        )
        copy.start()
        copy.wait()
        sum_ref[pl.ds(mine, length), :] += landing[step][...]
        start = mine
        kept.append((mine, length))
    mine, length = kept[-1]
    all_ref[pl.ds(mine, length), :] = sum_ref[pl.ds(mine, length), :]
    for step in reversed(range(count)):
        mine, length = kept[step]
        rows = all_ref.at[pl.ds(mine, length), :]
        copy = pltpu.make_async_remote_copy(
            src_ref=rows,
            dst_ref=rows,
            send_sem=send_sem.at[count + step],
            recv_sem=recv_sem.at[count + step],
            device_id=partners[step],
            device_id_type=MESH,
        )
        copy.start()
        copy.wait()
    out_ref[...] = all_ref[...]


def all_reduce(x, axes, number, name):
    steps = []
    for axis in axes:
        size = lax.axis_size(axis)
        if size & (size - 1):
            return lax.psum(x, axes)
        steps += [(axis, bit) for bit in range(size.bit_length() - 1)]
    rows, columns = x.shape
    if rows % (8 << len(steps)):
        return lax.psum(x, axes)
    count = len(steps)
    vmem = pl.BlockSpec(memory_space=pltpu.VMEM)
    return pl.pallas_call(
        functools.partial(reduce_kernel, tuple(steps)),
        out_shape=jax.ShapeDtypeStruct(x.shape, f32),
        in_specs=[vmem],
        out_specs=vmem,
        scratch_shapes=[pltpu.VMEM((rows, columns), f32)] * 2
        + [pltpu.VMEM((rows >> (step + 1), columns), f32) for step in range(count)]
        + [pltpu.SemaphoreType.DMA((2 * count,)), pltpu.SemaphoreType.DMA((2 * count,))],
        compiler_params=pltpu.CompilerParams(collective_id=number, has_side_effects=True),
        name=name,
    )(x)


def gram_of(matrix):
    return jnp.dot(matrix.T, matrix, precision=highest, preferred_element_type=f32)


def split_two(x):
    high = x.astype(bf16)
    return high, (x - high.astype(f32)).astype(bf16)


def split_three(x):
    high = x.astype(bf16)
    rest = x - high.astype(f32)
    middle = rest.astype(bf16)
    return high, middle, (rest - middle.astype(f32)).astype(bf16)


def aligned(value, step):
    return pl.multiple_of(value, step)


def dot_t(left, right):
    return lax.dot_general(left, right, (((0,), (0,)), ((), ())), preferred_element_type=f32)


def dot_exact(left, right):
    l_high, l_middle, l_low = left
    r_high, r_middle, r_low = right
    dot = functools.partial(jnp.dot, preferred_element_type=f32)
    small = dot(l_low, r_high) + dot(l_high, r_low) + dot(l_middle, r_middle)
    return dot(l_high, r_high) + (dot(l_middle, r_high) + dot(l_high, r_middle) + small)


def gram_add(x, even_ref, odd_ref):
    high, middle, low = split_three(x)
    pair = jnp.concatenate([high, middle], axis=0)
    even_ref[...] += dot_t(pair, pair)
    odd_ref[...] += dot_t(
        jnp.concatenate([high, high], axis=0), jnp.concatenate([middle, low], axis=0)
    )


def gram_rows(x_ref, even_ref, odd_ref):
    even_ref[...] = jnp.zeros_like(even_ref)
    odd_ref[...] = jnp.zeros_like(odd_ref)
    group = min(4, x_ref.shape[0])

    def step(at, carry):
        rows = x_ref[pl.ds(at * group, group)]
        gram_add(rows.reshape(-1, rows.shape[2]), even_ref, odd_ref)
        return carry

    lax.fori_loop(0, x_ref.shape[0] // group, step, 0)
    odd = odd_ref[...]
    return even_ref[...] + (odd + odd.T)


def enter(axes):
    barrier = pltpu.get_barrier_semaphore()
    count = 0
    for axis in axes:
        size, here = lax.axis_size(axis), lax.axis_index(axis)
        for step in range(1, size):
            pl.semaphore_signal(
                barrier, inc=1, device_id={axis: (here + step) % size}, device_id_type=MESH
            )
            count += 1
    pl.semaphore_wait(barrier, count)


class Net:
    def __init__(self, send, recv):
        self.send, self.recv, self.copies = send, recv, []

    def copy(self, src, dst, to):
        at = len(self.copies)
        copy = pltpu.make_async_remote_copy(
            src_ref=src,
            dst_ref=dst,
            send_sem=self.send.at[at],
            recv_sem=self.recv.at[at],
            device_id=to,
            device_id_type=MESH,
        )
        copy.start()
        self.copies.append(copy)
        return copy

    def scatter(self, axis, src, land):
        size, here = lax.axis_size(axis), lax.axis_index(axis)
        rows = land.shape[1]
        land[here] = src[pl.ds(aligned(here * rows, 8), rows), :]
        copies = []
        for step in range(1, size):
            to = (here + step) % size
            block = src.at[pl.ds(aligned(to * rows, 8), rows), :]
            copies.append(self.copy(block, land.at[here], {axis: to}))
        return copies

    def share(self, axis, src, land):
        size, here = lax.axis_size(axis), lax.axis_index(axis)
        land[here] = src[...]
        return [
            self.copy(src, land.at[here], {axis: (here + step) % size}) for step in range(1, size)
        ]

    def spread(self, axis, full, rows):
        size, here = lax.axis_size(axis), lax.axis_index(axis)
        own = full.at[pl.ds(aligned(here * rows, 8), rows), :]
        return [self.copy(own, own, {axis: (here + step) % size}) for step in range(1, size)]

    def finish(self):
        for copy in self.copies:
            copy.wait_send()


def arrive(copies):
    for copy in copies:
        copy.wait_recv()


def total_of(land):
    total = land[0]
    for at in range(1, land.shape[0]):
        total += land[at]
    return total


def first_kernel(
    edge, list_ref, x_hbm, orb_ref, nu_ref, parts_out, table_out, inverse_out, s_nu_out,
    x_buf, parts, table, even, odd, gram, gram_land, work, x_sem, send, recv, hop_send, hop_recv
):
    slots = list_ref.shape[1]
    here, size = lax.axis_index("orb"), lax.axis_size("orb")
    mine = lax.axis_index("aux")
    rank = nu_ref.shape[2]
    orb_rows = orb_ref.shape[0] * edge
    first_base = mine * (P_SIZE // lax.axis_size("aux") // edge)
    gram_rows_each = gram_land.shape[1]

    def load(slot):
        return pltpu.make_async_copy(x_hbm.at[slot], x_buf.at[slot], x_sem.at[slot])

    for slot in range(slots):
        load(slot).start()
    enter(("aux", "orb"))
    net = Net(send, recv)

    def hop(way, distance, slot):
        at = ((here - way * distance) * slots + slot) * edge
        rows = parts.at[pl.ds(aligned(at, edge), edge), :]
        lane = 0 if way > 0 else 1
        return pltpu.make_async_remote_copy(
            src_ref=rows,
            dst_ref=rows,
            send_sem=hop_send.at[lane, distance, slot],
            recv_sem=hop_recv.at[lane, distance, slot],
            device_id={"orb": here + way},
            device_id_type=MESH,
        )

    def landed(way, distance, slot):
        at = ((here - way * distance) * slots + slot) * edge
        rows = parts.at[pl.ds(aligned(at, edge), edge), :]
        lane = 0 if way > 0 else 1
        return pltpu.make_async_remote_copy(
            src_ref=rows,
            dst_ref=rows,
            send_sem=hop_send.at[lane, distance - 1, slot],
            recv_sem=hop_recv.at[lane, distance - 1, slot],
            device_id={"orb": here - way},
            device_id_type=MESH,
        )

    def goes(way, distance):
        at = here if way > 0 else size - 1 - here
        return (at + size - 1 - distance) // (size - 1) * ((2 * size - 3 - at) // (size - 1)) > 0

    def ends(way, distance):
        return here == size - 1 if way > 0 else here == 0

    def forward(distance, slot):
        for way in (1, -1):

            @pl.when(goes(way, distance))
            def _():
                landed(way, distance, slot).wait_recv()
                hop(way, distance, slot).start()

    def slot_step(slot, carry):
        load(slot).wait()
        nu_block = nu_ref[list_ref[2, slot]]
        orb_block = orb_ref[lax.rem(list_ref[1, slot], orb_ref.shape[0])]
        group = 4
        total = jnp.zeros((edge, rank), f32)
        for start in range(0, edge, group):
            x_high, x_low = split_two(x_buf[slot, :, start * edge:(start + group) * edge])
            stacked = jnp.concatenate([x_high, x_low], axis=0)
            product = jnp.concatenate(
                [nu_block * orb_block[j:j + 1, :] for j in range(start, start + group)], axis=0
            )
            high, low = split_two(product)
            main = jnp.dot(stacked, high, preferred_element_type=f32)
            rest = jnp.dot(x_high, low, preferred_element_type=f32)
            total += main[:edge] + (main[edge:] + rest)
        live = list_ref[3, slot].astype(f32)
        parts[pl.ds(aligned((here * slots + slot) * edge, edge), edge), :] = total * live
        for way in (1, -1):

            @pl.when(goes(way, 0))
            def _():
                hop(way, 0, slot).start()

        return carry

    early, late = slots // 4, slots - slots // 4
    lax.fori_loop(0, early, slot_step, 0)

    row = lax.broadcasted_iota(jnp.int32, (slots, table.shape[1]), 0)
    own_at = jnp.zeros((slots, table.shape[1]), f32)
    for slot in range(slots):
        value = (list_ref[0, slot] - first_base).astype(f32)
        own_at = jnp.where(row == slot, value, own_at)
    table[pl.ds(aligned(here * slots, 8), slots), :] = own_at
    table_copies = net.spread("orb", table, slots)
    gram[...] = gram_rows(orb_ref, even, odd)
    gram_copies = []
    for step in range(1, size):
        block = gram.at[pl.ds(aligned(mine * gram_rows_each, 8), gram_rows_each), :]
        gram_copies.append(net.copy(block, gram_land.at[here], {"orb": (here + step) % size}))
    gram_land[here] = gram[pl.ds(aligned(mine * gram_rows_each, 8), gram_rows_each), :]
    s_nu = gram_rows(nu_ref, even, odd) / NU
    s_nu_out[...] = s_nu
    lax.fori_loop(early, late, slot_step, 0)
    arrive(gram_copies)
    work[pl.ds(aligned(mine * gram_rows_each, 8), gram_rows_each), :] = total_of(gram_land)
    share_copies = net.spread("aux", work, gram_rows_each)
    lax.fori_loop(late, slots, slot_step, 0)

    if size > 2:

        def near(slot, carry):
            forward(1, slot)
            return carry

        lax.fori_loop(0, slots, near, 0)
    arrive(share_copies)
    even[...] = work[...] / (orb_rows * size) * s_nu_out[...] + jnp.where(
        eye_mask(rank), ridge_weight, 0.0
    )

    def beside(step):
        if size > 3:
            forward(2, step)

    sweep_inverse(even, beside if rank // PANEL == slots else None)
    inverse_out[...] = -even[...]
    far = 2 if rank // PANEL != slots else 3
    for distance in range(far, size - 1):

        def pass_on(slot, carry, distance=distance):
            forward(distance, slot)
            return carry

        lax.fori_loop(0, slots, pass_on, 0)

    def last(slot, carry):
        for way in (1, -1):
            for distance in range(1, size):

                @pl.when(ends(way, distance))
                def _():
                    landed(way, distance, slot).wait_recv()

            for distance in range(size - 1):

                @pl.when(goes(way, distance))
                def _():
                    hop(way, distance, slot).wait_send()

        return carry

    lax.fori_loop(0, slots, last, 0)
    arrive(table_copies)
    net.finish()
    parts_out[...] = parts[...]
    table_out[...] = table[...].astype(jnp.int32)


def solve_kernel(edge, blocks, at_ref, part_ref, inverse_ref, a_ref, gram_ref, total_ref, even, odd):
    total_ref[...] = jnp.zeros_like(total_ref)

    def add_block(block, carry):
        rows = pl.ds(aligned(at_ref[block, 0] * edge, edge), edge)
        total_ref[rows, :] += part_ref[pl.ds(aligned(block * edge, edge), edge), :]
        return carry

    lax.fori_loop(0, blocks, add_block, 0)
    inverse = split_three(inverse_ref[...])
    even[...] = jnp.zeros_like(even)
    odd[...] = jnp.zeros_like(odd)
    chunk = min(512, total_ref.shape[0])

    def apply(step, carry):
        rows = pl.ds(aligned(step * chunk, chunk), chunk)
        solved = dot_exact(split_three(total_ref[rows, :]), inverse)
        a_ref[rows, :] = solved
        gram_add(solved, even, odd)
        return carry

    lax.fori_loop(0, total_ref.shape[0] // chunk, apply, 0)
    cross = odd[...]
    gram_ref[...] = even[...] + (cross + cross.T)


def second_kernel(edge, index_ref, x_ref, a_ref, nu_ref, e_ref, out_ref):
    slot = pl.program_id(0)
    first_at = pl.multiple_of(index_ref[0, slot] * edge, edge)
    second_at = pl.multiple_of(index_ref[1, slot] * edge, edge)
    third_at = pl.multiple_of(index_ref[2, slot] * edge, edge)
    live = index_ref[3, slot] > 0

    @pl.when(slot == 0)
    def _():
        out_ref[...] = jnp.zeros_like(out_ref)

    nu_block = nu_ref[pl.ds(third_at, edge), :]
    a_high, a_low = split_two(a_ref[pl.ds(first_at, edge), :])
    weights = jnp.concatenate([a_high, a_high, a_low, a_low], axis=0)
    group = 8
    for start in range(0, edge, group):
        x_high, x_low = split_two(x_ref[0, :, start * edge:(start + group) * edge])
        turned = jnp.concatenate([x_high, x_low], axis=0).T
        e = jnp.dot(
            jnp.concatenate([turned, turned], axis=1), weights, preferred_element_type=f32
        )
        e_ref[0, start * edge:(start + group) * edge, :] = e
        sums = jnp.sum(e.reshape(group, edge, e.shape[1]) * nu_block[None], axis=1)
        rows = pl.ds(pl.multiple_of(second_at + start, group), group)
        out_ref[rows, :] += jnp.where(live, sums, 0.0)


def third_kernel(edge, index_ref, e_ref, b_ref, out_ref):
    slot = pl.program_id(0)
    second_at = pl.multiple_of(index_ref[1, slot] * edge, edge)
    third_at = pl.multiple_of(index_ref[2, slot] * edge, edge)

    @pl.when(slot == 0)
    def _():
        out_ref[...] = jnp.zeros_like(out_ref)

    b_block = b_ref[pl.ds(second_at, edge), :]
    total = jnp.zeros((edge, b_block.shape[1]), f32)
    for j in range(edge):
        total += e_ref[0, j * edge:(j + 1) * edge, :] * b_block[j:j + 1, :]
    out_ref[pl.ds(third_at, edge), :] += jnp.where(index_ref[3, slot] > 0, total, 0.0)


def eye_mask(n):
    return lax.broadcasted_iota(jnp.int32, (n, n), 0) == lax.broadcasted_iota(jnp.int32, (n, n), 1)


def unit_gram(gram, rows):
    diagonal = jnp.where(eye_mask(gram.shape[0]), gram, 0.0)
    along = jnp.sqrt(jnp.sum(diagonal, axis=0, keepdims=True) / rows + epsilon)
    down = jnp.sqrt(jnp.sum(diagonal, axis=1, keepdims=True) / rows + epsilon)
    return gram / down / along / rows, along


def sweep_inverse(a_ref, beside=None):
    n = a_ref.shape[0]
    lane = lax.broadcasted_iota(jnp.int32, (PANEL, n), 1)
    row = lax.broadcasted_iota(jnp.int32, (PANEL, n), 0)

    def panel_step(step, carry):
        if beside is not None:
            beside(step)
        before = a_ref[:PANEL, :]
        panel = before
        for k in range(0, PANEL, 2):
            first = jnp.broadcast_to(panel[:, k:k + 1], panel.shape)
            second = jnp.broadcast_to(panel[:, k + 1:k + 2], panel.shape)
            at_first, at_second = lane == k, lane == k + 1
            unit_first = jnp.where(at_second[:1], 0.0, panel[k:k + 1, :])
            unit_first = jnp.where(at_first[:1], 1.0, unit_first)
            unit_second = jnp.where(at_first[:1], 0.0, panel[k + 1:k + 2, :])
            unit_second = jnp.where(at_second[:1], 1.0, unit_second)
            inverse = 1.0 / first[k:k + 1, :]
            across = second[k:k + 1, :]
            factor = first[k + 1:k + 2, :] * inverse
            inverse_schur = 1.0 / (second[k + 1:k + 2, :] - factor * across)
            new_second = (unit_second - factor * unit_first) * inverse_schur
            new_first = (unit_first - across * new_second) * inverse
            kept = jnp.where(at_first | at_second, 0.0, panel)
            panel = kept - first * new_first - second * new_second
            panel = jnp.where(row == k, new_first, jnp.where(row == k + 1, new_second, panel))
        own = lane < PANEL
        update = jnp.where(own, -panel, panel)
        w_high, w_middle, w_low = split_three(before)
        z_high, z_middle, z_low = split_three(update)
        left = jnp.concatenate([w_low, w_middle, w_high, w_middle, w_high, w_high], axis=0)
        right = jnp.concatenate([z_high, z_middle, z_low, z_high, z_middle, z_high], axis=0)
        change = lax.dot_general(
            left, right, (((0,), (0,)), ((), ())), preferred_element_type=f32
        )
        others = jnp.where(own[:1], 0.0, a_ref[PANEL:, :]) - change[PANEL:, :]
        a_ref[:n - PANEL, :] = pltpu.roll(others, n - PANEL, 1)
        a_ref[n - PANEL:, :] = pltpu.roll(update, n - PANEL, 1)
        return carry

    lax.fori_loop(0, n // PANEL, panel_step, 0)


def inverse_kernel(left_rows, right_rows, left_ref, right_ref, inverse_ref, scale_ref, a_ref):
    left = left_ref[...]
    if left_rows:
        left, scale_ref[...] = unit_gram(left, left_rows)
    else:
        scale_ref[...] = jnp.ones_like(scale_ref)
    right = right_ref[...]
    if right_rows:
        right, _ = unit_gram(right, right_rows)
    n = left.shape[0]
    a_ref[...] = left * right + jnp.where(eye_mask(n), ridge_weight, 0.0)
    sweep_inverse(a_ref)
    inverse_ref[...] = -a_ref[...]


def inverse_of(left, right, left_rows, right_rows, name):
    n = left.shape[0]
    whole = pl.BlockSpec(memory_space=pltpu.VMEM)
    return pl.pallas_call(
        functools.partial(inverse_kernel, left_rows, right_rows),
        out_shape=(jax.ShapeDtypeStruct((n, n), f32), jax.ShapeDtypeStruct((1, n), f32)),
        in_specs=[whole, whole],
        out_specs=(whole, whole),
        scratch_shapes=[pltpu.VMEM((n, n), f32)],
        compiler_params=pltpu.CompilerParams(vmem_limit_bytes=16 << 20),
        cost_estimate=pl.CostEstimate(flops=10**9, bytes_accessed=4 * n * n * 4, transcendentals=0),
        name=name,
    )(left, right)


def per_device(tiles, tile_list, orb_factor, nu_factor):
    slots, edge = tiles.shape[0], tiles.shape[1]
    rank = nu_factor.shape[1]
    first_rows = P_SIZE // lax.axis_size("aux")
    orb_rows = orb_factor.shape[0]
    orb_size = lax.axis_size("orb")
    tile_width = tiles.shape[2]
    index = tile_list - jnp.stack(
        [
            lax.axis_index("aux") * (first_rows // edge),
            lax.axis_index("orb") * (orb_rows // edge),
            jnp.int32(0),
            jnp.int32(0),
        ]
    ).astype(jnp.int32)[:, None]
    tile_spec = pl.BlockSpec((1, edge, tile_width), lambda s, i: (s, 0, 0))

    def full(rows):
        return pl.BlockSpec((rows, rank), lambda s, i: (0, 0))

    aux_size = lax.axis_size("aux")
    vmem = pl.BlockSpec(memory_space=pltpu.VMEM)
    blocks = slots * orb_size
    square = pltpu.VMEM((rank, rank), f32)
    net_count = 2 * (orb_size - 1) + aux_size - 1
    parts, table, inverse_first, s_nu = pl.pallas_call(
        functools.partial(first_kernel, edge),
        out_shape=(
            jax.ShapeDtypeStruct((blocks * edge, rank), f32),
            jax.ShapeDtypeStruct((blocks, 128), jnp.int32),
            jax.ShapeDtypeStruct((rank, rank), f32),
            jax.ShapeDtypeStruct((rank, rank), f32),
        ),
        in_specs=[
            pl.BlockSpec(memory_space=pltpu.SMEM),
            pl.BlockSpec(memory_space=pltpu.HBM),
            vmem,
            vmem,
        ],
        out_specs=(vmem, vmem, vmem, vmem),
        scratch_shapes=[
            pltpu.VMEM((slots, edge, tile_width), f32),
            pltpu.VMEM((blocks * edge, rank), f32),
            pltpu.VMEM((blocks, 128), f32),
            square,
            square,
            square,
            pltpu.VMEM((orb_size, rank // aux_size, rank), f32),
            square,
            pltpu.SemaphoreType.DMA((slots,)),
            pltpu.SemaphoreType.DMA((net_count,)),
            pltpu.SemaphoreType.DMA((net_count,)),
            pltpu.SemaphoreType.DMA((2, orb_size - 1, slots)),
            pltpu.SemaphoreType.DMA((2, orb_size - 1, slots)),
        ],
        compiler_params=pltpu.CompilerParams(
            collective_id=5, has_side_effects=True, vmem_limit_bytes=32 << 20
        ),
        name="first_gather",
    )(tile_list, tiles, orb_factor.reshape(-1, edge, rank), nu_factor.reshape(-1, edge, rank))
    a_new, gram_a = pl.pallas_call(
        functools.partial(solve_kernel, edge, blocks),
        out_shape=(
            jax.ShapeDtypeStruct((first_rows, rank), f32),
            jax.ShapeDtypeStruct((rank, rank), f32),
        ),
        in_specs=[pl.BlockSpec(memory_space=pltpu.SMEM), vmem, vmem],
        out_specs=(vmem, vmem),
        scratch_shapes=[pltpu.VMEM((first_rows, rank), f32), square, square],
        name="solve_first",
    )(table, parts, inverse_first)
    gram_a = all_reduce(gram_a, ("aux",), 1, "sum_gram_first")

    e_all, partial_second = pl.pallas_call(
        functools.partial(second_kernel, edge),
        out_shape=(
            jax.ShapeDtypeStruct((slots, tile_width, rank), f32),
            jax.ShapeDtypeStruct((orb_rows, rank), f32),
        ),
        grid_spec=pltpu.PrefetchScalarGridSpec(
            num_scalar_prefetch=1,
            grid=(slots,),
            in_specs=[tile_spec, full(first_rows), full(nu_factor.shape[0])],
            out_specs=(
                pl.BlockSpec((1, tile_width, rank), lambda s, i: (s, 0, 0)),
                full(orb_rows),
            ),
        ),
        name="mode_second",
    )(index, tiles, a_new, nu_factor)
    sums_first = jnp.sum(jnp.where(eye_mask(rank), gram_a, 0.0), axis=0)
    scale_first = jnp.sqrt(sums_first / P_SIZE + epsilon)
    second_sums = all_reduce(partial_second / scale_first, ("aux",), 2, "sum_second")
    inverse_second, _ = inverse_of(gram_a, s_nu, P_SIZE, 0, "inverse_second")
    aux_factor = a_new / scale_first
    b_new = jnp.dot(second_sums, inverse_second, precision=highest, preferred_element_type=f32)
    gram_b = all_reduce(gram_of(b_new), ("orb",), 3, "sum_gram_second")

    partial_third = pl.pallas_call(
        functools.partial(third_kernel, edge),
        out_shape=jax.ShapeDtypeStruct((nu_factor.shape[0], rank), f32),
        grid_spec=pltpu.PrefetchScalarGridSpec(
            num_scalar_prefetch=1,
            grid=(slots,),
            in_specs=[
                pl.BlockSpec((1, tile_width, rank), lambda s, i: (s, 0, 0)),
                full(orb_rows),
            ],
            out_specs=full(nu_factor.shape[0]),
        ),
        name="mode_third",
    )(index, e_all, b_new)
    third_sums = all_reduce(partial_third, ("aux", "orb"), 4, "sum_third")
    inverse_third, scale_second = inverse_of(gram_b, gram_a, MU, P_SIZE, "inverse_third")
    orb_updated = b_new / scale_second
    c_new = jnp.dot(
        third_sums / scale_first / scale_second,
        inverse_third,
        precision=highest,
        preferred_element_type=f32,
    )
    scale_third = jnp.sqrt(jnp.sum(c_new * c_new, axis=0) / NU + epsilon)
    nu_updated = c_new / scale_third
    return (aux_factor, orb_updated, nu_updated)


def solution(mesh):
    return jax.shard_map(
        per_device,
        mesh=mesh,
        in_specs=(P(("aux", "orb"), None, None), P(None, ("aux", "orb")), P("orb", None), P()),
        out_specs=(P("aux", None), P("orb", None), P()),
        check_vma=False,
    )
```

```python
import functools

import jax
import jax.numpy as jnp
from jax import lax
from jax.experimental import pallas as pl
from jax.experimental.pallas import tpu as pltpu
from jax.sharding import PartitionSpec as P

P_SIZE = 16384
MU = 4096
NU = 512

ridge_weight = 0.5
epsilon = 1e-06
highest = lax.Precision.HIGHEST
f32 = jnp.float32
bf16 = jnp.bfloat16
PANEL = 32


MESH = pl.DeviceIdType.MESH


def split_two(x):
    high = x.astype(bf16)
    return high, (x - high.astype(f32)).astype(bf16)


def split_three(x):
    high = x.astype(bf16)
    rest = x - high.astype(f32)
    middle = rest.astype(bf16)
    return high, middle, (rest - middle.astype(f32)).astype(bf16)


def aligned(value, step):
    return pl.multiple_of(value, step)


def dot_t(left, right):
    return lax.dot_general(left, right, (((0,), (0,)), ((), ())), preferred_element_type=f32)


def dot_exact(left, right):
    l_high, l_middle, l_low = left
    r_high, r_middle, r_low = right
    dot = functools.partial(jnp.dot, preferred_element_type=f32)
    small = dot(l_low, r_high) + dot(l_high, r_low) + dot(l_middle, r_middle)
    return dot(l_high, r_high) + (dot(l_middle, r_high) + dot(l_high, r_middle) + small)


def gram_add(x, even_ref, odd_ref):
    high, middle, low = split_three(x)
    pair = jnp.concatenate([high, middle], axis=0)
    even_ref[...] += dot_t(pair, pair)
    odd_ref[...] += dot_t(
        jnp.concatenate([high, high], axis=0), jnp.concatenate([middle, low], axis=0)
    )


def gram_rows(x_ref, even_ref, odd_ref):
    even_ref[...] = jnp.zeros_like(even_ref)
    odd_ref[...] = jnp.zeros_like(odd_ref)
    group = min(4, x_ref.shape[0])

    def step(at, carry):
        rows = x_ref[pl.ds(at * group, group)]
        gram_add(rows.reshape(-1, rows.shape[2]), even_ref, odd_ref)
        return carry

    lax.fori_loop(0, x_ref.shape[0] // group, step, 0)
    odd = odd_ref[...]
    return even_ref[...] + (odd + odd.T)


def enter(axes):
    barrier = pltpu.get_barrier_semaphore()
    count = 0
    for axis in axes:
        size, here = lax.axis_size(axis), lax.axis_index(axis)
        for step in range(1, size):
            pl.semaphore_signal(
                barrier, inc=1, device_id={axis: (here + step) % size}, device_id_type=MESH
            )
            count += 1
    pl.semaphore_wait(barrier, count)


class Net:
    def __init__(self, send, recv):
        self.send, self.recv, self.copies = send, recv, []

    def copy(self, src, dst, to):
        at = len(self.copies)
        copy = pltpu.make_async_remote_copy(
            src_ref=src,
            dst_ref=dst,
            send_sem=self.send.at[at],
            recv_sem=self.recv.at[at],
            device_id=to,
            device_id_type=MESH,
        )
        copy.start()
        self.copies.append(copy)
        return copy

    def scatter(self, axis, src, land):
        size, here = lax.axis_size(axis), lax.axis_index(axis)
        rows = land.shape[1]
        land[here] = src[pl.ds(aligned(here * rows, 8), rows), :]
        copies = []
        for step in range(1, size):
            to = (here + step) % size
            block = src.at[pl.ds(aligned(to * rows, 8), rows), :]
            copies.append(self.copy(block, land.at[here], {axis: to}))
        return copies

    def share(self, axis, src, land):
        size, here = lax.axis_size(axis), lax.axis_index(axis)
        land[here] = src[...]
        return [
            self.copy(src, land.at[here], {axis: (here + step) % size}) for step in range(1, size)
        ]

    def spread(self, axis, full, rows):
        size, here = lax.axis_size(axis), lax.axis_index(axis)
        own = full.at[pl.ds(aligned(here * rows, 8), rows), :]
        return [self.copy(own, own, {axis: (here + step) % size}) for step in range(1, size)]

    def finish(self):
        for copy in self.copies:
            copy.wait_send()


def arrive(copies):
    for copy in copies:
        copy.wait_recv()


def total_of(land):
    total = land[0]
    for at in range(1, land.shape[0]):
        total += land[at]
    return total


def first_kernel(
    edge, list_ref, x_hbm, orb_ref, nu_ref, parts_out, table_out, inverse_out, s_nu_out,
    x_buf, parts, table, even, odd, gram, gram_land, work, x_sem, send, recv, hop_send, hop_recv
):
    slots = list_ref.shape[1]
    here, size = lax.axis_index("orb"), lax.axis_size("orb")
    mine = lax.axis_index("aux")
    rank = nu_ref.shape[2]
    orb_rows = orb_ref.shape[0] * edge
    first_base = mine * (P_SIZE // lax.axis_size("aux") // edge)
    gram_rows_each = gram_land.shape[1]

    def load(slot):
        return pltpu.make_async_copy(x_hbm.at[slot], x_buf.at[slot], x_sem.at[slot])

    for slot in range(slots):
        load(slot).start()
    enter(("aux", "orb"))
    net = Net(send, recv)

    def hop(way, distance, slot):
        at = ((here - way * distance) * slots + slot) * edge
        rows = parts.at[pl.ds(aligned(at, edge), edge), :]
        lane = 0 if way > 0 else 1
        return pltpu.make_async_remote_copy(
            src_ref=rows,
            dst_ref=rows,
            send_sem=hop_send.at[lane, distance, slot],
            recv_sem=hop_recv.at[lane, distance, slot],
            device_id={"orb": here + way},
            device_id_type=MESH,
        )

    def landed(way, distance, slot):
        at = ((here - way * distance) * slots + slot) * edge
        rows = parts.at[pl.ds(aligned(at, edge), edge), :]
        lane = 0 if way > 0 else 1
        return pltpu.make_async_remote_copy(
            src_ref=rows,
            dst_ref=rows,
            send_sem=hop_send.at[lane, distance - 1, slot],
            recv_sem=hop_recv.at[lane, distance - 1, slot],
            device_id={"orb": here - way},
            device_id_type=MESH,
        )

    def goes(way, distance):
        at = here if way > 0 else size - 1 - here
        return (at + size - 1 - distance) // (size - 1) * ((2 * size - 3 - at) // (size - 1)) > 0

    def ends(way, distance):
        return here == size - 1 if way > 0 else here == 0

    def forward(distance, slot):
        for way in (1, -1):

            @pl.when(goes(way, distance))
            def _():
                landed(way, distance, slot).wait_recv()
                hop(way, distance, slot).start()

    def slot_step(slot, carry):
        load(slot).wait()
        nu_block = nu_ref[list_ref[2, slot]]
        orb_block = orb_ref[lax.rem(list_ref[1, slot], orb_ref.shape[0])]
        group = 4
        total = jnp.zeros((edge, rank), f32)
        for start in range(0, edge, group):
            x_high, x_low = split_two(x_buf[slot, :, start * edge:(start + group) * edge])
            stacked = jnp.concatenate([x_high, x_low], axis=0)
            product = jnp.concatenate(
                [nu_block * orb_block[j:j + 1, :] for j in range(start, start + group)], axis=0
            )
            high, low = split_two(product)
            main = jnp.dot(stacked, high, preferred_element_type=f32)
            rest = jnp.dot(x_high, low, preferred_element_type=f32)
            total += main[:edge] + (main[edge:] + rest)
        live = list_ref[3, slot].astype(f32)
        parts[pl.ds(aligned((here * slots + slot) * edge, edge), edge), :] = total * live
        for way in (1, -1):

            @pl.when(goes(way, 0))
            def _():
                hop(way, 0, slot).start()

        return carry

    early, late = slots // 4, slots - slots // 4
    lax.fori_loop(0, early, slot_step, 0)

    row = lax.broadcasted_iota(jnp.int32, (slots, table.shape[1]), 0)
    own_at = jnp.zeros((slots, table.shape[1]), f32)
    for slot in range(slots):
        value = (list_ref[0, slot] - first_base).astype(f32)
        own_at = jnp.where(row == slot, value, own_at)
    table[pl.ds(aligned(here * slots, 8), slots), :] = own_at
    table_copies = net.spread("orb", table, slots)
    gram[...] = gram_rows(orb_ref, even, odd)
    gram_copies = []
    for step in range(1, size):
        block = gram.at[pl.ds(aligned(mine * gram_rows_each, 8), gram_rows_each), :]
        gram_copies.append(net.copy(block, gram_land.at[here], {"orb": (here + step) % size}))
    gram_land[here] = gram[pl.ds(aligned(mine * gram_rows_each, 8), gram_rows_each), :]
    s_nu = gram_rows(nu_ref, even, odd) / NU
    s_nu_out[...] = s_nu
    lax.fori_loop(early, late, slot_step, 0)
    arrive(gram_copies)
    work[pl.ds(aligned(mine * gram_rows_each, 8), gram_rows_each), :] = total_of(gram_land)
    share_copies = net.spread("aux", work, gram_rows_each)
    lax.fori_loop(late, slots, slot_step, 0)

    if size > 2:

        def near(slot, carry):
            forward(1, slot)
            return carry

        lax.fori_loop(0, slots, near, 0)
    arrive(share_copies)
    even[...] = work[...] / (orb_rows * size) * s_nu_out[...] + jnp.where(
        eye_mask(rank), ridge_weight, 0.0
    )

    def beside(step):
        if size > 3:
            forward(2, step)

    sweep_inverse(even, beside if rank // PANEL == slots else None)
    inverse_out[...] = -even[...]
    far = 2 if rank // PANEL != slots else 3
    for distance in range(far, size - 1):

        def pass_on(slot, carry, distance=distance):
            forward(distance, slot)
            return carry

        lax.fori_loop(0, slots, pass_on, 0)

    def last(slot, carry):
        for way in (1, -1):
            for distance in range(1, size):

                @pl.when(ends(way, distance))
                def _():
                    landed(way, distance, slot).wait_recv()

            for distance in range(size - 1):

                @pl.when(goes(way, distance))
                def _():
                    hop(way, distance, slot).wait_send()

        return carry

    lax.fori_loop(0, slots, last, 0)
    arrive(table_copies)
    net.finish()
    parts_out[...] = parts[...]
    table_out[...] = table[...].astype(jnp.int32)


def solve_kernel(edge, blocks, at_ref, part_ref, inverse_ref, a_ref, gram_ref, total_ref, even, odd):
    total_ref[...] = jnp.zeros_like(total_ref)

    def add_block(block, carry):
        rows = pl.ds(aligned(at_ref[block, 0] * edge, edge), edge)
        total_ref[rows, :] += part_ref[pl.ds(aligned(block * edge, edge), edge), :]
        return carry

    lax.fori_loop(0, blocks, add_block, 0)
    inverse = split_three(inverse_ref[...])
    even[...] = jnp.zeros_like(even)
    odd[...] = jnp.zeros_like(odd)
    chunk = min(512, total_ref.shape[0])

    def apply(step, carry):
        rows = pl.ds(aligned(step * chunk, chunk), chunk)
        solved = dot_exact(split_three(total_ref[rows, :]), inverse)
        a_ref[rows, :] = solved
        gram_add(solved, even, odd)
        return carry

    lax.fori_loop(0, total_ref.shape[0] // chunk, apply, 0)
    cross = odd[...]
    gram_ref[...] = even[...] + (cross + cross.T)


def eye_mask(n):
    return lax.broadcasted_iota(jnp.int32, (n, n), 0) == lax.broadcasted_iota(jnp.int32, (n, n), 1)


def unit_gram(gram, rows):
    diagonal = jnp.where(eye_mask(gram.shape[0]), gram, 0.0)
    along = jnp.sqrt(jnp.sum(diagonal, axis=0, keepdims=True) / rows + epsilon)
    down = jnp.sqrt(jnp.sum(diagonal, axis=1, keepdims=True) / rows + epsilon)
    return gram / down / along / rows, along


def sweep_inverse(a_ref, beside=None, first=0, last=None):
    n = a_ref.shape[0]
    lane = lax.broadcasted_iota(jnp.int32, (PANEL, n), 1)
    row = lax.broadcasted_iota(jnp.int32, (PANEL, n), 0)

    def panel_step(step, carry):
        if beside is not None:
            beside(step)
        before = a_ref[:PANEL, :]
        panel = before
        for k in range(0, PANEL, 2):
            first = jnp.broadcast_to(panel[:, k:k + 1], panel.shape)
            second = jnp.broadcast_to(panel[:, k + 1:k + 2], panel.shape)
            at_first, at_second = lane == k, lane == k + 1
            unit_first = jnp.where(at_second[:1], 0.0, panel[k:k + 1, :])
            unit_first = jnp.where(at_first[:1], 1.0, unit_first)
            unit_second = jnp.where(at_first[:1], 0.0, panel[k + 1:k + 2, :])
            unit_second = jnp.where(at_second[:1], 1.0, unit_second)
            inverse = 1.0 / first[k:k + 1, :]
            across = second[k:k + 1, :]
            factor = first[k + 1:k + 2, :] * inverse
            inverse_schur = 1.0 / (second[k + 1:k + 2, :] - factor * across)
            new_second = (unit_second - factor * unit_first) * inverse_schur
            new_first = (unit_first - across * new_second) * inverse
            kept = jnp.where(at_first | at_second, 0.0, panel)
            panel = kept - first * new_first - second * new_second
            panel = jnp.where(row == k, new_first, jnp.where(row == k + 1, new_second, panel))
        own = lane < PANEL
        update = jnp.where(own, -panel, panel)
        w_high, w_middle, w_low = split_three(before)
        z_high, z_middle, z_low = split_three(update)
        left = jnp.concatenate([w_low, w_middle, w_high, w_middle, w_high, w_high], axis=0)
        right = jnp.concatenate([z_high, z_middle, z_low, z_high, z_middle, z_high], axis=0)
        change = lax.dot_general(
            left, right, (((0,), (0,)), ((), ())), preferred_element_type=f32
        )
        others = jnp.where(own[:1], 0.0, a_ref[PANEL:, :]) - change[PANEL:, :]
        a_ref[:n - PANEL, :] = pltpu.roll(others, n - PANEL, 1)
        a_ref[n - PANEL:, :] = pltpu.roll(update, n - PANEL, 1)
        return carry

    lax.fori_loop(first, n // PANEL if last is None else last, panel_step, 0)


def sweep_kernel(
    edge, list_ref, x_hbm, nu_ref, a_ref, gram_ref, s_nu_ref, b_out, c_out, scale_out,
    x_buf, e_ref, part, work, even, odd, gram_land, gram_a, terms, terms_land, b_full, b_blocks,
    gram_b, z_land, gram_sum, thirds, thirds_land, thirds_z, third_sums, x_sem, send, recv
):
    slots = list_ref.shape[1]
    here, size = lax.axis_index("orb"), lax.axis_size("orb")
    mine, count = lax.axis_index("aux"), lax.axis_size("aux")
    rank = nu_ref.shape[2]
    orb_rows, nu_rows = b_full.shape[0], third_sums.shape[0]
    half = slots // 2

    def load(slot):
        return pltpu.make_async_copy(x_hbm.at[slot], x_buf.at[slot], x_sem.at[slot])

    for slot in range(slots):
        load(slot).start()
    enter(("aux", "orb"))
    net = Net(send, recv)
    gram_copies = net.scatter("aux", gram_ref, gram_land)

    def rows_of(ref):
        return pl.ds(aligned(mine * (ref.shape[0] // count), 8), ref.shape[0] // count)

    def second_step(slot, carry):
        load(slot).wait()
        nu_block = nu_ref[list_ref[2, slot]]
        a_high, a_low = split_two(a_ref[lax.rem(list_ref[0, slot], a_ref.shape[0])])
        weights = jnp.concatenate([a_high, a_high, a_low, a_low], axis=0)
        group = 8
        for start in range(0, edge, group):
            x_high, x_low = split_two(x_buf[slot, :, start * edge:(start + group) * edge])
            turned = jnp.concatenate([x_high, x_low], axis=0).T
            e = jnp.dot(
                jnp.concatenate([turned, turned], axis=1), weights, preferred_element_type=f32
            )
            e_ref[slot, start * edge:(start + group) * edge, :] = e
            part[slot, start:start + group, :] = jnp.sum(
                e.reshape(group, edge, rank) * nu_block[None], axis=1
            )
        return carry

    def gather_blocks(dimension, out_ref):
        blocks = out_ref.shape[0] // edge
        places = [lax.rem(list_ref[dimension, slot], blocks) for slot in range(slots)]
        lives = [list_ref[3, slot].astype(f32) for slot in range(slots)]

        def block_step(block, carry):
            total = jnp.zeros((edge, rank), f32)
            for slot in range(slots):
                weight = (places[slot] == block).astype(f32) * lives[slot]
                total += part[slot] * weight
            out_ref[pl.ds(aligned(block * edge, edge), edge), :] = total
            return carry

        lax.fori_loop(0, blocks, block_step, 0)

    lax.fori_loop(0, half, second_step, 0)
    arrive(gram_copies)
    gram_a[rows_of(gram_a), :] = total_of(gram_land)
    gram_copies = net.spread("aux", gram_a, rank // count)
    lax.fori_loop(half, slots, second_step, 0)
    gather_blocks(1, terms)
    terms_copies = net.scatter("aux", terms, terms_land)

    arrive(gram_copies)
    unit_a, scale_a = unit_gram(gram_a[...], P_SIZE)
    ridge = jnp.where(eye_mask(rank), ridge_weight, 0.0)
    work[...] = unit_a * s_nu_ref[...] + ridge
    sweep_inverse(work)
    inverse = split_three(-work[...])
    arrive(terms_copies)
    b_own = dot_exact(split_three(total_of(terms_land) / scale_a), inverse)
    b_full[rows_of(b_full), :] = b_own
    b_copies = net.spread("aux", b_full, orb_rows // count)
    scale_out[...] = jnp.broadcast_to(scale_a, scale_out.shape)
    arrive(b_copies)
    b_blocks[...] = b_full[...].reshape(b_blocks.shape)
    gram_b[...] = gram_rows(b_blocks, even, odd)
    z_copies = net.share("orb", gram_b.at[rows_of(gram_b), :], z_land)

    def third_step(slot, carry):
        b_block = b_blocks[lax.rem(list_ref[1, slot], b_blocks.shape[0])]
        total = jnp.zeros((edge, rank), f32)
        for j in range(edge):
            total += e_ref[slot, j * edge:(j + 1) * edge, :] * b_block[j:j + 1, :]
        part[slot] = total
        return carry

    lax.fori_loop(0, half, third_step, 0)
    arrive(z_copies)
    gram_sum[rows_of(gram_sum), :] = total_of(z_land)
    gram_copies = net.spread("aux", gram_sum, rank // count)
    lax.fori_loop(half, slots, third_step, 0)
    gather_blocks(2, thirds)
    third_copies = net.scatter("aux", thirds, thirds_land)

    arrive(gram_copies)
    unit_b, scale_b = unit_gram(gram_sum[...], orb_rows * size)
    work[...] = unit_b * unit_gram(gram_a[...], P_SIZE)[0] + ridge
    panels = rank // PANEL
    sweep_inverse(work, None, 0, panels // 2)
    arrive(third_copies)
    thirds_land[mine] = total_of(thirds_land)
    third_copies = net.share("orb", thirds_land.at[mine], thirds_z)
    sweep_inverse(work, None, panels // 2, panels - 1)
    arrive(third_copies)
    third_sums[rows_of(third_sums), :] = total_of(thirds_z)
    third_copies = net.spread("aux", third_sums, nu_rows // count)
    sweep_inverse(work, None, panels - 1, panels)
    inverse = split_three(-work[...])
    b_out[...] = b_full[...] / scale_b
    arrive(third_copies)
    c_new = dot_exact(split_three(third_sums[...] / scale_a / scale_b), inverse)
    scale_c = jnp.sqrt(jnp.sum(c_new * c_new, axis=0, keepdims=True) / nu_rows + epsilon)
    c_out[...] = c_new / scale_c
    net.finish()


def per_device(tiles, tile_list, orb_factor, nu_factor):
    slots, edge = tiles.shape[0], tiles.shape[1]
    rank = nu_factor.shape[1]
    first_rows = P_SIZE // lax.axis_size("aux")
    orb_rows = orb_factor.shape[0]
    orb_size = lax.axis_size("orb")
    tile_width = tiles.shape[2]
    aux_size = lax.axis_size("aux")
    vmem = pl.BlockSpec(memory_space=pltpu.VMEM)
    blocks = slots * orb_size
    square = pltpu.VMEM((rank, rank), f32)
    net_count = 2 * (orb_size - 1) + aux_size - 1
    parts, table, inverse_first, s_nu = pl.pallas_call(
        functools.partial(first_kernel, edge),
        out_shape=(
            jax.ShapeDtypeStruct((blocks * edge, rank), f32),
            jax.ShapeDtypeStruct((blocks, 128), jnp.int32),
            jax.ShapeDtypeStruct((rank, rank), f32),
            jax.ShapeDtypeStruct((rank, rank), f32),
        ),
        in_specs=[
            pl.BlockSpec(memory_space=pltpu.SMEM),
            pl.BlockSpec(memory_space=pltpu.HBM),
            vmem,
            vmem,
        ],
        out_specs=(vmem, vmem, vmem, vmem),
        scratch_shapes=[
            pltpu.VMEM((slots, edge, tile_width), f32),
            pltpu.VMEM((blocks * edge, rank), f32),
            pltpu.VMEM((blocks, 128), f32),
            square,
            square,
            square,
            pltpu.VMEM((orb_size, rank // aux_size, rank), f32),
            square,
            pltpu.SemaphoreType.DMA((slots,)),
            pltpu.SemaphoreType.DMA((net_count,)),
            pltpu.SemaphoreType.DMA((net_count,)),
            pltpu.SemaphoreType.DMA((2, orb_size - 1, slots)),
            pltpu.SemaphoreType.DMA((2, orb_size - 1, slots)),
        ],
        compiler_params=pltpu.CompilerParams(
            collective_id=5, has_side_effects=True, vmem_limit_bytes=60 << 20
        ),
        name="first_gather",
    )(tile_list, tiles, orb_factor.reshape(-1, edge, rank), nu_factor.reshape(-1, edge, rank))
    a_new, gram_a = pl.pallas_call(
        functools.partial(solve_kernel, edge, blocks),
        out_shape=(
            jax.ShapeDtypeStruct((first_rows, rank), f32),
            jax.ShapeDtypeStruct((rank, rank), f32),
        ),
        in_specs=[pl.BlockSpec(memory_space=pltpu.SMEM), vmem, vmem],
        out_specs=(vmem, vmem),
        scratch_shapes=[pltpu.VMEM((first_rows, rank), f32), square, square],
        compiler_params=pltpu.CompilerParams(vmem_limit_bytes=60 << 20),
        name="solve_first",
    )(table, parts, inverse_first)
    orb_blocks = orb_rows // edge
    nu_rows = nu_factor.shape[0]
    net_count = 7 * (aux_size - 1) + 2 * (orb_size - 1)

    def room(*shape):
        return pltpu.VMEM(shape, f32)

    orb_updated, nu_updated, scale = pl.pallas_call(
        functools.partial(sweep_kernel, edge),
        out_shape=(
            jax.ShapeDtypeStruct((orb_rows, rank), f32),
            jax.ShapeDtypeStruct((nu_rows, rank), f32),
            jax.ShapeDtypeStruct((8, rank), f32),
        ),
        in_specs=[
            pl.BlockSpec(memory_space=pltpu.SMEM),
            pl.BlockSpec(memory_space=pltpu.HBM),
            vmem,
            vmem,
            vmem,
            vmem,
        ],
        out_specs=(vmem, vmem, vmem),
        scratch_shapes=[
            room(slots, edge, tile_width),
            room(slots, tile_width, rank),
            room(slots, edge, rank),
            square,
            square,
            square,
            room(aux_size, rank // aux_size, rank),
            square,
            room(orb_rows, rank),
            room(aux_size, orb_rows // aux_size, rank),
            room(orb_rows, rank),
            room(orb_blocks, edge, rank),
            square,
            room(orb_size, rank // aux_size, rank),
            square,
            room(nu_rows, rank),
            room(aux_size, nu_rows // aux_size, rank),
            room(orb_size, nu_rows // aux_size, rank),
            room(nu_rows, rank),
            pltpu.SemaphoreType.DMA((slots,)),
            pltpu.SemaphoreType.DMA((net_count,)),
            pltpu.SemaphoreType.DMA((net_count,)),
        ],
        compiler_params=pltpu.CompilerParams(
            collective_id=6, has_side_effects=True, vmem_limit_bytes=60 << 20
        ),
        name="second_third",
    )(
        tile_list,
        tiles,
        nu_factor.reshape(-1, edge, rank),
        a_new.reshape(-1, edge, rank),
        gram_a,
        s_nu,
    )
    return (a_new / scale[:1], orb_updated, nu_updated)


def solution(mesh):
    return jax.shard_map(
        per_device,
        mesh=mesh,
        in_specs=(P(("aux", "orb"), None, None), P(None, ("aux", "orb")), P("orb", None), P()),
        out_specs=(P("aux", None), P("orb", None), P()),
        check_vma=False,
    )
```

```python
import functools

import jax
import jax.numpy as jnp
from jax import lax
from jax.experimental import pallas as pl
from jax.experimental.pallas import tpu as pltpu
from jax.sharding import PartitionSpec as P

P_SIZE = 16384
MU = 4096
NU = 512

ridge_weight = 0.5
epsilon = 1e-06
highest = lax.Precision.HIGHEST
f32 = jnp.float32
bf16 = jnp.bfloat16
PANEL = 32


MESH = pl.DeviceIdType.MESH


def split_two(x):
    high = x.astype(bf16)
    return high, (x - high.astype(f32)).astype(bf16)


def split_three(x):
    high = x.astype(bf16)
    rest = x - high.astype(f32)
    middle = rest.astype(bf16)
    return high, middle, (rest - middle.astype(f32)).astype(bf16)


def aligned(value, step):
    return pl.multiple_of(value, step)


def dot_t(left, right):
    return lax.dot_general(left, right, (((0,), (0,)), ((), ())), preferred_element_type=f32)


def dot_exact(left, right):
    l_high, l_middle, l_low = left
    r_high, r_middle, r_low = right
    dot = functools.partial(jnp.dot, preferred_element_type=f32)
    small = dot(l_low, r_high) + dot(l_high, r_low) + dot(l_middle, r_middle)
    return dot(l_high, r_high) + (dot(l_middle, r_high) + dot(l_high, r_middle) + small)


def gram_add(x, even_ref, odd_ref):
    high, middle, low = split_three(x)
    pair = jnp.concatenate([high, middle], axis=0)
    even_ref[...] += dot_t(pair, pair)
    odd_ref[...] += dot_t(
        jnp.concatenate([high, high], axis=0), jnp.concatenate([middle, low], axis=0)
    )


def gram_rows(x_ref, even_ref, odd_ref):
    even_ref[...] = jnp.zeros_like(even_ref)
    odd_ref[...] = jnp.zeros_like(odd_ref)
    group = min(4, x_ref.shape[0])

    def step(at, carry):
        rows = x_ref[pl.ds(at * group, group)]
        gram_add(rows.reshape(-1, rows.shape[2]), even_ref, odd_ref)
        return carry

    lax.fori_loop(0, x_ref.shape[0] // group, step, 0)
    odd = odd_ref[...]
    return even_ref[...] + (odd + odd.T)


def enter(axes):
    barrier = pltpu.get_barrier_semaphore()
    count = 0
    for axis in axes:
        size, here = lax.axis_size(axis), lax.axis_index(axis)
        for step in range(1, size):
            pl.semaphore_signal(
                barrier, inc=1, device_id={axis: (here + step) % size}, device_id_type=MESH
            )
            count += 1
    pl.semaphore_wait(barrier, count)


class Net:
    def __init__(self, send, recv):
        self.send, self.recv, self.copies = send, recv, []

    def copy(self, src, dst, to):
        at = len(self.copies)
        copy = pltpu.make_async_remote_copy(
            src_ref=src,
            dst_ref=dst,
            send_sem=self.send.at[at],
            recv_sem=self.recv.at[at],
            device_id=to,
            device_id_type=MESH,
        )
        copy.start()
        self.copies.append(copy)
        return copy

    def scatter(self, axis, src, land):
        size, here = lax.axis_size(axis), lax.axis_index(axis)
        rows = land.shape[1]
        land[here] = src[pl.ds(aligned(here * rows, 8), rows), :]
        copies = []
        for step in range(1, size):
            to = (here + step) % size
            block = src.at[pl.ds(aligned(to * rows, 8), rows), :]
            copies.append(self.copy(block, land.at[here], {axis: to}))
        return copies

    def share(self, axis, src, land):
        size, here = lax.axis_size(axis), lax.axis_index(axis)
        land[here] = src[...]
        return [
            self.copy(src, land.at[here], {axis: (here + step) % size}) for step in range(1, size)
        ]

    def spread(self, axis, full, rows):
        size, here = lax.axis_size(axis), lax.axis_index(axis)
        own = full.at[pl.ds(aligned(here * rows, 8), rows), :]
        return [self.copy(own, own, {axis: (here + step) % size}) for step in range(1, size)]

    def finish(self):
        for copy in self.copies:
            copy.wait_send()


def arrive(copies):
    for copy in copies:
        copy.wait_recv()


def total_of(land):
    total = land[0]
    for at in range(1, land.shape[0]):
        total += land[at]
    return total


def first_kernel(
    edge, list_ref, x_hbm, orb_ref, nu_ref, parts_out, table_out, inverse_out, s_nu_out,
    x_buf, parts, table, even, odd, gram, gram_land, work, x_sem, send, recv, hop_send, hop_recv
):
    slots = list_ref.shape[1]
    here, size = lax.axis_index("orb"), lax.axis_size("orb")
    mine = lax.axis_index("aux")
    rank = nu_ref.shape[2]
    orb_rows = orb_ref.shape[0] * edge
    first_base = mine * (P_SIZE // lax.axis_size("aux") // edge)
    gram_rows_each = gram_land.shape[1]

    def load(slot):
        return pltpu.make_async_copy(x_hbm.at[slot], x_buf.at[slot], x_sem.at[slot])

    for slot in range(slots):
        load(slot).start()
    enter(("aux", "orb"))
    net = Net(send, recv)

    def hop(way, distance, slot):
        at = ((here - way * distance) * slots + slot) * edge
        rows = parts.at[pl.ds(aligned(at, edge), edge), :]
        lane = 0 if way > 0 else 1
        return pltpu.make_async_remote_copy(
            src_ref=rows,
            dst_ref=rows,
            send_sem=hop_send.at[lane, distance, slot],
            recv_sem=hop_recv.at[lane, distance, slot],
            device_id={"orb": here + way},
            device_id_type=MESH,
        )

    def landed(way, distance, slot):
        at = ((here - way * distance) * slots + slot) * edge
        rows = parts.at[pl.ds(aligned(at, edge), edge), :]
        lane = 0 if way > 0 else 1
        return pltpu.make_async_remote_copy(
            src_ref=rows,
            dst_ref=rows,
            send_sem=hop_send.at[lane, distance - 1, slot],
            recv_sem=hop_recv.at[lane, distance - 1, slot],
            device_id={"orb": here - way},
            device_id_type=MESH,
        )

    def goes(way, distance):
        at = here if way > 0 else size - 1 - here
        return (at + size - 1 - distance) // (size - 1) * ((2 * size - 3 - at) // (size - 1)) > 0

    def ends(way, distance):
        return here == size - 1 if way > 0 else here == 0

    def forward(distance, slot):
        for way in (1, -1):

            @pl.when(goes(way, distance))
            def _():
                landed(way, distance, slot).wait_recv()
                hop(way, distance, slot).start()

    def slot_step(slot, carry):
        load(slot).wait()
        nu_block = nu_ref[list_ref[2, slot]]
        orb_block = orb_ref[lax.rem(list_ref[1, slot], orb_ref.shape[0])]
        group = 4
        total = jnp.zeros((edge, rank), f32)
        for start in range(0, edge, group):
            x_high, x_low = split_two(x_buf[slot, :, start * edge:(start + group) * edge])
            stacked = jnp.concatenate([x_high, x_low], axis=0)
            product = jnp.concatenate(
                [nu_block * orb_block[j:j + 1, :] for j in range(start, start + group)], axis=0
            )
            high, low = split_two(product)
            main = jnp.dot(stacked, high, preferred_element_type=f32)
            rest = jnp.dot(x_high, low, preferred_element_type=f32)
            total += main[:edge] + (main[edge:] + rest)
        live = list_ref[3, slot].astype(f32)
        parts[pl.ds(aligned((here * slots + slot) * edge, edge), edge), :] = total * live
        for way in (1, -1):

            @pl.when(goes(way, 0))
            def _():
                hop(way, 0, slot).start()

        return carry

    early, late = slots // 4, slots - slots // 4
    lax.fori_loop(0, early, slot_step, 0)

    row = lax.broadcasted_iota(jnp.int32, (slots, table.shape[1]), 0)
    own_at = jnp.zeros((slots, table.shape[1]), f32)
    for slot in range(slots):
        value = (list_ref[0, slot] - first_base).astype(f32)
        own_at = jnp.where(row == slot, value, own_at)
    table[pl.ds(aligned(here * slots, 8), slots), :] = own_at
    table_copies = net.spread("orb", table, slots)
    gram[...] = gram_rows(orb_ref, even, odd)
    gram_copies = []
    for step in range(1, size):
        block = gram.at[pl.ds(aligned(mine * gram_rows_each, 8), gram_rows_each), :]
        gram_copies.append(net.copy(block, gram_land.at[here], {"orb": (here + step) % size}))
    gram_land[here] = gram[pl.ds(aligned(mine * gram_rows_each, 8), gram_rows_each), :]
    s_nu = gram_rows(nu_ref, even, odd) / NU
    s_nu_out[...] = s_nu
    lax.fori_loop(early, late, slot_step, 0)
    arrive(gram_copies)
    work[pl.ds(aligned(mine * gram_rows_each, 8), gram_rows_each), :] = total_of(gram_land)
    share_copies = net.spread("aux", work, gram_rows_each)
    lax.fori_loop(late, slots, slot_step, 0)

    if size > 2:

        def near(slot, carry):
            forward(1, slot)
            return carry

        lax.fori_loop(0, slots, near, 0)
    arrive(share_copies)
    even[...] = work[...] / (orb_rows * size) * s_nu_out[...] + jnp.where(
        eye_mask(rank), ridge_weight, 0.0
    )

    def beside(step):
        if size > 3:
            forward(2, step)

    sweep_inverse(even, beside if rank // PANEL == slots else None)
    inverse_out[...] = -even[...]
    far = 2 if rank // PANEL != slots else 3
    for distance in range(far, size - 1):

        def pass_on(slot, carry, distance=distance):
            forward(distance, slot)
            return carry

        lax.fori_loop(0, slots, pass_on, 0)

    def last(slot, carry):
        for way in (1, -1):
            for distance in range(1, size):

                @pl.when(ends(way, distance))
                def _():
                    landed(way, distance, slot).wait_recv()

            for distance in range(size - 1):

                @pl.when(goes(way, distance))
                def _():
                    hop(way, distance, slot).wait_send()

        return carry

    lax.fori_loop(0, slots, last, 0)
    arrive(table_copies)
    net.finish()
    parts_out[...] = parts[...]
    table_out[...] = table[...].astype(jnp.int32)


def solve_kernel(edge, blocks, at_ref, part_ref, inverse_ref, a_ref, gram_ref, total_ref, even, odd):
    total_ref[...] = jnp.zeros_like(total_ref)

    def add_block(block, carry):
        rows = pl.ds(aligned(at_ref[block, 0] * edge, edge), edge)
        total_ref[rows, :] += part_ref[pl.ds(aligned(block * edge, edge), edge), :]
        return carry

    lax.fori_loop(0, blocks, add_block, 0)
    inverse = split_three(inverse_ref[...])
    even[...] = jnp.zeros_like(even)
    odd[...] = jnp.zeros_like(odd)
    chunk = min(512, total_ref.shape[0])

    def apply(step, carry):
        rows = pl.ds(aligned(step * chunk, chunk), chunk)
        solved = dot_exact(split_three(total_ref[rows, :]), inverse)
        a_ref[rows, :] = solved
        gram_add(solved, even, odd)
        return carry

    lax.fori_loop(0, total_ref.shape[0] // chunk, apply, 0)
    cross = odd[...]
    gram_ref[...] = even[...] + (cross + cross.T)


def eye_mask(n):
    return lax.broadcasted_iota(jnp.int32, (n, n), 0) == lax.broadcasted_iota(jnp.int32, (n, n), 1)


def unit_gram(gram, rows):
    diagonal = jnp.where(eye_mask(gram.shape[0]), gram, 0.0)
    along = jnp.sqrt(jnp.sum(diagonal, axis=0, keepdims=True) / rows + epsilon)
    down = jnp.sqrt(jnp.sum(diagonal, axis=1, keepdims=True) / rows + epsilon)
    return gram / down / along / rows, along


def pivot_panel(tiles, cols, lane, row):
    height = len(tiles[0])
    sub = tiles[0][0].shape[0]

    def columns(first):
        return [
            [jnp.broadcast_to(tile[:, k:k + 1], tile.shape) for tile in tiles[0]]
            for k in range(first, first + cols)
        ]

    def take(pieces, k):
        at = k % sub
        return pieces[k // sub][at:at + 1, :]

    def step(pieces, firsts, seconds, k, new_first, new_second, clear=None):
        out = []
        for g in range(height):
            base = pieces[g] if clear is None else jnp.where(clear, 0.0, pieces[g])
            value = base - firsts[g] * new_first - seconds[g] * new_second
            if g == k // sub:
                value = jnp.where(row == k % sub, new_first, value)
                value = jnp.where(row == k % sub + 1, new_second, value)
            out.append(value)
        return out

    now = columns(0)
    later = None
    for start in range(0, height * sub, cols):
        for j in range(0, cols, 2):
            k = start + j
            if j == cols // 2 and start + cols < height * sub:
                later = columns(start + cols)
            firsts, seconds = now[j], now[j + 1]
            a, b = take(firsts, k), take(seconds, k)
            c, d = take(firsts, k + 1), take(seconds, k + 1)
            scale = 1.0 / (a * d - b * c)
            a, b, c, d = d * scale, b * scale, c * scale, a * scale
            for i in range(j + 2, cols):
                up, down = take(now[i], k), take(now[i], k + 1)
                now[i] = step(now[i], firsts, seconds, k, a * up - b * down, d * down - c * up)
            if later is not None:
                for i in range(cols):
                    up, down = take(later[i], k), take(later[i], k + 1)
                    later[i] = step(
                        later[i], firsts, seconds, k, a * up - b * down, d * down - c * up
                    )
            for h, pieces in enumerate(tiles):
                up, down = take(pieces, k), take(pieces, k + 1)
                clear = None
                if h == 0:
                    at_up, at_down = lane == k, lane == k + 1
                    clear = at_up | at_down
                    up = jnp.where(at_up[:1], 1.0, jnp.where(at_down[:1], 0.0, up))
                    down = jnp.where(at_down[:1], 1.0, jnp.where(at_up[:1], 0.0, down))
                tiles[h] = step(
                    pieces, firsts, seconds, k, a * up - b * down, d * down - c * up, clear
                )
        now, later = later, None
    return tiles


def sweep_inverse(a_ref, beside=None, first=0, last=None):
    n = a_ref.shape[0]
    sub, wide = 8, 128
    lane = lax.broadcasted_iota(jnp.int32, (PANEL, n), 1)
    tile_lane = lax.broadcasted_iota(jnp.int32, (sub, wide), 1)
    tile_row = lax.broadcasted_iota(jnp.int32, (sub, wide), 0)

    def panel_step(step, carry):
        if beside is not None:
            beside(step)
        before = a_ref[:PANEL, :]
        tiles = [
            [before[g:g + sub, h:h + wide] for g in range(0, PANEL, sub)]
            for h in range(0, n, wide)
        ]
        tiles = pivot_panel(tiles, 8, tile_lane, tile_row)
        panel = jnp.concatenate([jnp.concatenate(pieces, axis=0) for pieces in tiles], axis=1)
        own = lane < PANEL
        update = jnp.where(own, -panel, panel)
        w_high, w_middle, w_low = split_three(before)
        z_high, z_middle, z_low = split_three(update)
        left = jnp.concatenate([w_low, w_middle, w_high, w_middle, w_high, w_high], axis=0)
        right = jnp.concatenate([z_high, z_middle, z_low, z_high, z_middle, z_high], axis=0)
        change = lax.dot_general(
            left, right, (((0,), (0,)), ((), ())), preferred_element_type=f32
        )
        others = jnp.where(own[:1], 0.0, a_ref[PANEL:, :]) - change[PANEL:, :]
        a_ref[:n - PANEL, :] = pltpu.roll(others, n - PANEL, 1)
        a_ref[n - PANEL:, :] = pltpu.roll(update, n - PANEL, 1)
        return carry

    lax.fori_loop(first, n // PANEL if last is None else last, panel_step, 0)


def sweep_kernel(
    edge, list_ref, x_hbm, nu_ref, a_ref, gram_ref, s_nu_ref, b_out, c_out, scale_out,
    x_buf, e_ref, part, work, even, odd, gram_land, gram_a, terms, terms_land, b_full, b_blocks,
    gram_b, z_land, gram_sum, thirds, thirds_land, thirds_z, third_sums, x_sem, send, recv
):
    slots = list_ref.shape[1]
    here, size = lax.axis_index("orb"), lax.axis_size("orb")
    mine, count = lax.axis_index("aux"), lax.axis_size("aux")
    rank = nu_ref.shape[2]
    orb_rows, nu_rows = b_full.shape[0], third_sums.shape[0]
    half = slots // 2

    def load(slot):
        return pltpu.make_async_copy(x_hbm.at[slot], x_buf.at[slot], x_sem.at[slot])

    for slot in range(slots):
        load(slot).start()
    enter(("aux", "orb"))
    net = Net(send, recv)
    gram_copies = net.scatter("aux", gram_ref, gram_land)

    def rows_of(ref):
        return pl.ds(aligned(mine * (ref.shape[0] // count), 8), ref.shape[0] // count)

    def second_step(slot, carry):
        load(slot).wait()
        nu_block = nu_ref[list_ref[2, slot]]
        a_high, a_low = split_two(a_ref[lax.rem(list_ref[0, slot], a_ref.shape[0])])
        weights = jnp.concatenate([a_high, a_high, a_low, a_low], axis=0)
        group = 8
        for start in range(0, edge, group):
            x_high, x_low = split_two(x_buf[slot, :, start * edge:(start + group) * edge])
            turned = jnp.concatenate([x_high, x_low], axis=0).T
            e = jnp.dot(
                jnp.concatenate([turned, turned], axis=1), weights, preferred_element_type=f32
            )
            e_ref[slot, start * edge:(start + group) * edge, :] = e
            part[slot, start:start + group, :] = jnp.sum(
                e.reshape(group, edge, rank) * nu_block[None], axis=1
            )
        return carry

    def gather_blocks(dimension, out_ref):
        blocks = out_ref.shape[0] // edge
        places = [lax.rem(list_ref[dimension, slot], blocks) for slot in range(slots)]
        lives = [list_ref[3, slot].astype(f32) for slot in range(slots)]

        def block_step(block, carry):
            total = jnp.zeros((edge, rank), f32)
            for slot in range(slots):
                weight = (places[slot] == block).astype(f32) * lives[slot]
                total += part[slot] * weight
            out_ref[pl.ds(aligned(block * edge, edge), edge), :] = total
            return carry

        lax.fori_loop(0, blocks, block_step, 0)

    lax.fori_loop(0, half, second_step, 0)
    arrive(gram_copies)
    gram_a[rows_of(gram_a), :] = total_of(gram_land)
    gram_copies = net.spread("aux", gram_a, rank // count)
    lax.fori_loop(half, slots, second_step, 0)
    gather_blocks(1, terms)
    terms_copies = net.scatter("aux", terms, terms_land)

    arrive(gram_copies)
    unit_a, scale_a = unit_gram(gram_a[...], P_SIZE)
    ridge = jnp.where(eye_mask(rank), ridge_weight, 0.0)
    work[...] = unit_a * s_nu_ref[...] + ridge
    sweep_inverse(work)
    inverse = split_three(-work[...])
    arrive(terms_copies)
    b_own = dot_exact(split_three(total_of(terms_land) / scale_a), inverse)
    b_full[rows_of(b_full), :] = b_own
    b_copies = net.spread("aux", b_full, orb_rows // count)
    scale_out[...] = jnp.broadcast_to(scale_a, scale_out.shape)
    arrive(b_copies)
    b_blocks[...] = b_full[...].reshape(b_blocks.shape)
    gram_b[...] = gram_rows(b_blocks, even, odd)
    z_copies = net.share("orb", gram_b.at[rows_of(gram_b), :], z_land)

    def third_step(slot, carry):
        b_block = b_blocks[lax.rem(list_ref[1, slot], b_blocks.shape[0])]
        total = jnp.zeros((edge, rank), f32)
        for j in range(edge):
            total += e_ref[slot, j * edge:(j + 1) * edge, :] * b_block[j:j + 1, :]
        part[slot] = total
        return carry

    lax.fori_loop(0, slots, third_step, 0)
    gather_blocks(2, thirds)
    third_copies = net.scatter("aux", thirds, thirds_land)
    arrive(z_copies)
    gram_sum[rows_of(gram_sum), :] = total_of(z_land)
    gram_copies = net.spread("aux", gram_sum, rank // count)

    arrive(gram_copies)
    unit_b, scale_b = unit_gram(gram_sum[...], orb_rows * size)
    work[...] = unit_b * unit_gram(gram_a[...], P_SIZE)[0] + ridge
    panels = rank // PANEL
    sweep_inverse(work, None, 0, panels // 2)
    arrive(third_copies)
    thirds_land[mine] = total_of(thirds_land)
    third_copies = net.share("orb", thirds_land.at[mine], thirds_z)
    sweep_inverse(work, None, panels // 2, panels - 1)
    arrive(third_copies)
    third_sums[rows_of(third_sums), :] = total_of(thirds_z)
    third_copies = net.spread("aux", third_sums, nu_rows // count)
    sweep_inverse(work, None, panels - 1, panels)
    inverse = split_three(-work[...])
    b_out[...] = b_full[...] / scale_b
    arrive(third_copies)
    c_new = dot_exact(split_three(third_sums[...] / scale_a / scale_b), inverse)
    scale_c = jnp.sqrt(jnp.sum(c_new * c_new, axis=0, keepdims=True) / nu_rows + epsilon)
    c_out[...] = c_new / scale_c
    net.finish()


def per_device(tiles, tile_list, orb_factor, nu_factor):
    slots, edge = tiles.shape[0], tiles.shape[1]
    rank = nu_factor.shape[1]
    first_rows = P_SIZE // lax.axis_size("aux")
    orb_rows = orb_factor.shape[0]
    orb_size = lax.axis_size("orb")
    tile_width = tiles.shape[2]
    aux_size = lax.axis_size("aux")
    vmem = pl.BlockSpec(memory_space=pltpu.VMEM)
    blocks = slots * orb_size
    square = pltpu.VMEM((rank, rank), f32)
    net_count = 2 * (orb_size - 1) + aux_size - 1
    parts, table, inverse_first, s_nu = pl.pallas_call(
        functools.partial(first_kernel, edge),
        out_shape=(
            jax.ShapeDtypeStruct((blocks * edge, rank), f32),
            jax.ShapeDtypeStruct((blocks, 128), jnp.int32),
            jax.ShapeDtypeStruct((rank, rank), f32),
            jax.ShapeDtypeStruct((rank, rank), f32),
        ),
        in_specs=[
            pl.BlockSpec(memory_space=pltpu.SMEM),
            pl.BlockSpec(memory_space=pltpu.HBM),
            vmem,
            vmem,
        ],
        out_specs=(vmem, vmem, vmem, vmem),
        scratch_shapes=[
            pltpu.VMEM((slots, edge, tile_width), f32),
            pltpu.VMEM((blocks * edge, rank), f32),
            pltpu.VMEM((blocks, 128), f32),
            square,
            square,
            square,
            pltpu.VMEM((orb_size, rank // aux_size, rank), f32),
            square,
            pltpu.SemaphoreType.DMA((slots,)),
            pltpu.SemaphoreType.DMA((net_count,)),
            pltpu.SemaphoreType.DMA((net_count,)),
            pltpu.SemaphoreType.DMA((2, orb_size - 1, slots)),
            pltpu.SemaphoreType.DMA((2, orb_size - 1, slots)),
        ],
        compiler_params=pltpu.CompilerParams(
            collective_id=5, has_side_effects=True, vmem_limit_bytes=60 << 20
        ),
        name="first_gather",
    )(tile_list, tiles, orb_factor.reshape(-1, edge, rank), nu_factor.reshape(-1, edge, rank))
    a_new, gram_a = pl.pallas_call(
        functools.partial(solve_kernel, edge, blocks),
        out_shape=(
            jax.ShapeDtypeStruct((first_rows, rank), f32),
            jax.ShapeDtypeStruct((rank, rank), f32),
        ),
        in_specs=[pl.BlockSpec(memory_space=pltpu.SMEM), vmem, vmem],
        out_specs=(vmem, vmem),
        scratch_shapes=[pltpu.VMEM((first_rows, rank), f32), square, square],
        compiler_params=pltpu.CompilerParams(vmem_limit_bytes=60 << 20),
        name="solve_first",
    )(table, parts, inverse_first)
    orb_blocks = orb_rows // edge
    nu_rows = nu_factor.shape[0]
    net_count = 7 * (aux_size - 1) + 2 * (orb_size - 1)

    def room(*shape):
        return pltpu.VMEM(shape, f32)

    orb_updated, nu_updated, scale = pl.pallas_call(
        functools.partial(sweep_kernel, edge),
        out_shape=(
            jax.ShapeDtypeStruct((orb_rows, rank), f32),
            jax.ShapeDtypeStruct((nu_rows, rank), f32),
            jax.ShapeDtypeStruct((8, rank), f32),
        ),
        in_specs=[
            pl.BlockSpec(memory_space=pltpu.SMEM),
            pl.BlockSpec(memory_space=pltpu.HBM),
            vmem,
            vmem,
            vmem,
            vmem,
        ],
        out_specs=(vmem, vmem, vmem),
        scratch_shapes=[
            room(slots, edge, tile_width),
            room(slots, tile_width, rank),
            room(slots, edge, rank),
            square,
            square,
            square,
            room(aux_size, rank // aux_size, rank),
            square,
            room(orb_rows, rank),
            room(aux_size, orb_rows // aux_size, rank),
            room(orb_rows, rank),
            room(orb_blocks, edge, rank),
            square,
            room(orb_size, rank // aux_size, rank),
            square,
            room(nu_rows, rank),
            room(aux_size, nu_rows // aux_size, rank),
            room(orb_size, nu_rows // aux_size, rank),
            room(nu_rows, rank),
            pltpu.SemaphoreType.DMA((slots,)),
            pltpu.SemaphoreType.DMA((net_count,)),
            pltpu.SemaphoreType.DMA((net_count,)),
        ],
        compiler_params=pltpu.CompilerParams(
            collective_id=6, has_side_effects=True, vmem_limit_bytes=60 << 20
        ),
        name="second_third",
    )(
        tile_list,
        tiles,
        nu_factor.reshape(-1, edge, rank),
        a_new.reshape(-1, edge, rank),
        gram_a,
        s_nu,
    )
    return (a_new / scale[:1], orb_updated, nu_updated)


def solution(mesh):
    return jax.shard_map(
        per_device,
        mesh=mesh,
        in_specs=(P(("aux", "orb"), None, None), P(None, ("aux", "orb")), P("orb", None), P()),
        out_specs=(P("aux", None), P("orb", None), P()),
        check_vma=False,
    )
```

```python
import functools

import jax
import jax.numpy as jnp
from jax import lax
from jax.experimental import pallas as pl
from jax.experimental.pallas import tpu as pltpu
from jax.sharding import PartitionSpec as P

P_SIZE = 16384
MU = 4096
NU = 512

ridge_weight = 0.5
epsilon = 1e-06
highest = lax.Precision.HIGHEST
f32 = jnp.float32
bf16 = jnp.bfloat16
PANEL = 32


MESH = pl.DeviceIdType.MESH


def split_two(x):
    high = x.astype(bf16)
    return high, (x - high.astype(f32)).astype(bf16)


def split_three(x):
    high = x.astype(bf16)
    rest = x - high.astype(f32)
    middle = rest.astype(bf16)
    return high, middle, (rest - middle.astype(f32)).astype(bf16)


def aligned(value, step):
    return pl.multiple_of(value, step)


def dot_t(left, right):
    return lax.dot_general(left, right, (((0,), (0,)), ((), ())), preferred_element_type=f32)


def dot_exact(left, right):
    l_high, l_middle, l_low = left
    r_high, r_middle, r_low = right
    dot = functools.partial(jnp.dot, preferred_element_type=f32)
    small = dot(l_low, r_high) + dot(l_high, r_low) + dot(l_middle, r_middle)
    return dot(l_high, r_high) + (dot(l_middle, r_high) + dot(l_high, r_middle) + small)


def gram_add(x, even_ref, odd_ref):
    high, middle, low = split_three(x)
    pair = jnp.concatenate([high, middle], axis=0)
    even_ref[...] += dot_t(pair, pair)
    odd_ref[...] += dot_t(
        jnp.concatenate([high, high], axis=0), jnp.concatenate([middle, low], axis=0)
    )


def gram_rows(x_ref, even_ref, odd_ref):
    even_ref[...] = jnp.zeros_like(even_ref)
    odd_ref[...] = jnp.zeros_like(odd_ref)
    group = min(4, x_ref.shape[0])

    def step(at, carry):
        rows = x_ref[pl.ds(at * group, group)]
        gram_add(rows.reshape(-1, rows.shape[2]), even_ref, odd_ref)
        return carry

    lax.fori_loop(0, x_ref.shape[0] // group, step, 0)
    odd = odd_ref[...]
    return even_ref[...] + (odd + odd.T)


def enter(axes):
    barrier = pltpu.get_barrier_semaphore()
    count = 0
    for axis in axes:
        size, here = lax.axis_size(axis), lax.axis_index(axis)
        for step in range(1, size):
            pl.semaphore_signal(
                barrier, inc=1, device_id={axis: (here + step) % size}, device_id_type=MESH
            )
            count += 1
    pl.semaphore_wait(barrier, count)


class Net:
    def __init__(self, send, recv):
        self.send, self.recv, self.copies = send, recv, []

    def copy(self, src, dst, to):
        at = len(self.copies)
        copy = pltpu.make_async_remote_copy(
            src_ref=src,
            dst_ref=dst,
            send_sem=self.send.at[at],
            recv_sem=self.recv.at[at],
            device_id=to,
            device_id_type=MESH,
        )
        copy.start()
        self.copies.append(copy)
        return copy

    def scatter(self, axis, src, land):
        size, here = lax.axis_size(axis), lax.axis_index(axis)
        rows = land.shape[1]
        land[here] = src[pl.ds(aligned(here * rows, 8), rows), :]
        copies = []
        for step in range(1, size):
            to = (here + step) % size
            block = src.at[pl.ds(aligned(to * rows, 8), rows), :]
            copies.append(self.copy(block, land.at[here], {axis: to}))
        return copies

    def share(self, axis, src, land):
        size, here = lax.axis_size(axis), lax.axis_index(axis)
        land[here] = src[...]
        return [
            self.copy(src, land.at[here], {axis: (here + step) % size}) for step in range(1, size)
        ]

    def spread(self, axis, full, rows):
        size, here = lax.axis_size(axis), lax.axis_index(axis)
        own = full.at[pl.ds(aligned(here * rows, 8), rows), :]
        return [self.copy(own, own, {axis: (here + step) % size}) for step in range(1, size)]

    def spread_pairs(self, axis, full, rows, landed=None):
        size, here = lax.axis_size(axis), lax.axis_index(axis)
        chips, chip, core = size // 2, here // 2, here % 2
        other = here + 1 - 2 * core

        def block(owner):
            return full.at[pl.ds(aligned(owner * rows, 8), rows), :]

        own = block(here)
        far = [
            self.copy(own, own, {axis: (chip + step) % chips * 2 + core})
            for step in range(1, chips)
        ]
        near = [self.copy(own, own, {axis: other})]
        if landed is not None:
            landed(here)
        for step, copy in enumerate(far, 1):
            source = (chip + chips - step) % chips * 2
            copy.wait_recv()
            near.append(self.copy(block(source + core), block(source + core), {axis: other}))
            if landed is not None:
                landed(source + core)
        for step, copy in enumerate(near):
            copy.wait_recv()
            if landed is not None:
                landed((chip + chips - step) % chips * 2 + 1 - core)

    def finish(self):
        for copy in self.copies:
            copy.wait_send()


def arrive(copies):
    for copy in copies:
        copy.wait_recv()


def total_of(land):
    total = land[0]
    for at in range(1, land.shape[0]):
        total += land[at]
    return total


def eye_mask(n):
    return lax.broadcasted_iota(jnp.int32, (n, n), 0) == lax.broadcasted_iota(jnp.int32, (n, n), 1)


def unit_gram(gram, rows):
    diagonal = jnp.where(eye_mask(gram.shape[0]), gram, 0.0)
    along = jnp.sqrt(jnp.sum(diagonal, axis=0, keepdims=True) / rows + epsilon)
    down = jnp.sqrt(jnp.sum(diagonal, axis=1, keepdims=True) / rows + epsilon)
    return gram / down / along / rows, along


def pivot_panel(tiles, cols, lane, row):
    height = len(tiles[0])
    sub = tiles[0][0].shape[0]

    def columns(first):
        return [
            [jnp.broadcast_to(tile[:, k:k + 1], tile.shape) for tile in tiles[0]]
            for k in range(first, first + cols)
        ]

    def take(pieces, k):
        at = k % sub
        return pieces[k // sub][at:at + 1, :]

    def step(pieces, firsts, seconds, k, new_first, new_second, clear=None):
        out = []
        for g in range(height):
            base = pieces[g] if clear is None else jnp.where(clear, 0.0, pieces[g])
            value = base - firsts[g] * new_first - seconds[g] * new_second
            if g == k // sub:
                value = jnp.where(row == k % sub, new_first, value)
                value = jnp.where(row == k % sub + 1, new_second, value)
            out.append(value)
        return out

    now = columns(0)
    later = None
    for start in range(0, height * sub, cols):
        for j in range(0, cols, 2):
            k = start + j
            if j == cols // 2 and start + cols < height * sub:
                later = columns(start + cols)
            firsts, seconds = now[j], now[j + 1]
            a, b = take(firsts, k), take(seconds, k)
            c, d = take(firsts, k + 1), take(seconds, k + 1)
            scale = 1.0 / (a * d - b * c)
            a, b, c, d = d * scale, b * scale, c * scale, a * scale
            for i in range(j + 2, cols):
                up, down = take(now[i], k), take(now[i], k + 1)
                now[i] = step(now[i], firsts, seconds, k, a * up - b * down, d * down - c * up)
            if later is not None:
                for i in range(cols):
                    up, down = take(later[i], k), take(later[i], k + 1)
                    later[i] = step(
                        later[i], firsts, seconds, k, a * up - b * down, d * down - c * up
                    )
            for h, pieces in enumerate(tiles):
                up, down = take(pieces, k), take(pieces, k + 1)
                clear = None
                if h == 0:
                    at_up, at_down = lane == k, lane == k + 1
                    clear = at_up | at_down
                    up = jnp.where(at_up[:1], 1.0, jnp.where(at_down[:1], 0.0, up))
                    down = jnp.where(at_down[:1], 1.0, jnp.where(at_up[:1], 0.0, down))
                tiles[h] = step(
                    pieces, firsts, seconds, k, a * up - b * down, d * down - c * up, clear
                )
        now, later = later, None
    return tiles


def sweep_inverse(a_ref, beside=None, first=0, last=None):
    n = a_ref.shape[0]
    sub, wide = 8, 128
    lane = lax.broadcasted_iota(jnp.int32, (PANEL, n), 1)
    tile_lane = lax.broadcasted_iota(jnp.int32, (sub, wide), 1)
    tile_row = lax.broadcasted_iota(jnp.int32, (sub, wide), 0)

    def panel_step(step, carry):
        if beside is not None:
            beside(step)
        before = a_ref[:PANEL, :]
        tiles = [
            [before[g:g + sub, h:h + wide] for g in range(0, PANEL, sub)]
            for h in range(0, n, wide)
        ]
        tiles = pivot_panel(tiles, 8, tile_lane, tile_row)
        panel = jnp.concatenate([jnp.concatenate(pieces, axis=0) for pieces in tiles], axis=1)
        own = lane < PANEL
        update = jnp.where(own, -panel, panel)
        w_high, w_middle, w_low = split_three(before)
        z_high, z_middle, z_low = split_three(update)
        left = jnp.concatenate([w_low, w_middle, w_high, w_middle, w_high, w_high], axis=0)
        right = jnp.concatenate([z_high, z_middle, z_low, z_high, z_middle, z_high], axis=0)
        change = lax.dot_general(
            left, right, (((0,), (0,)), ((), ())), preferred_element_type=f32
        )
        others = jnp.where(own[:1], 0.0, a_ref[PANEL:, :]) - change[PANEL:, :]
        a_ref[:n - PANEL, :] = pltpu.roll(others, n - PANEL, 1)
        a_ref[n - PANEL:, :] = pltpu.roll(update, n - PANEL, 1)
        return carry

    lax.fori_loop(first, n // PANEL if last is None else last, panel_step, 0)


def sweep_kernel(
    edge, list_ref, x_hbm, orb_ref, nu_ref, a_out, b_out, c_out, scale_out, room, sems
):
    slots = list_ref.shape[1]
    here, size = lax.axis_index("orb"), lax.axis_size("orb")
    mine, count = lax.axis_index("aux"), lax.axis_size("aux")
    rank = nu_ref.shape[2]
    x_buf, parts, table, a_ref, e_ref, part = (
        room[name] for name in ("x", "parts", "table", "a", "e", "part")
    )
    work, even, odd = room["work"], room["even"], room["odd"]
    orb_rows, nu_rows = orb_ref.shape[0] * edge, nu_ref.shape[0] * edge
    first_base = mine * a_ref.shape[0]
    hop_send, hop_recv = sems["hop_send"], sems["hop_recv"]

    def load(slot):
        return pltpu.make_async_copy(x_hbm.at[slot], x_buf.at[slot], sems["x"].at[slot])

    def rows_of(ref, owner=mine):
        rows = ref.shape[0] // count
        return pl.ds(aligned(owner * rows, 8), rows)

    for slot in range(slots):
        load(slot).start()
    enter(("aux", "orb"))
    net = Net(sems["send"], sems["recv"])

    def part_rows(source, slot):
        return parts.at[pl.ds(aligned((source * slots + slot) * edge, edge), edge), :]

    def hop(way, distance, slot):
        rows = part_rows(here - way * distance, slot)
        lane = (1 - way) // 2
        return pltpu.make_async_remote_copy(
            src_ref=rows,
            dst_ref=rows,
            send_sem=hop_send.at[lane, distance, slot],
            recv_sem=hop_recv.at[lane, distance, slot],
            device_id={"orb": here + way},
            device_id_type=MESH,
        )

    def landed(way, distance, slot):
        rows = part_rows(here - way * distance, slot)
        lane = (1 - way) // 2
        return pltpu.make_async_remote_copy(
            src_ref=rows,
            dst_ref=rows,
            send_sem=hop_send.at[lane, distance - 1, slot],
            recv_sem=hop_recv.at[lane, distance - 1, slot],
            device_id={"orb": here - way},
            device_id_type=MESH,
        )

    def place(way):
        return (size - 1) * ((1 - way) // 2) + way * here

    def goes(way, distance):
        at = place(way)
        return (at + size - 1 - distance) // (size - 1) * ((2 * size - 3 - at) // (size - 1)) > 0

    def forward(distance, slot):
        for way in (1, -1):

            @pl.when(goes(way, distance))
            def _():
                landed(way, distance, slot).wait_recv()
                hop(way, distance, slot).start()

    def slot_step(slot, carry):
        load(slot).wait()
        nu_block = nu_ref[list_ref[2, slot]]
        orb_block = orb_ref[lax.rem(list_ref[1, slot], orb_ref.shape[0])]
        group = 4
        total = jnp.zeros((edge, rank), f32)
        for start in range(0, edge, group):
            x_high, x_low = split_two(x_buf[slot, :, start * edge:(start + group) * edge])
            stacked = jnp.concatenate([x_high, x_low], axis=0)
            product = jnp.concatenate(
                [nu_block * orb_block[j:j + 1, :] for j in range(start, start + group)], axis=0
            )
            high, low = split_two(product)
            main = jnp.dot(stacked, high, preferred_element_type=f32)
            rest = jnp.dot(x_high, low, preferred_element_type=f32)
            total += main[:edge] + (main[edge:] + rest)
        live = list_ref[3, slot].astype(f32)
        part_rows(here, slot)[...] = total * live
        for way in (1, -1):

            @pl.when(goes(way, 0))
            def _():
                hop(way, 0, slot).start()

        return carry

    early, late = slots // 4, slots - slots // 4
    lax.fori_loop(0, early, slot_step, 0)

    half = slots // 2
    row = lax.broadcasted_iota(jnp.int32, table.shape[1:], 0)
    for piece in range(2):
        own_at = jnp.zeros(table.shape[1:], f32)
        for slot in range(half):
            value = (list_ref[0, piece * half + slot] - first_base).astype(f32)
            own_at = jnp.where(row == slot, value, own_at)
        table[2 * here + piece] = own_at
    own_table = table.at[pl.ds(2 * here, 2)]
    table_copies = [
        net.copy(own_table, own_table, {"orb": (here + step) % size}) for step in range(1, size)
    ]
    orb_gram, orb_land, orb_sum = room["orb_gram"], room["orb_land"], room["orb_sum"]
    orb_gram[...] = gram_rows(orb_ref, even, odd)
    gram_copies = net.share("orb", orb_gram.at[rows_of(orb_gram), :], orb_land)
    room["s_nu"][...] = gram_rows(nu_ref, even, odd) / NU
    lax.fori_loop(early, late, slot_step, 0)
    arrive(gram_copies)
    orb_sum[rows_of(orb_sum), :] = total_of(orb_land)
    gram_copies = net.spread("aux", orb_sum, rank // count)
    lax.fori_loop(late, slots, slot_step, 0)

    if size > 2:

        def pass_near(slot, carry):
            forward(1, slot)
            return carry

        lax.fori_loop(0, slots, pass_near, 0)
    arrive(gram_copies)
    ridge = jnp.where(eye_mask(rank), ridge_weight, 0.0)
    work[...] = orb_sum[...] / (orb_rows * size) * room["s_nu"][...] + ridge
    panels = rank // PANEL
    together = panels == slots

    def beside(step):
        if size > 3:
            forward(2, step)

    sweep_inverse(work, beside if together else None)
    for at, piece in enumerate(split_three(-work[...])):
        room["inverse"][at] = piece
    for distance in range(3 if together else 2, size - 1):

        def pass_on(slot, carry, distance=distance):
            forward(distance, slot)
            return carry

        lax.fori_loop(0, slots, pass_on, 0)
    arrive(table_copies)

    def add_rows(source, piece, clear):
        start = piece * half
        rows = parts[pl.ds(aligned((source * slots + start) * edge, edge), half * edge), :]
        inverse = tuple(room["inverse"][at] for at in range(3))
        room["q"][...] = dot_exact(split_three(rows), inverse)
        places = table[2 * source + piece]

        def block_step(block, carry):
            name = jnp.full((1, rank), block, jnp.int32).astype(f32)
            total = jnp.zeros((edge, rank), f32) if clear else a_ref[block]
            for slot in range(half):
                weight = jnp.where(places[slot:slot + 1, :] == name, 1.0, 0.0)
                total += room["q"][slot * edge:(slot + 1) * edge, :] * weight
            a_ref[block] = total
            return carry

        lax.fori_loop(0, a_ref.shape[0], block_step, 0)

    add_rows(here, 0, True)
    add_rows(here, 1, False)

    def source_step(at, carry):
        distance, way = at // 2 + 1, 1 - at % 2 * 2
        source = here - way * distance

        @pl.when((source + size) // size * ((2 * size - 1 - source) // size) > 0)
        def _():
            def half_step(piece, carry):
                @pl.when(place(way) == size - 1)
                def _():
                    for slot in range(half):
                        landed(way, distance, piece * half + slot).wait_recv()

                add_rows(source, piece, False)
                return carry

            lax.fori_loop(0, 2, half_step, 0)

        return carry

    lax.fori_loop(0, 2 * (size - 1), source_step, 0)
    save_a = pltpu.make_async_copy(a_ref, a_out, sems["save"].at[0])
    save_a.start()

    gram_a, gram_land = room["gram_a"], room["gram_land"]
    room["gram"][...] = gram_rows(a_ref, even, odd)
    gram_copies = net.scatter("aux", room["gram"], gram_land)

    def second_step(slot, carry):
        nu_block = nu_ref[list_ref[2, slot]]
        a_high, a_low = split_two(a_ref[lax.rem(list_ref[0, slot], a_ref.shape[0])])
        weights = jnp.concatenate([a_high, a_high, a_low, a_low], axis=0)
        group = 8
        for start in range(0, edge, group):
            x_high, x_low = split_two(x_buf[slot, :, start * edge:(start + group) * edge])
            turned = jnp.concatenate([x_high, x_low], axis=0).T
            e = jnp.dot(
                jnp.concatenate([turned, turned], axis=1), weights, preferred_element_type=f32
            )
            e_ref[slot, start * edge:(start + group) * edge, :] = e
            part[slot, start:start + group, :] = jnp.sum(
                e.reshape(group, edge, rank) * nu_block[None], axis=1
            )
        return carry

    def gather_blocks(dimension, out_ref):
        blocks = out_ref.shape[0] // edge
        places = [lax.rem(list_ref[dimension, slot], blocks) for slot in range(slots)]
        lives = [list_ref[3, slot].astype(f32) for slot in range(slots)]

        def block_step(block, carry):
            total = jnp.zeros((edge, rank), f32)
            for slot in range(slots):
                weight = (places[slot] == block).astype(f32) * lives[slot]
                total += part[slot] * weight
            out_ref[pl.ds(aligned(block * edge, edge), edge), :] = total
            return carry

        lax.fori_loop(0, blocks, block_step, 0)

    lax.fori_loop(0, half, second_step, 0)
    arrive(gram_copies)
    gram_a[rows_of(gram_a), :] = total_of(gram_land)
    gram_copies = net.spread("aux", gram_a, rank // count)
    lax.fori_loop(half, slots, second_step, 0)
    gather_blocks(1, room["terms"])
    terms_copies = net.scatter("aux", room["terms"], room["terms_land"])

    arrive(gram_copies)
    unit_a, scale_a = unit_gram(gram_a[...], P_SIZE)
    work[...] = unit_a * room["s_nu"][...] + ridge
    sweep_inverse(work)
    inverse = split_three(-work[...])
    arrive(terms_copies)
    b_full, b_blocks = room["b"], room["b_blocks"]
    b_full[rows_of(b_full), :] = dot_exact(
        split_three(total_of(room["terms_land"]) / scale_a), inverse
    )
    even[...] = jnp.zeros_like(even)
    odd[...] = jnp.zeros_like(odd)

    def b_landed(owner):
        gram_add(b_full[rows_of(b_full, owner), :], even, odd)

    net.spread_pairs("aux", b_full, orb_rows // count, b_landed)
    gram_b = room["gram_b"]
    cross = odd[...]
    gram_b[...] = even[...] + (cross + cross.T)
    z_copies = net.share("orb", gram_b.at[rows_of(gram_b), :], room["z_land"])
    save_b = pltpu.make_async_copy(b_full, b_out, sems["save"].at[1])
    save_b.start()
    b_blocks[...] = b_full[...].reshape(b_blocks.shape)

    def third_step(slot, carry):
        b_block = b_blocks[lax.rem(list_ref[1, slot], b_blocks.shape[0])]
        total = jnp.zeros((edge, rank), f32)
        for j in range(edge):
            total += e_ref[slot, j * edge:(j + 1) * edge, :] * b_block[j:j + 1, :]
        part[slot] = total
        return carry

    gram_sum = room["gram_sum"]
    thirds, thirds_land, third_sums = room["thirds"], room["thirds_land"], room["third_sums"]
    lax.fori_loop(0, half, third_step, 0)
    arrive(z_copies)
    gram_sum[rows_of(gram_sum), :] = total_of(room["z_land"])
    gram_copies = net.spread("aux", gram_sum, rank // count)
    lax.fori_loop(half, slots, third_step, 0)
    gather_blocks(2, thirds)
    third_copies = net.scatter("aux", thirds, thirds_land)

    arrive(gram_copies)
    unit_b, scale_b = unit_gram(gram_sum[...], orb_rows * size)
    work[...] = unit_b * unit_gram(gram_a[...], P_SIZE)[0] + ridge
    sweep_inverse(work, None, 0, panels // 2)
    arrive(third_copies)
    thirds_land[mine] = total_of(thirds_land)
    third_copies = net.share("orb", thirds_land.at[mine], room["thirds_z"])
    sweep_inverse(work, None, panels // 2, panels)
    inverse = split_three(-work[...])
    arrive(third_copies)
    third_sums[rows_of(third_sums), :] = total_of(room["thirds_z"])
    net.spread_pairs("aux", third_sums, nu_rows // count)
    c_new = dot_exact(split_three(third_sums[...] / scale_a / scale_b), inverse)
    scale_c = jnp.sqrt(jnp.sum(c_new * c_new, axis=0, keepdims=True) / nu_rows + epsilon)
    c_out[...] = c_new
    scale_out[0:1, :] = scale_a
    scale_out[1:2, :] = scale_b
    scale_out[2:3, :] = scale_c

    def last(slot, carry):
        for way in (1, -1):
            for distance in range(size - 1):

                @pl.when(goes(way, distance))
                def _():
                    hop(way, distance, slot).wait_send()

        return carry

    lax.fori_loop(0, slots, last, 0)
    save_a.wait()
    save_b.wait()
    net.finish()


def scale_kernel(a_hbm, b_hbm, c_hbm, scale_ref, a_out, b_out, c_out, a, b, c, load_sem, save_sem):
    pieces = []
    for at, (source, target, buffer) in enumerate(
        ((a_hbm, a_out, a), (b_hbm, b_out, b), (c_hbm, c_out, c))
    ):
        step = min(512, buffer.shape[0])
        for start in range(0, buffer.shape[0], step):
            number = len(pieces)
            rows = pl.ds(start, step)
            pieces.append(
                (
                    at,
                    buffer,
                    rows,
                    pltpu.make_async_copy(
                        source.at[rows, :], buffer.at[rows, :], load_sem.at[number]
                    ),
                    pltpu.make_async_copy(
                        buffer.at[rows, :], target.at[rows, :], save_sem.at[number]
                    ),
                )
            )
    for piece in pieces:
        piece[3].start()
    for at, buffer, rows, load, save in pieces:
        load.wait()
        buffer[rows, :] = buffer[rows, :] / scale_ref[at:at + 1, :]
        save.start()
    for piece in pieces:
        piece[4].wait()


def per_device(tiles, tile_list, orb_factor, nu_factor):
    slots, edge, tile_width = tiles.shape
    rank = nu_factor.shape[1]
    aux_size, orb_size = lax.axis_size("aux"), lax.axis_size("orb")
    first_rows = P_SIZE // aux_size
    orb_rows, nu_rows = orb_factor.shape[0], nu_factor.shape[0]
    square = (rank, rank)
    shapes = {
        "x": (slots, edge, tile_width),
        "parts": (orb_size * slots * edge, rank),
        "table": (orb_size * 2, 8, rank),
        "a": (first_rows // edge, edge, rank),
        "e": (slots, tile_width, rank),
        "part": (slots, edge, rank),
        "q": (slots // 2 * edge, rank),
        "orb_land": (orb_size, rank // aux_size, rank),
        "gram_land": (aux_size, rank // aux_size, rank),
        "terms": (orb_rows, rank),
        "terms_land": (aux_size, orb_rows // aux_size, rank),
        "b": (orb_rows, rank),
        "b_blocks": (orb_rows // edge, edge, rank),
        "z_land": (orb_size, rank // aux_size, rank),
        "thirds": (nu_rows, rank),
        "thirds_land": (aux_size, nu_rows // aux_size, rank),
        "thirds_z": (orb_size, nu_rows // aux_size, rank),
        "third_sums": (nu_rows, rank),
    }
    for name in ("work", "even", "odd", "orb_gram", "orb_sum", "s_nu", "gram", "gram_a", "gram_b", "gram_sum"):
        shapes[name] = square
    net_count = 8 * (aux_size - 1) + 4 * (orb_size - 1)
    dma = pltpu.SemaphoreType.DMA
    semaphores = {
        "x": dma((slots,)),
        "send": dma((net_count,)),
        "recv": dma((net_count,)),
        "hop_send": dma((2, orb_size - 1, slots)),
        "hop_recv": dma((2, orb_size - 1, slots)),
        "save": dma((2,)),
    }
    room = {name: pltpu.VMEM(shape, f32) for name, shape in shapes.items()}
    room["inverse"] = pltpu.VMEM((3,) + square, bf16)
    vmem = pl.BlockSpec(memory_space=pltpu.VMEM)
    hbm = pl.BlockSpec(memory_space=pltpu.HBM)

    def kernel(list_ref, x_hbm, orb_ref, nu_ref, a_out, b_out, c_out, scale_out, *scratch):
        names = list(room)
        sweep_kernel(
            edge, list_ref, x_hbm, orb_ref, nu_ref, a_out, b_out, c_out, scale_out,
            dict(zip(names, scratch)), dict(zip(semaphores, scratch[len(names):]))
        )

    a_new, b_new, c_new, scales = pl.pallas_call(
        kernel,
        out_shape=(
            jax.ShapeDtypeStruct((first_rows // edge, edge, rank), f32),
            jax.ShapeDtypeStruct((orb_rows, rank), f32),
            jax.ShapeDtypeStruct((nu_rows, rank), f32),
            jax.ShapeDtypeStruct((8, rank), f32),
        ),
        in_specs=[pl.BlockSpec(memory_space=pltpu.SMEM), hbm, vmem, vmem],
        out_specs=(hbm, hbm, vmem, vmem),
        scratch_shapes=list(room.values()) + list(semaphores.values()),
        compiler_params=pltpu.CompilerParams(
            collective_id=5, has_side_effects=True, vmem_limit_bytes=62 << 20
        ),
        name="sweep",
    )(tile_list, tiles, orb_factor.reshape(-1, edge, rank), nu_factor.reshape(-1, edge, rank))
    rows = (first_rows, orb_rows, nu_rows)
    count = sum(-(-size // 512) for size in rows)
    return pl.pallas_call(
        scale_kernel,
        out_shape=tuple(jax.ShapeDtypeStruct((size, rank), f32) for size in rows),
        in_specs=[hbm, hbm, hbm, vmem],
        out_specs=(hbm, hbm, hbm),
        scratch_shapes=[pltpu.VMEM((size, rank), f32) for size in rows]
        + [dma((count,)), dma((count,))],
        compiler_params=pltpu.CompilerParams(vmem_limit_bytes=60 << 20),
        name="scale",
    )(a_new.reshape(first_rows, rank), b_new, c_new, scales)


def solution(mesh):
    return jax.shard_map(
        per_device,
        mesh=mesh,
        in_specs=(P(("aux", "orb"), None, None), P(None, ("aux", "orb")), P("orb", None), P()),
        out_specs=(P("aux", None), P("orb", None), P()),
        check_vma=False,
    )
```

```python
import functools

import jax
import jax.numpy as jnp
from jax import lax
from jax.experimental import pallas as pl
from jax.experimental.pallas import tpu as pltpu
from jax.sharding import PartitionSpec as P

P_SIZE = 16384
MU = 4096
NU = 512

ridge_weight = 0.5
epsilon = 1e-06
highest = lax.Precision.HIGHEST
f32 = jnp.float32
bf16 = jnp.bfloat16
PANEL = 32


MESH = pl.DeviceIdType.MESH


def split_two(x):
    high = x.astype(bf16)
    return high, (x - high.astype(f32)).astype(bf16)


def split_three(x):
    high = x.astype(bf16)
    rest = x - high.astype(f32)
    middle = rest.astype(bf16)
    return high, middle, (rest - middle.astype(f32)).astype(bf16)


def aligned(value, step):
    return pl.multiple_of(value, step)


def dot_t(left, right):
    return lax.dot_general(left, right, (((0,), (0,)), ((), ())), preferred_element_type=f32)


def dot_exact(left, right):
    l_high, l_middle, l_low = left
    r_high, r_middle, r_low = right
    dot = functools.partial(jnp.dot, preferred_element_type=f32)
    small = dot(l_low, r_high) + dot(l_high, r_low) + dot(l_middle, r_middle)
    return dot(l_high, r_high) + (dot(l_middle, r_high) + dot(l_high, r_middle) + small)


def gram_add(x, even_ref, odd_ref):
    high, middle, low = split_three(x)
    even_ref[...] += dot_t(high, high) + dot_t(middle, middle)
    odd_ref[...] += dot_t(high, middle) + dot_t(high, low)


def gram_rows(x_ref, even_ref, odd_ref):
    even_ref[...] = jnp.zeros_like(even_ref)
    odd_ref[...] = jnp.zeros_like(odd_ref)
    group = min(4, x_ref.shape[0])

    def step(at, carry):
        rows = x_ref[pl.ds(at * group, group)]
        gram_add(rows.reshape(-1, rows.shape[2]), even_ref, odd_ref)
        return carry

    lax.fori_loop(0, x_ref.shape[0] // group, step, 0)
    odd = odd_ref[...]
    return even_ref[...] + (odd + odd.T)


def enter(axes):
    barrier = pltpu.get_barrier_semaphore()
    count = 0
    for axis in axes:
        size, here = lax.axis_size(axis), lax.axis_index(axis)
        for step in range(1, size):
            pl.semaphore_signal(
                barrier, inc=1, device_id={axis: (here + step) % size}, device_id_type=MESH
            )
            count += 1
    pl.semaphore_wait(barrier, count)


class Net:
    def __init__(self, send, recv):
        self.send, self.recv, self.copies = send, recv, []

    def plan(self, src, dst, to):
        at = len(self.copies)
        copy = pltpu.make_async_remote_copy(
            src_ref=src,
            dst_ref=dst,
            send_sem=self.send.at[at],
            recv_sem=self.recv.at[at],
            device_id=to,
            device_id_type=MESH,
        )
        self.copies.append(copy)
        return copy

    def copy(self, src, dst, to):
        copy = self.plan(src, dst, to)
        copy.start()
        return copy

    def scatter(self, axis, src, land):
        size, here = lax.axis_size(axis), lax.axis_index(axis)
        rows = land.shape[1]
        land[here] = src[pl.ds(aligned(here * rows, 8), rows), :]
        copies = []
        for step in range(1, size):
            to = (here + step) % size
            block = src.at[pl.ds(aligned(to * rows, 8), rows), :]
            copies.append(self.copy(block, land.at[here], {axis: to}))
        return copies

    def share(self, axis, src, land):
        size, here = lax.axis_size(axis), lax.axis_index(axis)
        land[here] = src[...]
        return [
            self.copy(src, land.at[here], {axis: (here + step) % size}) for step in range(1, size)
        ]

    def spread(self, axis, full, rows):
        size, here = lax.axis_size(axis), lax.axis_index(axis)
        own = full.at[pl.ds(aligned(here * rows, 8), rows), :]
        return [self.copy(own, own, {axis: (here + step) % size}) for step in range(1, size)]

    def finish(self):
        for copy in self.copies:
            copy.wait_send()


class PairSpread:
    def __init__(self, net, axis, block):
        size, here = lax.axis_size(axis), lax.axis_index(axis)
        chips, chip, core = size // 2, here // 2, here % 2
        other = here + 1 - 2 * core
        self.own = here
        self.near_from = [chip * 2 + 1 - core]
        self.far_from, self.far, self.relays = [], [], []
        own = block(here)
        self.near = [net.plan(own, own, {axis: other})]
        for step in range(1, chips):
            target = (chip + step) % chips * 2 + core
            self.far.append(net.plan(own, own, {axis: target}))
            source = (chip + chips - step) % chips * 2
            self.far_from.append(source + core)
            self.near_from.append(source + 1 - core)
            passed = block(source + core)
            self.near.append(net.plan(passed, passed, {axis: other}))

    def start(self):
        for copy in self.far:
            copy.start()
        self.near[0].start()

    def relay(self, landed=None):
        for copy, near, owner in zip(self.far, self.near[1:], self.far_from):
            copy.wait_recv()
            near.start()
            if landed is not None:
                landed(owner)

    def collect(self, landed=None):
        for copy, owner in zip(self.near, self.near_from):
            copy.wait_recv()
            if landed is not None:
                landed(owner)


class PairScatter:
    def __init__(self, net, axis, block, pair, stage, land):
        size, here = lax.axis_size(axis), lax.axis_index(axis)
        chips, chip, core = size // 2, here // 2, here % 2
        other = here + 1 - 2 * core
        self.chip, self.land, self.pair, self.stage = chip, land, pair, stage
        self.first, self.second, self.targets = [], [], []
        for step in range(1, chips + 1):
            target = (chip + step) % chips
            self.targets.append((target, block(target * 2 + core)))
            away = block(target * 2 + 1 - core)
            self.first.append(net.plan(away, pair.at[target], {axis: other}))
            if step < chips:
                self.second.append(
                    net.plan(stage.at[target], land.at[chip], {axis: target * 2 + core})
                )

    def start(self):
        for copy in self.first:
            copy.start()

    def relay(self):
        for copy, send, (target, own) in zip(self.first, self.second, self.targets):
            copy.wait_recv()
            self.stage[target] = own[...] + self.pair[target]
            send.start()
        self.first[-1].wait_recv()
        target, own = self.targets[-1]
        self.land[self.chip] = own[...] + self.pair[target]

    def total(self):
        arrive(self.second)
        return total_of(self.land)


def arrive(copies):
    for copy in copies:
        copy.wait_recv()


def total_of(land):
    total = land[0]
    for at in range(1, land.shape[0]):
        total += land[at]
    return total


def eye_mask(n):
    return lax.broadcasted_iota(jnp.int32, (n, n), 0) == lax.broadcasted_iota(jnp.int32, (n, n), 1)


def unit_gram(gram, rows):
    diagonal = jnp.where(eye_mask(gram.shape[0]), gram, 0.0)
    along = jnp.sqrt(jnp.sum(diagonal, axis=0, keepdims=True) / rows + epsilon)
    down = jnp.sqrt(jnp.sum(diagonal, axis=1, keepdims=True) / rows + epsilon)
    return gram / down / along / rows, along


def pivot_panel(tiles, cols, lane, row):
    height = len(tiles[0])
    sub = tiles[0][0].shape[0]

    def columns(first):
        return [
            [jnp.broadcast_to(tile[:, k:k + 1], tile.shape) for tile in tiles[0]]
            for k in range(first, first + cols)
        ]

    def take(pieces, k):
        at = k % sub
        return pieces[k // sub][at:at + 1, :]

    def step(pieces, firsts, seconds, k, new_first, new_second, clear=None):
        out = []
        for g in range(height):
            base = pieces[g] if clear is None else jnp.where(clear, 0.0, pieces[g])
            value = base - firsts[g] * new_first - seconds[g] * new_second
            if g == k // sub:
                value = jnp.where(row == k % sub, new_first, value)
                value = jnp.where(row == k % sub + 1, new_second, value)
            out.append(value)
        return out

    now = columns(0)
    later = None
    for start in range(0, height * sub, cols):
        for j in range(0, cols, 2):
            k = start + j
            if j == cols // 2 and start + cols < height * sub:
                later = columns(start + cols)
            firsts, seconds = now[j], now[j + 1]
            a, b = take(firsts, k), take(seconds, k)
            c, d = take(firsts, k + 1), take(seconds, k + 1)
            scale = 1.0 / (a * d - b * c)
            a, b, c, d = d * scale, b * scale, c * scale, a * scale
            for i in range(j + 2, cols):
                up, down = take(now[i], k), take(now[i], k + 1)
                now[i] = step(now[i], firsts, seconds, k, a * up - b * down, d * down - c * up)
            if later is not None:
                for i in range(cols):
                    up, down = take(later[i], k), take(later[i], k + 1)
                    later[i] = step(
                        later[i], firsts, seconds, k, a * up - b * down, d * down - c * up
                    )
            for h, pieces in enumerate(tiles):
                up, down = take(pieces, k), take(pieces, k + 1)
                clear = None
                if h == 0:
                    at_up, at_down = lane == k, lane == k + 1
                    clear = at_up | at_down
                    up = jnp.where(at_up[:1], 1.0, jnp.where(at_down[:1], 0.0, up))
                    down = jnp.where(at_down[:1], 1.0, jnp.where(at_up[:1], 0.0, down))
                tiles[h] = step(
                    pieces, firsts, seconds, k, a * up - b * down, d * down - c * up, clear
                )
        now, later = later, None
    return tiles


def sweep_inverse(a_ref, beside=None, first=0, last=None):
    n = a_ref.shape[0]
    sub, wide = 8, 128
    lane = lax.broadcasted_iota(jnp.int32, (PANEL, n), 1)
    tile_lane = lax.broadcasted_iota(jnp.int32, (sub, wide), 1)
    tile_row = lax.broadcasted_iota(jnp.int32, (sub, wide), 0)

    def panel_step(step, carry):
        if beside is not None:
            beside(step)
        before = a_ref[:PANEL, :]
        tiles = [
            [before[g:g + sub, h:h + wide] for g in range(0, PANEL, sub)]
            for h in range(0, n, wide)
        ]
        tiles = pivot_panel(tiles, 8, tile_lane, tile_row)
        panel = jnp.concatenate([jnp.concatenate(pieces, axis=0) for pieces in tiles], axis=1)
        own = lane < PANEL
        update = jnp.where(own, -panel, panel)
        w_high, w_middle, w_low = split_three(before)
        z_high, z_middle, z_low = split_three(update)
        left = jnp.concatenate([w_low, w_middle, w_high, w_middle, w_high, w_high], axis=0)
        right = jnp.concatenate([z_high, z_middle, z_low, z_high, z_middle, z_high], axis=0)
        change = lax.dot_general(
            left, right, (((0,), (0,)), ((), ())), preferred_element_type=f32
        )
        others = jnp.where(own[:1], 0.0, a_ref[PANEL:, :]) - change[PANEL:, :]
        a_ref[:n - PANEL, :] = pltpu.roll(others, n - PANEL, 1)
        a_ref[n - PANEL:, :] = pltpu.roll(update, n - PANEL, 1)
        return carry

    lax.fori_loop(first, n // PANEL if last is None else last, panel_step, 0)


def sweep_kernel(
    edge, list_ref, x_hbm, orb_ref, nu_ref, a_out, b_out, c_out, scale_out, room, sems
):
    slots = list_ref.shape[1]
    here, size = lax.axis_index("orb"), lax.axis_size("orb")
    mine, count = lax.axis_index("aux"), lax.axis_size("aux")
    rank = nu_ref.shape[2]
    x_buf, parts, table, a_ref, e_ref, part = (
        room[name] for name in ("x", "parts", "table", "a", "e", "part")
    )
    work, even, odd = room["work"], room["even"], room["odd"]
    orb_rows, nu_rows = orb_ref.shape[0] * edge, nu_ref.shape[0] * edge
    first_base = mine * a_ref.shape[0]
    hop_send, hop_recv = sems["hop_send"], sems["hop_recv"]

    def load(slot):
        return pltpu.make_async_copy(x_hbm.at[slot], x_buf.at[slot], sems["x"].at[slot])

    def rows_of(ref, owner=mine):
        rows = ref.shape[0] // count
        return pl.ds(aligned(owner * rows, 8), rows)

    for slot in range(slots):
        load(slot).start()
    enter(("aux", "orb"))
    net = Net(sems["send"], sems["recv"])

    def part_rows(source, slot):
        return parts.at[pl.ds(aligned((source * slots + slot) * edge, edge), edge), :]

    def hop(way, distance, slot):
        rows = part_rows(here - way * distance, slot)
        lane = (1 - way) // 2
        return pltpu.make_async_remote_copy(
            src_ref=rows,
            dst_ref=rows,
            send_sem=hop_send.at[lane, distance, slot],
            recv_sem=hop_recv.at[lane, distance, slot],
            device_id={"orb": here + way},
            device_id_type=MESH,
        )

    def landed(way, distance, slot):
        rows = part_rows(here - way * distance, slot)
        lane = (1 - way) // 2
        return pltpu.make_async_remote_copy(
            src_ref=rows,
            dst_ref=rows,
            send_sem=hop_send.at[lane, distance - 1, slot],
            recv_sem=hop_recv.at[lane, distance - 1, slot],
            device_id={"orb": here - way},
            device_id_type=MESH,
        )

    def place(way):
        return (size - 1) * ((1 - way) // 2) + way * here

    def goes(way, distance):
        at = place(way)
        return (at + size - 1 - distance) // (size - 1) * ((2 * size - 3 - at) // (size - 1)) > 0

    def forward(distance, slot):
        for way in (1, -1):

            @pl.when(goes(way, distance))
            def _():
                landed(way, distance, slot).wait_recv()
                hop(way, distance, slot).start()

    def slot_step(slot, carry):
        load(slot).wait()
        nu_block = nu_ref[list_ref[2, slot]]
        orb_block = orb_ref[lax.rem(list_ref[1, slot], orb_ref.shape[0])]
        group = 4
        total = jnp.zeros((edge, rank), f32)
        for start in range(0, edge, group):
            x_high, x_low = split_two(x_buf[slot, :, start * edge:(start + group) * edge])
            stacked = jnp.concatenate([x_high, x_low], axis=0)
            product = jnp.concatenate(
                [nu_block * orb_block[j:j + 1, :] for j in range(start, start + group)], axis=0
            )
            high, low = split_two(product)
            main = jnp.dot(stacked, high, preferred_element_type=f32)
            rest = jnp.dot(x_high, low, preferred_element_type=f32)
            total += main[:edge] + (main[edge:] + rest)
        live = list_ref[3, slot].astype(f32)
        part_rows(here, slot)[...] = total * live
        for way in (1, -1):

            @pl.when(goes(way, 0))
            def _():
                hop(way, 0, slot).start()

        return carry

    early, late = slots // 4, slots - slots // 4
    lax.fori_loop(0, early, slot_step, 0)

    half = slots // 2
    row = lax.broadcasted_iota(jnp.int32, table.shape[1:], 0)
    for piece in range(2):
        own_at = jnp.zeros(table.shape[1:], f32)
        for slot in range(half):
            value = (list_ref[0, piece * half + slot] - first_base).astype(f32)
            own_at = jnp.where(row == slot, value, own_at)
        table[2 * here + piece] = own_at
    own_table = table.at[pl.ds(2 * here, 2)]
    table_copies = [
        net.copy(own_table, own_table, {"orb": (here + step) % size}) for step in range(1, size)
    ]
    orb_gram, orb_land, orb_sum = room["orb_gram"], room["orb_land"], room["orb_sum"]
    orb_gram[...] = gram_rows(orb_ref, even, odd)
    gram_copies = net.share("orb", orb_gram.at[rows_of(orb_gram), :], orb_land)
    room["s_nu"][...] = gram_rows(nu_ref, even, odd) / NU
    lax.fori_loop(early, late, slot_step, 0)
    arrive(gram_copies)
    orb_sum[rows_of(orb_sum), :] = total_of(orb_land)
    gram_copies = net.spread("aux", orb_sum, rank // count)
    lax.fori_loop(late, slots, slot_step, 0)

    if size > 2:

        def pass_near(slot, carry):
            forward(1, slot)
            return carry

        lax.fori_loop(0, slots, pass_near, 0)
    arrive(gram_copies)
    ridge = jnp.where(eye_mask(rank), ridge_weight, 0.0)
    work[...] = orb_sum[...] / (orb_rows * size) * room["s_nu"][...] + ridge
    panels = rank // PANEL
    together = panels == slots

    def beside(step):
        if size > 3:
            forward(2, step)

    sweep_inverse(work, beside if together else None)
    for at, piece in enumerate(split_three(-work[...])):
        room["inverse"][at] = piece
    for distance in range(3 if together else 2, size - 1):

        def pass_on(slot, carry, distance=distance):
            forward(distance, slot)
            return carry

        lax.fori_loop(0, slots, pass_on, 0)
    arrive(table_copies)

    def add_rows(source, piece, clear):
        start = piece * half
        rows = parts[pl.ds(aligned((source * slots + start) * edge, edge), half * edge), :]
        inverse = tuple(room["inverse"][at] for at in range(3))
        room["q"][...] = dot_exact(split_three(rows), inverse)
        places = table[2 * source + piece]

        def block_step(block, carry):
            name = jnp.full((1, rank), block, jnp.int32).astype(f32)
            total = jnp.zeros((edge, rank), f32) if clear else a_ref[block]
            for slot in range(half):
                weight = jnp.where(places[slot:slot + 1, :] == name, 1.0, 0.0)
                total += room["q"][slot * edge:(slot + 1) * edge, :] * weight
            a_ref[block] = total
            return carry

        lax.fori_loop(0, a_ref.shape[0], block_step, 0)

    add_rows(here, 0, True)
    add_rows(here, 1, False)

    def source_step(at, carry):
        distance, way = at // 2 + 1, 1 - at % 2 * 2
        source = here - way * distance

        @pl.when((source + size) // size * ((2 * size - 1 - source) // size) > 0)
        def _():
            def half_step(piece, carry):
                @pl.when(place(way) == size - 1)
                def _():
                    for slot in range(half):
                        landed(way, distance, piece * half + slot).wait_recv()

                add_rows(source, piece, False)
                return carry

            lax.fori_loop(0, 2, half_step, 0)

        return carry

    lax.fori_loop(0, 2 * (size - 1), source_step, 0)
    save_a = pltpu.make_async_copy(a_ref, a_out, sems["save"].at[0])
    save_a.start()

    gram_a, gram_land = room["gram_a"], room["gram_land"]
    room["gram"][...] = gram_rows(a_ref, even, odd)
    gram_copies = net.scatter("aux", room["gram"], gram_land)

    def second_step(slot, carry):
        nu_block = nu_ref[list_ref[2, slot]]
        a_high, a_low = split_two(a_ref[lax.rem(list_ref[0, slot], a_ref.shape[0])])
        weights = jnp.concatenate([a_high, a_high, a_low, a_low], axis=0)
        group = 8
        for start in range(0, edge, group):
            x_high, x_low = split_two(x_buf[slot, :, start * edge:(start + group) * edge])
            turned = jnp.concatenate([x_high, x_low], axis=0).T
            e = jnp.dot(
                jnp.concatenate([turned, turned], axis=1), weights, preferred_element_type=f32
            )
            e_ref[slot, start * edge:(start + group) * edge, :] = e
            part[slot, start:start + group, :] = jnp.sum(
                e.reshape(group, edge, rank) * nu_block[None], axis=1
            )
        return carry

    def gather_blocks(dimension, out_ref, columns=slice(None)):
        blocks = out_ref.shape[0] // edge
        places = [lax.rem(list_ref[dimension, slot], blocks) for slot in range(slots)]
        lives = [list_ref[3, slot].astype(f32) for slot in range(slots)]

        def block_step(block, carry):
            total = jnp.zeros((edge, out_ref.shape[1]), f32)
            for slot in range(slots):
                weight = (places[slot] == block).astype(f32) * lives[slot]
                total += part[slot, :, columns] * weight
            out_ref[pl.ds(aligned(block * edge, edge), edge), :] = total
            return carry

        lax.fori_loop(0, blocks, block_step, 0)

    lax.fori_loop(0, half, second_step, 0)
    arrive(gram_copies)
    gram_a[rows_of(gram_a), :] = total_of(gram_land)
    gram_copies = net.spread("aux", gram_a, rank // count)
    lax.fori_loop(half, slots, second_step, 0)
    gather_blocks(1, room["terms"])
    terms = room["terms"]
    terms_sum = PairScatter(
        net, "aux", lambda owner: terms.at[rows_of(terms, owner), :],
        room["terms_pair"], room["terms_stage"], room["terms_land"]
    )
    terms_sum.start()

    arrive(gram_copies)
    unit_a, scale_a = unit_gram(gram_a[...], P_SIZE)
    work[...] = unit_a * room["s_nu"][...] + ridge

    def beside_second(step):
        @pl.when(step == 1)
        def _():
            terms_sum.relay()

    sweep_inverse(work, beside_second)
    inverse = split_three(-work[...])
    b_full, b_blocks = room["b"], room["b_blocks"]
    b_full[rows_of(b_full), :] = dot_exact(
        split_three(terms_sum.total() / scale_a), inverse
    )
    even[...] = jnp.zeros_like(even)
    odd[...] = jnp.zeros_like(odd)

    def b_landed(owner):
        gram_add(b_full[rows_of(b_full, owner), :], even, odd)

    b_spread = PairSpread(net, "aux", lambda owner: b_full.at[rows_of(b_full, owner), :])
    b_spread.start()
    b_landed(mine)
    b_spread.relay(b_landed)
    b_spread.collect(b_landed)
    gram_b = room["gram_b"]
    cross = odd[...]
    gram_b[...] = even[...] + (cross + cross.T)
    z_copies = net.share("orb", gram_b.at[rows_of(gram_b), :], room["z_land"])
    save_b = pltpu.make_async_copy(b_full, b_out, sems["save"].at[1])
    save_b.start()
    b_blocks[...] = b_full[...].reshape(b_blocks.shape)

    gram_sum = room["gram_sum"]
    thirds, thirds_land, thirds_z, third_sums = (
        room[name] for name in ("thirds", "thirds_land", "thirds_z", "third_sums")
    )
    wide = rank // 2

    def third_half(side):
        columns = slice(side * wide, (side + 1) * wide)

        def third_step(slot, carry):
            b_block = b_blocks[lax.rem(list_ref[1, slot], b_blocks.shape[0])][:, columns]
            total = jnp.zeros((edge, wide), f32)
            for j in range(edge):
                total += e_ref[slot, j * edge:(j + 1) * edge, columns] * b_block[j:j + 1, :]
            part[slot, :, columns] = total
            return carry

        lax.fori_loop(0, slots, third_step, 0)
        gather_blocks(2, thirds.at[side], columns)

    def third_spread(side):
        full = third_sums.at[side]
        rows = nu_rows // count
        return PairSpread(
            net, "aux", lambda owner: full.at[pl.ds(aligned(owner * rows, 8), rows), :]
        )

    third_half(0)
    third_copies = [net.scatter("aux", thirds.at[0], thirds_land.at[0])]
    third_half(1)
    arrive(z_copies)
    gram_sum[rows_of(gram_sum), :] = total_of(room["z_land"])
    gram_spread = PairSpread(net, "aux", lambda owner: gram_sum.at[rows_of(gram_sum, owner), :])
    gram_spread.start()
    third_copies.append(net.scatter("aux", thirds.at[1], thirds_land.at[1]))
    shares, spreads = [], []
    for side in range(2):
        own = thirds_land.at[side, mine]
        shares.append(
            [
                net.plan(own, thirds_z.at[side, here], {"orb": (here + step) % size})
                for step in range(1, size)
            ]
        )
        spreads.append(third_spread(side))

    def third_landed(side):
        arrive(third_copies[side])
        total = total_of(thirds_land.at[side])
        thirds_land[side, mine] = total
        thirds_z[side, here] = total
        for copy in shares[side]:
            copy.start()

    def third_summed(side):
        arrive(shares[side])
        third_sums[side, pl.ds(aligned(mine * (nu_rows // count), 8), nu_rows // count), :] = (
            total_of(thirds_z.at[side])
        )
        spreads[side].start()

    gram_spread.relay()
    gram_spread.collect()
    unit_b, scale_b = unit_gram(gram_sum[...], orb_rows * size)
    work[...] = unit_b * unit_gram(gram_a[...], P_SIZE)[0] + ridge

    def beside_third(step):
        for when, act, side in (
            (1, third_landed, 0), (3, third_landed, 1), (panels - 1, third_summed, 0)
        ):

            @pl.when(step == when)
            def _():
                act(side)

    sweep_inverse(work, beside_third)
    inverse = split_three(-work[...])
    spreads[0].relay()
    third_summed(1)
    spreads[0].collect()
    spreads[1].relay()
    spreads[1].collect()
    third_all = jnp.concatenate([third_sums[0], third_sums[1]], axis=1)
    c_new = dot_exact(split_three(third_all / scale_a / scale_b), inverse)
    scale_c = jnp.sqrt(jnp.sum(c_new * c_new, axis=0, keepdims=True) / nu_rows + epsilon)
    c_out[...] = c_new
    scale_out[0:1, :] = scale_a
    scale_out[1:2, :] = scale_b
    scale_out[2:3, :] = scale_c

    def last(slot, carry):
        for way in (1, -1):
            for distance in range(size - 1):

                @pl.when(goes(way, distance))
                def _():
                    hop(way, distance, slot).wait_send()

        return carry

    lax.fori_loop(0, slots, last, 0)
    save_a.wait()
    save_b.wait()
    net.finish()


def scale_kernel(a_hbm, b_hbm, c_hbm, scale_ref, a_out, b_out, c_out, a, b, c, load_sem, save_sem):
    pieces = []
    for at, (source, target, buffer) in enumerate(
        ((a_hbm, a_out, a), (b_hbm, b_out, b), (c_hbm, c_out, c))
    ):
        step = min(512, buffer.shape[0])
        for start in range(0, buffer.shape[0], step):
            number = len(pieces)
            rows = pl.ds(start, step)
            pieces.append(
                (
                    at,
                    buffer,
                    rows,
                    pltpu.make_async_copy(
                        source.at[rows, :], buffer.at[rows, :], load_sem.at[number]
                    ),
                    pltpu.make_async_copy(
                        buffer.at[rows, :], target.at[rows, :], save_sem.at[number]
                    ),
                )
            )
    for piece in pieces:
        piece[3].start()
    for at, buffer, rows, load, save in pieces:
        load.wait()
        buffer[rows, :] = buffer[rows, :] / scale_ref[at:at + 1, :]
        save.start()
    for piece in pieces:
        piece[4].wait()


def per_device(tiles, tile_list, orb_factor, nu_factor):
    slots, edge, tile_width = tiles.shape
    rank = nu_factor.shape[1]
    aux_size, orb_size = lax.axis_size("aux"), lax.axis_size("orb")
    first_rows = P_SIZE // aux_size
    orb_rows, nu_rows = orb_factor.shape[0], nu_factor.shape[0]
    square = (rank, rank)
    shapes = {
        "x": (slots, edge, tile_width),
        "parts": (orb_size * slots * edge, rank),
        "table": (orb_size * 2, 8, rank),
        "a": (first_rows // edge, edge, rank),
        "e": (slots, tile_width, rank),
        "part": (slots, edge, rank),
        "q": (slots // 2 * edge, rank),
        "orb_land": (orb_size, rank // aux_size, rank),
        "gram_land": (aux_size, rank // aux_size, rank),
        "terms": (orb_rows, rank),
        "terms_pair": (aux_size // 2, orb_rows // aux_size, rank),
        "terms_stage": (aux_size // 2, orb_rows // aux_size, rank),
        "terms_land": (aux_size // 2, orb_rows // aux_size, rank),
        "b": (orb_rows, rank),
        "b_blocks": (orb_rows // edge, edge, rank),
        "z_land": (orb_size, rank // aux_size, rank),
        "thirds": (2, nu_rows, rank // 2),
        "thirds_land": (2, aux_size, nu_rows // aux_size, rank // 2),
        "thirds_z": (2, orb_size, nu_rows // aux_size, rank // 2),
        "third_sums": (2, nu_rows, rank // 2),
    }
    for name in ("work", "even", "odd", "orb_gram", "orb_sum", "s_nu", "gram", "gram_a", "gram_b", "gram_sum"):
        shapes[name] = square
    net_count = 10 * (aux_size - 1) + 5 * (orb_size - 1)
    dma = pltpu.SemaphoreType.DMA
    semaphores = {
        "x": dma((slots,)),
        "send": dma((net_count,)),
        "recv": dma((net_count,)),
        "hop_send": dma((2, orb_size - 1, slots)),
        "hop_recv": dma((2, orb_size - 1, slots)),
        "save": dma((2,)),
    }
    room = {name: pltpu.VMEM(shape, f32) for name, shape in shapes.items()}
    room["inverse"] = pltpu.VMEM((3,) + square, bf16)
    vmem = pl.BlockSpec(memory_space=pltpu.VMEM)
    hbm = pl.BlockSpec(memory_space=pltpu.HBM)

    def kernel(list_ref, x_hbm, orb_ref, nu_ref, a_out, b_out, c_out, scale_out, *scratch):
        names = list(room)
        sweep_kernel(
            edge, list_ref, x_hbm, orb_ref, nu_ref, a_out, b_out, c_out, scale_out,
            dict(zip(names, scratch)), dict(zip(semaphores, scratch[len(names):]))
        )

    a_new, b_new, c_new, scales = pl.pallas_call(
        kernel,
        out_shape=(
            jax.ShapeDtypeStruct((first_rows // edge, edge, rank), f32),
            jax.ShapeDtypeStruct((orb_rows, rank), f32),
            jax.ShapeDtypeStruct((nu_rows, rank), f32),
            jax.ShapeDtypeStruct((8, rank), f32),
        ),
        in_specs=[pl.BlockSpec(memory_space=pltpu.SMEM), hbm, vmem, vmem],
        out_specs=(hbm, hbm, vmem, vmem),
        scratch_shapes=list(room.values()) + list(semaphores.values()),
        compiler_params=pltpu.CompilerParams(
            collective_id=5, has_side_effects=True, vmem_limit_bytes=62 << 20
        ),
        name="sweep",
    )(tile_list, tiles, orb_factor.reshape(-1, edge, rank), nu_factor.reshape(-1, edge, rank))
    rows = (first_rows, orb_rows, nu_rows)
    count = sum(-(-size // 512) for size in rows)
    return pl.pallas_call(
        scale_kernel,
        out_shape=tuple(jax.ShapeDtypeStruct((size, rank), f32) for size in rows),
        in_specs=[hbm, hbm, hbm, vmem],
        out_specs=(hbm, hbm, hbm),
        scratch_shapes=[pltpu.VMEM((size, rank), f32) for size in rows]
        + [dma((count,)), dma((count,))],
        compiler_params=pltpu.CompilerParams(vmem_limit_bytes=60 << 20),
        name="scale",
    )(a_new.reshape(first_rows, rank), b_new, c_new, scales)


def solution(mesh):
    return jax.shard_map(
        per_device,
        mesh=mesh,
        in_specs=(P(("aux", "orb"), None, None), P(None, ("aux", "orb")), P("orb", None), P()),
        out_specs=(P("aux", None), P("orb", None), P()),
        check_vma=False,
    )
```

```python
import functools

import jax
import jax.numpy as jnp
from jax import lax
from jax.experimental import pallas as pl
from jax.experimental.pallas import tpu as pltpu
from jax.sharding import PartitionSpec as P

P_SIZE = 16384
MU = 4096
NU = 512

ridge_weight = 0.5
epsilon = 1e-06
highest = lax.Precision.HIGHEST
f32 = jnp.float32
bf16 = jnp.bfloat16
PANEL = 32


MESH = pl.DeviceIdType.MESH


def split_two(x):
    high = x.astype(bf16)
    return high, (x - high.astype(f32)).astype(bf16)


def split_three(x):
    high = x.astype(bf16)
    rest = x - high.astype(f32)
    middle = rest.astype(bf16)
    return high, middle, (rest - middle.astype(f32)).astype(bf16)


def aligned(value, step):
    return pl.multiple_of(value, step)


def dot_t(left, right):
    return lax.dot_general(left, right, (((0,), (0,)), ((), ())), preferred_element_type=f32)


def dot_exact(left, right):
    l_high, l_middle, l_low = left
    r_high, r_middle, r_low = right
    dot = functools.partial(jnp.dot, preferred_element_type=f32)
    small = dot(l_low, r_high) + dot(l_high, r_low) + dot(l_middle, r_middle)
    return dot(l_high, r_high) + (dot(l_middle, r_high) + dot(l_high, r_middle) + small)


def gram_add(x, even_ref, odd_ref):
    high, middle, low = split_three(x)
    even_ref[...] += dot_t(high, high) + dot_t(middle, middle)
    odd_ref[...] += dot_t(high, middle) + dot_t(high, low)


def gram_rows(x_ref, even_ref, odd_ref):
    even_ref[...] = jnp.zeros_like(even_ref)
    odd_ref[...] = jnp.zeros_like(odd_ref)
    group = min(8, x_ref.shape[0])

    def step(at, carry):
        rows = x_ref[pl.ds(at * group, group)]
        gram_add(rows.reshape(-1, rows.shape[2]), even_ref, odd_ref)
        return carry

    lax.fori_loop(0, x_ref.shape[0] // group, step, 0)
    odd = odd_ref[...]
    return even_ref[...] + (odd + odd.T)


def enter(axes):
    barrier = pltpu.get_barrier_semaphore()
    count = 0
    for axis in axes:
        size, here = lax.axis_size(axis), lax.axis_index(axis)
        for step in range(1, size):
            pl.semaphore_signal(
                barrier, inc=1, device_id={axis: (here + step) % size}, device_id_type=MESH
            )
            count += 1
    pl.semaphore_wait(barrier, count)


class Net:
    def __init__(self, send, recv):
        self.send, self.recv, self.copies = send, recv, []

    def plan(self, src, dst, to):
        at = len(self.copies)
        copy = pltpu.make_async_remote_copy(
            src_ref=src,
            dst_ref=dst,
            send_sem=self.send.at[at],
            recv_sem=self.recv.at[at],
            device_id=to,
            device_id_type=MESH,
        )
        self.copies.append(copy)
        return copy

    def copy(self, src, dst, to):
        copy = self.plan(src, dst, to)
        copy.start()
        return copy

    def scatter(self, axis, src, land):
        size, here = lax.axis_size(axis), lax.axis_index(axis)
        rows = land.shape[1]
        land[here] = src[pl.ds(aligned(here * rows, 8), rows), :]
        copies = []
        for step in range(1, size):
            to = (here + step) % size
            block = src.at[pl.ds(aligned(to * rows, 8), rows), :]
            copies.append(self.copy(block, land.at[here], {axis: to}))
        return copies

    def share(self, axis, src, land):
        size, here = lax.axis_size(axis), lax.axis_index(axis)
        land[here] = src[...]
        return [
            self.copy(src, land.at[here], {axis: (here + step) % size}) for step in range(1, size)
        ]

    def spread(self, axis, full, rows):
        size, here = lax.axis_size(axis), lax.axis_index(axis)
        own = full.at[pl.ds(aligned(here * rows, 8), rows), :]
        return [self.copy(own, own, {axis: (here + step) % size}) for step in range(1, size)]

    def finish(self):
        for copy in self.copies:
            copy.wait_send()


class PairSpread:
    def __init__(self, net, axis, block):
        size, here = lax.axis_size(axis), lax.axis_index(axis)
        chips, chip, core = size // 2, here // 2, here % 2
        other = here + 1 - 2 * core
        self.own = here
        self.near_from = [chip * 2 + 1 - core]
        self.far_from, self.far, self.relays = [], [], []
        own = block(here)
        self.near = [net.plan(own, own, {axis: other})]
        for step in range(1, chips):
            target = (chip + step) % chips * 2 + core
            self.far.append(net.plan(own, own, {axis: target}))
            source = (chip + chips - step) % chips * 2
            self.far_from.append(source + core)
            self.near_from.append(source + 1 - core)
            passed = block(source + core)
            self.near.append(net.plan(passed, passed, {axis: other}))

    def start(self):
        for copy in self.far:
            copy.start()
        self.near[0].start()

    def relay(self, landed=None):
        for copy, near, owner in zip(self.far, self.near[1:], self.far_from):
            copy.wait_recv()
            near.start()
            if landed is not None:
                landed(owner)

    def collect(self, landed=None):
        for copy, owner in zip(self.near, self.near_from):
            copy.wait_recv()
            if landed is not None:
                landed(owner)


class PairScatter:
    def __init__(self, net, axis, block, pair, stage, land):
        size, here = lax.axis_size(axis), lax.axis_index(axis)
        chips, chip, core = size // 2, here // 2, here % 2
        other = here + 1 - 2 * core
        self.chip, self.land, self.pair, self.stage = chip, land, pair, stage
        self.first, self.second, self.targets = [], [], []
        for step in range(1, chips + 1):
            target = (chip + step) % chips
            self.targets.append((target, block(target * 2 + core)))
            away = block(target * 2 + 1 - core)
            self.first.append(net.plan(away, pair.at[target], {axis: other}))
            if step < chips:
                self.second.append(
                    net.plan(stage.at[target], land.at[chip], {axis: target * 2 + core})
                )

    def start(self):
        for copy in self.first:
            copy.start()

    def relay(self):
        for copy, send, (target, own) in zip(self.first, self.second, self.targets):
            copy.wait_recv()
            self.stage[target] = own[...] + self.pair[target]
            send.start()
        self.first[-1].wait_recv()
        target, own = self.targets[-1]
        self.land[self.chip] = own[...] + self.pair[target]

    def total(self):
        arrive(self.second)
        return total_of(self.land)


def arrive(copies):
    for copy in copies:
        copy.wait_recv()


def total_of(land):
    total = land[0]
    for at in range(1, land.shape[0]):
        total += land[at]
    return total


def eye_mask(n):
    return lax.broadcasted_iota(jnp.int32, (n, n), 0) == lax.broadcasted_iota(jnp.int32, (n, n), 1)


def unit_gram(gram, rows):
    diagonal = jnp.where(eye_mask(gram.shape[0]), gram, 0.0)
    along = jnp.sqrt(jnp.sum(diagonal, axis=0, keepdims=True) / rows + epsilon)
    down = jnp.sqrt(jnp.sum(diagonal, axis=1, keepdims=True) / rows + epsilon)
    return gram / down / along / rows, along


def pivot_panel(tiles, cols, lane, row):
    height = len(tiles[0])
    sub = tiles[0][0].shape[0]

    def columns(first):
        return [
            [jnp.broadcast_to(tile[:, k:k + 1], tile.shape) for tile in tiles[0]]
            for k in range(first, first + cols)
        ]

    def take(pieces, k):
        at = k % sub
        return pieces[k // sub][at:at + 1, :]

    def step(pieces, firsts, seconds, k, new_first, new_second, clear=None):
        out = []
        for g in range(height):
            base = pieces[g] if clear is None else jnp.where(clear, 0.0, pieces[g])
            value = base - firsts[g] * new_first - seconds[g] * new_second
            if g == k // sub:
                value = jnp.where(row == k % sub, new_first, value)
                value = jnp.where(row == k % sub + 1, new_second, value)
            out.append(value)
        return out

    now = columns(0)
    later = None
    for start in range(0, height * sub, cols):
        for j in range(0, cols, 2):
            k = start + j
            if j == cols - 2 and start + cols < height * sub:
                later = columns(start + cols)
            firsts, seconds = now[j], now[j + 1]
            a, b = take(firsts, k), take(seconds, k)
            c, d = take(firsts, k + 1), take(seconds, k + 1)
            scale = 1.0 / (a * d - b * c)
            a, b, c, d = d * scale, b * scale, c * scale, a * scale
            for i in range(j + 2, cols):
                up, down = take(now[i], k), take(now[i], k + 1)
                now[i] = step(now[i], firsts, seconds, k, a * up - b * down, d * down - c * up)
            if later is not None:
                for i in range(cols):
                    up, down = take(later[i], k), take(later[i], k + 1)
                    later[i] = step(
                        later[i], firsts, seconds, k, a * up - b * down, d * down - c * up
                    )
            for h, pieces in enumerate(tiles):
                up, down = take(pieces, k), take(pieces, k + 1)
                clear = None
                if h == 0:
                    at_up, at_down = lane == k, lane == k + 1
                    clear = at_up | at_down
                    up = jnp.where(at_up[:1], 1.0, jnp.where(at_down[:1], 0.0, up))
                    down = jnp.where(at_down[:1], 1.0, jnp.where(at_up[:1], 0.0, down))
                tiles[h] = step(
                    pieces, firsts, seconds, k, a * up - b * down, d * down - c * up, clear
                )
        now, later = later, None
    return tiles


def sweep_inverse(a_ref, beside=None, first=0, last=None):
    n = a_ref.shape[0]
    sub, wide = 8, 128
    lane = lax.broadcasted_iota(jnp.int32, (PANEL, n), 1)
    tile_lane = lax.broadcasted_iota(jnp.int32, (sub, wide), 1)
    tile_row = lax.broadcasted_iota(jnp.int32, (sub, wide), 0)

    def panel_step(step, carry):
        if beside is not None:
            beside(step)
        before = a_ref[:PANEL, :]
        tiles = [
            [before[g:g + sub, h:h + wide] for g in range(0, PANEL, sub)]
            for h in range(0, n, wide)
        ]
        tiles = pivot_panel(tiles, 8, tile_lane, tile_row)
        panel = jnp.concatenate([jnp.concatenate(pieces, axis=0) for pieces in tiles], axis=1)
        own = lane < PANEL
        update = jnp.where(own, -panel, panel)
        w_high, w_middle, w_low = split_three(before)
        z_high, z_middle, z_low = split_three(update)
        left = jnp.concatenate([w_low, w_middle, w_high, w_middle, w_high, w_high], axis=0)
        right = jnp.concatenate([z_high, z_middle, z_low, z_high, z_middle, z_high], axis=0)
        change = lax.dot_general(
            left, right, (((0,), (0,)), ((), ())), preferred_element_type=f32
        )
        others = jnp.where(own[:1], 0.0, a_ref[PANEL:, :]) - change[PANEL:, :]
        a_ref[:n - PANEL, :] = pltpu.roll(others, n - PANEL, 1)
        a_ref[n - PANEL:, :] = pltpu.roll(update, n - PANEL, 1)
        return carry

    lax.fori_loop(first, n // PANEL if last is None else last, panel_step, 0)


def sweep_kernel(
    edge, list_ref, x_hbm, orb_ref, nu_ref, a_out, b_out, c_out, scale_out, room, sems
):
    slots = list_ref.shape[1]
    here, size = lax.axis_index("orb"), lax.axis_size("orb")
    mine, count = lax.axis_index("aux"), lax.axis_size("aux")
    rank = nu_ref.shape[2]
    x_buf, parts, table, a_ref, e_ref, part = (
        room[name] for name in ("x", "parts", "table", "a", "e", "part")
    )
    work, even, odd = room["work"], room["even"], room["odd"]
    orb_rows, nu_rows = orb_ref.shape[0] * edge, nu_ref.shape[0] * edge
    first_base = mine * a_ref.shape[0]
    hop_send, hop_recv = sems["hop_send"], sems["hop_recv"]

    def load(slot):
        return pltpu.make_async_copy(x_hbm.at[slot], x_buf.at[slot], sems["x"].at[slot])

    def rows_of(ref, owner=mine):
        rows = ref.shape[0] // count
        return pl.ds(aligned(owner * rows, 8), rows)

    for slot in range(slots):
        load(slot).start()
    enter(("aux", "orb"))
    net = Net(sems["send"], sems["recv"])

    def part_rows(source, slot):
        return parts.at[pl.ds(aligned((source * slots + slot) * edge, edge), edge), :]

    def hop(way, distance, slot):
        rows = part_rows(here - way * distance, slot)
        lane = (1 - way) // 2
        return pltpu.make_async_remote_copy(
            src_ref=rows,
            dst_ref=rows,
            send_sem=hop_send.at[lane, distance, slot],
            recv_sem=hop_recv.at[lane, distance, slot],
            device_id={"orb": here + way},
            device_id_type=MESH,
        )

    def landed(way, distance, slot):
        rows = part_rows(here - way * distance, slot)
        lane = (1 - way) // 2
        return pltpu.make_async_remote_copy(
            src_ref=rows,
            dst_ref=rows,
            send_sem=hop_send.at[lane, distance - 1, slot],
            recv_sem=hop_recv.at[lane, distance - 1, slot],
            device_id={"orb": here - way},
            device_id_type=MESH,
        )

    def place(way):
        return (size - 1) * ((1 - way) // 2) + way * here

    def goes(way, distance):
        at = place(way)
        return (at + size - 1 - distance) // (size - 1) * ((2 * size - 3 - at) // (size - 1)) > 0

    def forward(distance, slot):
        for way in (1, -1):

            @pl.when(goes(way, distance))
            def _():
                landed(way, distance, slot).wait_recv()
                hop(way, distance, slot).start()

    def slot_step(slot, carry):
        load(slot).wait()
        nu_block = nu_ref[list_ref[2, slot]]
        orb_block = orb_ref[lax.rem(list_ref[1, slot], orb_ref.shape[0])]
        group = 4
        total = jnp.zeros((edge, rank), f32)
        for start in range(0, edge, group):
            x_high, x_low = split_two(x_buf[slot, :, start * edge:(start + group) * edge])
            stacked = jnp.concatenate([x_high, x_low], axis=0)
            product = jnp.concatenate(
                [nu_block * orb_block[j:j + 1, :] for j in range(start, start + group)], axis=0
            )
            high, low = split_two(product)
            main = jnp.dot(stacked, high, preferred_element_type=f32)
            rest = jnp.dot(x_high, low, preferred_element_type=f32)
            total += main[:edge] + (main[edge:] + rest)
        live = list_ref[3, slot].astype(f32)
        part_rows(here, slot)[...] = total * live
        for way in (1, -1):

            @pl.when(goes(way, 0))
            def _():
                hop(way, 0, slot).start()

        return carry

    early, late = slots // 4, slots - slots // 4
    lax.fori_loop(0, early, slot_step, 0)

    half = slots // 2
    row = lax.broadcasted_iota(jnp.int32, table.shape[1:], 0)
    for piece in range(2):
        own_at = jnp.zeros(table.shape[1:], f32)
        for slot in range(half):
            value = (list_ref[0, piece * half + slot] - first_base).astype(f32)
            own_at = jnp.where(row == slot, value, own_at)
        table[2 * here + piece] = own_at
    own_table = table.at[pl.ds(2 * here, 2)]
    table_copies = [
        net.copy(own_table, own_table, {"orb": (here + step) % size}) for step in range(1, size)
    ]
    orb_gram, orb_land, orb_sum = room["orb_gram"], room["orb_land"], room["orb_sum"]
    orb_gram[...] = gram_rows(orb_ref, even, odd)
    gram_copies = net.share("orb", orb_gram.at[rows_of(orb_gram), :], orb_land)
    room["s_nu"][...] = gram_rows(nu_ref, even, odd) / NU
    lax.fori_loop(early, late, slot_step, 0)
    arrive(gram_copies)
    orb_sum[rows_of(orb_sum), :] = total_of(orb_land)
    gram_copies = net.spread("aux", orb_sum, rank // count)
    lax.fori_loop(late, slots, slot_step, 0)

    if size > 2:

        def pass_near(slot, carry):
            forward(1, slot)
            return carry

        lax.fori_loop(0, slots, pass_near, 0)
    arrive(gram_copies)
    ridge = jnp.where(eye_mask(rank), ridge_weight, 0.0)
    work[...] = orb_sum[...] / (orb_rows * size) * room["s_nu"][...] + ridge
    panels = rank // PANEL
    together = panels == slots

    def beside(step):
        if size > 3:
            forward(2, step)

    sweep_inverse(work, beside if together else None)
    for at, piece in enumerate(split_three(-work[...])):
        room["inverse"][at] = piece
    for distance in range(3 if together else 2, size - 1):

        def pass_on(slot, carry, distance=distance):
            forward(distance, slot)
            return carry

        lax.fori_loop(0, slots, pass_on, 0)
    arrive(table_copies)

    def add_rows(source, piece, clear):
        start = piece * half
        rows = parts[pl.ds(aligned((source * slots + start) * edge, edge), half * edge), :]
        inverse = tuple(room["inverse"][at] for at in range(3))
        room["q"][...] = dot_exact(split_three(rows), inverse)
        places = table[2 * source + piece]

        def block_step(block, carry):
            name = jnp.full((1, rank), block, jnp.int32).astype(f32)
            total = jnp.zeros((edge, rank), f32) if clear else a_ref[block]
            for slot in range(half):
                weight = jnp.where(places[slot:slot + 1, :] == name, 1.0, 0.0)
                total += room["q"][slot * edge:(slot + 1) * edge, :] * weight
            a_ref[block] = total
            return carry

        lax.fori_loop(0, a_ref.shape[0], block_step, 0)

    add_rows(here, 0, True)
    add_rows(here, 1, False)

    def source_step(at, carry):
        distance, way = at // 2 + 1, 1 - at % 2 * 2
        source = here - way * distance

        @pl.when((source + size) // size * ((2 * size - 1 - source) // size) > 0)
        def _():
            def half_step(piece, carry):
                @pl.when(place(way) == size - 1)
                def _():
                    for slot in range(half):
                        landed(way, distance, piece * half + slot).wait_recv()

                add_rows(source, piece, False)
                return carry

            lax.fori_loop(0, 2, half_step, 0)

        return carry

    lax.fori_loop(0, 2 * (size - 1), source_step, 0)
    save_a = pltpu.make_async_copy(a_ref, a_out, sems["save"].at[0])
    save_a.start()

    gram_a, gram_land = room["gram_a"], room["gram_land"]
    room["gram"][...] = gram_rows(a_ref, even, odd)
    gram_copies = net.scatter("aux", room["gram"], gram_land)

    def second_step(slot, carry):
        nu_block = nu_ref[list_ref[2, slot]]
        a_high, a_low = split_two(a_ref[lax.rem(list_ref[0, slot], a_ref.shape[0])])
        weights = jnp.concatenate([a_high, a_high, a_low, a_low], axis=0)
        group = 8
        for start in range(0, edge, group):
            x_high, x_low = split_two(x_buf[slot, :, start * edge:(start + group) * edge])
            turned = jnp.concatenate([x_high, x_low], axis=0).T
            e = jnp.dot(
                jnp.concatenate([turned, turned], axis=1), weights, preferred_element_type=f32
            )
            e_ref[slot, start * edge:(start + group) * edge, :] = e
            part[slot, start:start + group, :] = jnp.sum(
                e.reshape(group, edge, rank) * nu_block[None], axis=1
            )
        return carry

    def gather_blocks(dimension, out_ref, columns=slice(None)):
        blocks = out_ref.shape[0] // edge
        places = [lax.rem(list_ref[dimension, slot], blocks) for slot in range(slots)]
        lives = [list_ref[3, slot].astype(f32) for slot in range(slots)]

        def block_step(block, carry):
            total = jnp.zeros((edge, out_ref.shape[1]), f32)
            for slot in range(slots):
                weight = (places[slot] == block).astype(f32) * lives[slot]
                total += part[slot, :, columns] * weight
            out_ref[pl.ds(aligned(block * edge, edge), edge), :] = total
            return carry

        lax.fori_loop(0, blocks, block_step, 0)

    lax.fori_loop(0, half, second_step, 0)
    arrive(gram_copies)
    gram_a[rows_of(gram_a), :] = total_of(gram_land)
    gram_copies = net.spread("aux", gram_a, rank // count)
    lax.fori_loop(half, slots, second_step, 0)
    gather_blocks(1, room["terms"])
    terms = room["terms"]
    terms_sum = PairScatter(
        net, "aux", lambda owner: terms.at[rows_of(terms, owner), :],
        room["terms_pair"], room["terms_stage"], room["terms_land"]
    )
    terms_sum.start()

    arrive(gram_copies)
    unit_a, scale_a = unit_gram(gram_a[...], P_SIZE)
    work[...] = unit_a * room["s_nu"][...] + ridge

    def beside_second(step):
        @pl.when(step == 1)
        def _():
            terms_sum.relay()

    sweep_inverse(work, beside_second)
    inverse = split_three(-work[...])
    b_full, b_blocks = room["b"], room["b_blocks"]
    b_full[rows_of(b_full), :] = dot_exact(
        split_three(terms_sum.total() / scale_a), inverse
    )
    even[...] = jnp.zeros_like(even)
    odd[...] = jnp.zeros_like(odd)

    def b_landed(owner):
        gram_add(b_full[rows_of(b_full, owner), :], even, odd)

    b_spread = PairSpread(net, "aux", lambda owner: b_full.at[rows_of(b_full, owner), :])
    b_spread.start()
    b_landed(mine)
    b_spread.relay(b_landed)
    b_spread.collect(b_landed)
    gram_b = room["gram_b"]
    cross = odd[...]
    gram_b[...] = even[...] + (cross + cross.T)
    z_copies = net.share("orb", gram_b.at[rows_of(gram_b), :], room["z_land"])
    save_b = pltpu.make_async_copy(b_full, b_out, sems["save"].at[1])
    save_b.start()
    b_blocks[...] = b_full[...].reshape(b_blocks.shape)

    gram_sum = room["gram_sum"]
    thirds, thirds_land, thirds_z, third_sums = (
        room[name] for name in ("thirds", "thirds_land", "thirds_z", "third_sums")
    )
    wide = rank // 2

    def third_half(side):
        columns = slice(side * wide, (side + 1) * wide)

        def third_step(slot, carry):
            b_block = b_blocks[lax.rem(list_ref[1, slot], b_blocks.shape[0])][:, columns]
            total = jnp.zeros((edge, wide), f32)
            for j in range(edge):
                total += e_ref[slot, j * edge:(j + 1) * edge, columns] * b_block[j:j + 1, :]
            part[slot, :, columns] = total
            return carry

        lax.fori_loop(0, slots, third_step, 0)
        gather_blocks(2, thirds.at[side], columns)

    def third_spread(side):
        full = third_sums.at[side]
        rows = nu_rows // count
        return PairSpread(
            net, "aux", lambda owner: full.at[pl.ds(aligned(owner * rows, 8), rows), :]
        )

    third_half(0)
    third_copies = [net.scatter("aux", thirds.at[0], thirds_land.at[0])]
    third_half(1)
    arrive(z_copies)
    gram_sum[rows_of(gram_sum), :] = total_of(room["z_land"])
    gram_spread = PairSpread(net, "aux", lambda owner: gram_sum.at[rows_of(gram_sum, owner), :])
    gram_spread.start()
    third_copies.append(net.scatter("aux", thirds.at[1], thirds_land.at[1]))
    shares, spreads = [], []
    for side in range(2):
        own = thirds_land.at[side, mine]
        shares.append(
            [
                net.plan(own, thirds_z.at[side, here], {"orb": (here + step) % size})
                for step in range(1, size)
            ]
        )
        spreads.append(third_spread(side))

    def third_landed(side):
        arrive(third_copies[side])
        total = total_of(thirds_land.at[side])
        thirds_land[side, mine] = total
        thirds_z[side, here] = total
        for copy in shares[side]:
            copy.start()

    def third_summed(side):
        arrive(shares[side])
        third_sums[side, pl.ds(aligned(mine * (nu_rows // count), 8), nu_rows // count), :] = (
            total_of(thirds_z.at[side])
        )
        spreads[side].start()

    gram_spread.relay()
    third_landed(0)
    gram_spread.collect()
    unit_b, scale_b = unit_gram(gram_sum[...], orb_rows * size)
    work[...] = unit_b * unit_gram(gram_a[...], P_SIZE)[0] + ridge

    def beside_third(step):
        for when, act, side in (
            (2, third_landed, 1), (panels - 3, third_summed, 0)
        ):

            @pl.when(step == when)
            def _():
                act(side)

    sweep_inverse(work, beside_third)
    inverse = split_three(-work[...])
    third_summed(1)
    for spread in spreads:
        spread.relay()
    for spread in spreads:
        spread.collect()
    third_all = jnp.concatenate([third_sums[0], third_sums[1]], axis=1)
    c_new = dot_exact(split_three(third_all / scale_a / scale_b), inverse)
    scale_c = jnp.sqrt(jnp.sum(c_new * c_new, axis=0, keepdims=True) / nu_rows + epsilon)
    c_out[...] = c_new
    scale_out[0:1, :] = scale_a
    scale_out[1:2, :] = scale_b
    scale_out[2:3, :] = scale_c

    def last(slot, carry):
        for way in (1, -1):
            for distance in range(size - 1):

                @pl.when(goes(way, distance))
                def _():
                    hop(way, distance, slot).wait_send()

        return carry

    lax.fori_loop(0, slots, last, 0)
    save_a.wait()
    save_b.wait()
    net.finish()


def scale_kernel(a_hbm, b_hbm, c_hbm, scale_ref, a_out, b_out, c_out, a, b, c, load_sem, save_sem):
    pieces = []
    for at, (source, target, buffer) in enumerate(
        ((a_hbm, a_out, a), (b_hbm, b_out, b), (c_hbm, c_out, c))
    ):
        step = min(512, buffer.shape[0])
        for start in range(0, buffer.shape[0], step):
            number = len(pieces)
            rows = pl.ds(start, step)
            pieces.append(
                (
                    at,
                    buffer,
                    rows,
                    pltpu.make_async_copy(
                        source.at[rows, :], buffer.at[rows, :], load_sem.at[number]
                    ),
                    pltpu.make_async_copy(
                        buffer.at[rows, :], target.at[rows, :], save_sem.at[number]
                    ),
                )
            )
    for piece in pieces:
        piece[3].start()
    for at, buffer, rows, load, save in pieces:
        load.wait()
        buffer[rows, :] = buffer[rows, :] / scale_ref[at:at + 1, :]
        save.start()
    for piece in pieces:
        piece[4].wait()


def per_device(tiles, tile_list, orb_factor, nu_factor):
    slots, edge, tile_width = tiles.shape
    rank = nu_factor.shape[1]
    aux_size, orb_size = lax.axis_size("aux"), lax.axis_size("orb")
    first_rows = P_SIZE // aux_size
    orb_rows, nu_rows = orb_factor.shape[0], nu_factor.shape[0]
    square = (rank, rank)
    shapes = {
        "x": (slots, edge, tile_width),
        "parts": (orb_size * slots * edge, rank),
        "table": (orb_size * 2, 8, rank),
        "a": (first_rows // edge, edge, rank),
        "e": (slots, tile_width, rank),
        "part": (slots, edge, rank),
        "q": (slots // 2 * edge, rank),
        "orb_land": (orb_size, rank // aux_size, rank),
        "gram_land": (aux_size, rank // aux_size, rank),
        "terms": (orb_rows, rank),
        "terms_pair": (aux_size // 2, orb_rows // aux_size, rank),
        "terms_stage": (aux_size // 2, orb_rows // aux_size, rank),
        "terms_land": (aux_size // 2, orb_rows // aux_size, rank),
        "b": (orb_rows, rank),
        "b_blocks": (orb_rows // edge, edge, rank),
        "z_land": (orb_size, rank // aux_size, rank),
        "thirds": (2, nu_rows, rank // 2),
        "thirds_land": (2, aux_size, nu_rows // aux_size, rank // 2),
        "thirds_z": (2, orb_size, nu_rows // aux_size, rank // 2),
        "third_sums": (2, nu_rows, rank // 2),
    }
    for name in ("work", "even", "odd", "orb_gram", "orb_sum", "s_nu", "gram", "gram_a", "gram_b", "gram_sum"):
        shapes[name] = square
    net_count = 10 * (aux_size - 1) + 5 * (orb_size - 1)
    dma = pltpu.SemaphoreType.DMA
    semaphores = {
        "x": dma((slots,)),
        "send": dma((net_count,)),
        "recv": dma((net_count,)),
        "hop_send": dma((2, orb_size - 1, slots)),
        "hop_recv": dma((2, orb_size - 1, slots)),
        "save": dma((2,)),
    }
    room = {name: pltpu.VMEM(shape, f32) for name, shape in shapes.items()}
    room["inverse"] = pltpu.VMEM((3,) + square, bf16)
    vmem = pl.BlockSpec(memory_space=pltpu.VMEM)
    hbm = pl.BlockSpec(memory_space=pltpu.HBM)

    def kernel(list_ref, x_hbm, orb_ref, nu_ref, a_out, b_out, c_out, scale_out, *scratch):
        names = list(room)
        sweep_kernel(
            edge, list_ref, x_hbm, orb_ref, nu_ref, a_out, b_out, c_out, scale_out,
            dict(zip(names, scratch)), dict(zip(semaphores, scratch[len(names):]))
        )

    a_new, b_new, c_new, scales = pl.pallas_call(
        kernel,
        out_shape=(
            jax.ShapeDtypeStruct((first_rows // edge, edge, rank), f32),
            jax.ShapeDtypeStruct((orb_rows, rank), f32),
            jax.ShapeDtypeStruct((nu_rows, rank), f32),
            jax.ShapeDtypeStruct((8, rank), f32),
        ),
        in_specs=[pl.BlockSpec(memory_space=pltpu.SMEM), hbm, vmem, vmem],
        out_specs=(hbm, hbm, vmem, vmem),
        scratch_shapes=list(room.values()) + list(semaphores.values()),
        compiler_params=pltpu.CompilerParams(
            collective_id=5, has_side_effects=True, vmem_limit_bytes=62 << 20
        ),
        name="sweep",
    )(tile_list, tiles, orb_factor.reshape(-1, edge, rank), nu_factor.reshape(-1, edge, rank))
    rows = (first_rows, orb_rows, nu_rows)
    count = sum(-(-size // 512) for size in rows)
    return pl.pallas_call(
        scale_kernel,
        out_shape=tuple(jax.ShapeDtypeStruct((size, rank), f32) for size in rows),
        in_specs=[hbm, hbm, hbm, vmem],
        out_specs=(hbm, hbm, hbm),
        scratch_shapes=[pltpu.VMEM((size, rank), f32) for size in rows]
        + [dma((count,)), dma((count,))],
        compiler_params=pltpu.CompilerParams(vmem_limit_bytes=60 << 20),
        name="scale",
    )(a_new.reshape(first_rows, rank), b_new, c_new, scales)


def solution(mesh):
    return jax.shard_map(
        per_device,
        mesh=mesh,
        in_specs=(P(("aux", "orb"), None, None), P(None, ("aux", "orb")), P("orb", None), P()),
        out_specs=(P("aux", None), P("orb", None), P()),
        check_vma=False,
    )
```

```python
import functools

import jax
import jax.numpy as jnp
from jax import lax
from jax.experimental import pallas as pl
from jax.experimental.pallas import tpu as pltpu
from jax.sharding import PartitionSpec as P

P_SIZE = 16384
MU = 4096
NU = 512

ridge_weight = 0.5
epsilon = 1e-06
highest = lax.Precision.HIGHEST
f32 = jnp.float32
bf16 = jnp.bfloat16
PANEL = 32


MESH = pl.DeviceIdType.MESH


def split_two(x):
    high = x.astype(bf16)
    return high, (x - high.astype(f32)).astype(bf16)


def split_three(x):
    high = x.astype(bf16)
    rest = x - high.astype(f32)
    middle = rest.astype(bf16)
    return high, middle, (rest - middle.astype(f32)).astype(bf16)


def aligned(value, step):
    return pl.multiple_of(value, step)


def dot_t(left, right):
    return lax.dot_general(left, right, (((0,), (0,)), ((), ())), preferred_element_type=f32)


def dot_exact(left, right):
    l_high, l_middle, l_low = left
    r_high, r_middle, r_low = right
    dot = functools.partial(jnp.dot, preferred_element_type=f32)
    small = dot(l_low, r_high) + dot(l_high, r_low) + dot(l_middle, r_middle)
    return dot(l_high, r_high) + (dot(l_middle, r_high) + dot(l_high, r_middle) + small)


def gram_add(x, even_ref, odd_ref):
    high, middle, low = split_three(x)
    even_ref[...] += dot_t(high, high) + dot_t(middle, middle)
    odd_ref[...] += dot_t(high, middle) + dot_t(high, low)


def gram_rows(x_ref, even_ref, odd_ref):
    even_ref[...] = jnp.zeros_like(even_ref)
    odd_ref[...] = jnp.zeros_like(odd_ref)
    group = min(8, x_ref.shape[0])

    def step(at, carry):
        rows = x_ref[pl.ds(at * group, group)]
        gram_add(rows.reshape(-1, rows.shape[2]), even_ref, odd_ref)
        return carry

    lax.fori_loop(0, x_ref.shape[0] // group, step, 0)
    odd = odd_ref[...]
    return even_ref[...] + (odd + odd.T)


def enter(axes):
    barrier = pltpu.get_barrier_semaphore()
    count = 0
    for axis in axes:
        size, here = lax.axis_size(axis), lax.axis_index(axis)
        for step in range(1, size):
            pl.semaphore_signal(
                barrier, inc=1, device_id={axis: (here + step) % size}, device_id_type=MESH
            )
            count += 1
    pl.semaphore_wait(barrier, count)


class Net:
    def __init__(self, send, recv):
        self.send, self.recv, self.copies = send, recv, []

    def plan(self, src, dst, to):
        at = len(self.copies)
        copy = pltpu.make_async_remote_copy(
            src_ref=src,
            dst_ref=dst,
            send_sem=self.send.at[at],
            recv_sem=self.recv.at[at],
            device_id=to,
            device_id_type=MESH,
        )
        self.copies.append(copy)
        return copy

    def copy(self, src, dst, to):
        copy = self.plan(src, dst, to)
        copy.start()
        return copy

    def scatter(self, axis, src, land):
        size, here = lax.axis_size(axis), lax.axis_index(axis)
        rows = land.shape[1]
        land[here] = src[pl.ds(aligned(here * rows, 8), rows), :]
        copies = []
        for step in range(1, size):
            to = (here + step) % size
            block = src.at[pl.ds(aligned(to * rows, 8), rows), :]
            copies.append(self.copy(block, land.at[here], {axis: to}))
        return copies

    def share(self, axis, src, land):
        size, here = lax.axis_size(axis), lax.axis_index(axis)
        land[here] = src[...]
        return [
            self.copy(src, land.at[here], {axis: (here + step) % size}) for step in range(1, size)
        ]

    def spread(self, axis, full, rows):
        size, here = lax.axis_size(axis), lax.axis_index(axis)
        own = full.at[pl.ds(aligned(here * rows, 8), rows), :]
        return [self.copy(own, own, {axis: (here + step) % size}) for step in range(1, size)]

    def finish(self):
        for copy in self.copies:
            copy.wait_send()


class PairSpread:
    def __init__(self, net, axis, block):
        size, here = lax.axis_size(axis), lax.axis_index(axis)
        chips, chip, core = size // 2, here // 2, here % 2
        other = here + 1 - 2 * core
        self.own = here
        self.near_from = [chip * 2 + 1 - core]
        self.far_from, self.far, self.relays = [], [], []
        own = block(here)
        self.near = [net.plan(own, own, {axis: other})]
        for step in range(1, chips):
            target = (chip + step) % chips * 2 + core
            self.far.append(net.plan(own, own, {axis: target}))
            source = (chip + chips - step) % chips * 2
            self.far_from.append(source + core)
            self.near_from.append(source + 1 - core)
            passed = block(source + core)
            self.near.append(net.plan(passed, passed, {axis: other}))

    def start(self):
        for copy in self.far:
            copy.start()
        self.near[0].start()

    def relay(self, landed=None):
        for copy, near, owner in zip(self.far, self.near[1:], self.far_from):
            copy.wait_recv()
            near.start()
            if landed is not None:
                landed(owner)

    def collect(self, landed=None):
        for copy, owner in zip(self.near, self.near_from):
            copy.wait_recv()
            if landed is not None:
                landed(owner)


class PairScatter:
    def __init__(self, net, axis, block, pair, stage, land):
        size, here = lax.axis_size(axis), lax.axis_index(axis)
        chips, chip, core = size // 2, here // 2, here % 2
        other = here + 1 - 2 * core
        self.chip, self.land, self.pair, self.stage = chip, land, pair, stage
        self.first, self.second, self.targets = [], [], []
        for step in range(1, chips + 1):
            target = (chip + step) % chips
            self.targets.append((target, block(target * 2 + core)))
            away = block(target * 2 + 1 - core)
            self.first.append(net.plan(away, pair.at[target], {axis: other}))
            if step < chips:
                self.second.append(
                    net.plan(stage.at[target], land.at[chip], {axis: target * 2 + core})
                )

    def start(self):
        for copy in self.first:
            copy.start()

    def relay(self):
        for copy, send, (target, own) in zip(self.first, self.second, self.targets):
            copy.wait_recv()
            self.stage[target] = own[...] + self.pair[target]
            send.start()
        self.first[-1].wait_recv()
        target, own = self.targets[-1]
        self.land[self.chip] = own[...] + self.pair[target]

    def total(self):
        arrive(self.second)
        return total_of(self.land)


def arrive(copies):
    for copy in copies:
        copy.wait_recv()


def total_of(land):
    total = land[0]
    for at in range(1, land.shape[0]):
        total += land[at]
    return total


def eye_mask(n):
    return lax.broadcasted_iota(jnp.int32, (n, n), 0) == lax.broadcasted_iota(jnp.int32, (n, n), 1)


def unit_gram(gram, rows):
    diagonal = jnp.where(eye_mask(gram.shape[0]), gram, 0.0)
    along = jnp.sqrt(jnp.sum(diagonal, axis=0, keepdims=True) / rows + epsilon)
    down = jnp.sqrt(jnp.sum(diagonal, axis=1, keepdims=True) / rows + epsilon)
    return gram / down / along / rows, along


def pivot_panel(tiles, cols, lane, row):
    height = len(tiles[0])
    sub = tiles[0][0].shape[0]

    def columns(first):
        return [
            [jnp.broadcast_to(tile[:, k:k + 1], tile.shape) for tile in tiles[0]]
            for k in range(first, first + cols)
        ]

    def take(pieces, k):
        at = k % sub
        return pieces[k // sub][at:at + 1, :]

    def step(pieces, firsts, seconds, k, new_first, new_second, clear=None):
        out = []
        for g in range(height):
            base = pieces[g] if clear is None else jnp.where(clear, 0.0, pieces[g])
            value = base - firsts[g] * new_first - seconds[g] * new_second
            if g == k // sub:
                value = jnp.where(row == k % sub, new_first, value)
                value = jnp.where(row == k % sub + 1, new_second, value)
            out.append(value)
        return out

    now = columns(0)
    later = None
    for start in range(0, height * sub, cols):
        for j in range(0, cols, 2):
            k = start + j
            if j == cols - 2 and start + cols < height * sub:
                later = columns(start + cols)
            firsts, seconds = now[j], now[j + 1]
            a, b = take(firsts, k), take(seconds, k)
            c, d = take(firsts, k + 1), take(seconds, k + 1)
            scale = 1.0 / (a * d - b * c)
            a, b, c, d = d * scale, b * scale, c * scale, a * scale
            for i in range(j + 2, cols):
                up, down = take(now[i], k), take(now[i], k + 1)
                now[i] = step(now[i], firsts, seconds, k, a * up - b * down, d * down - c * up)
            if later is not None:
                for i in range(cols):
                    up, down = take(later[i], k), take(later[i], k + 1)
                    later[i] = step(
                        later[i], firsts, seconds, k, a * up - b * down, d * down - c * up
                    )
            for h, pieces in enumerate(tiles):
                up, down = take(pieces, k), take(pieces, k + 1)
                clear = None
                if h == 0:
                    at_up, at_down = lane == k, lane == k + 1
                    clear = at_up | at_down
                    up = jnp.where(at_up[:1], 1.0, jnp.where(at_down[:1], 0.0, up))
                    down = jnp.where(at_down[:1], 1.0, jnp.where(at_up[:1], 0.0, down))
                tiles[h] = step(
                    pieces, firsts, seconds, k, a * up - b * down, d * down - c * up, clear
                )
        now, later = later, None
    return tiles


def sweep_inverse(a_ref, beside=None, first=0, last=None):
    n = a_ref.shape[0]
    sub, wide = 8, 128
    lane = lax.broadcasted_iota(jnp.int32, (PANEL, n), 1)
    tile_lane = lax.broadcasted_iota(jnp.int32, (sub, wide), 1)
    tile_row = lax.broadcasted_iota(jnp.int32, (sub, wide), 0)

    def panel_step(step, carry):
        if beside is not None:
            beside(step)
        before = a_ref[:PANEL, :]
        tiles = [
            [before[g:g + sub, h:h + wide] for g in range(0, PANEL, sub)]
            for h in range(0, n, wide)
        ]
        tiles = pivot_panel(tiles, 8, tile_lane, tile_row)
        panel = jnp.concatenate([jnp.concatenate(pieces, axis=0) for pieces in tiles], axis=1)
        own = lane < PANEL
        update = jnp.where(own, -panel, panel)
        w_high, w_middle, w_low = split_three(before)
        z_high, z_middle, z_low = split_three(update)
        left = jnp.concatenate([w_low, w_middle, w_high, w_middle, w_high, w_high], axis=0)
        right = jnp.concatenate([z_high, z_middle, z_low, z_high, z_middle, z_high], axis=0)
        change = lax.dot_general(
            left, right, (((0,), (0,)), ((), ())), preferred_element_type=f32
        )
        others = jnp.where(own[:1], 0.0, a_ref[PANEL:, :]) - change[PANEL:, :]
        a_ref[:n - PANEL, :] = pltpu.roll(others, n - PANEL, 1)
        a_ref[n - PANEL:, :] = pltpu.roll(update, n - PANEL, 1)
        return carry

    lax.fori_loop(first, n // PANEL if last is None else last, panel_step, 0)


def sweep_kernel(
    edge, list_ref, x_hbm, orb_hbm, nu_hbm, a_out, b_out, c_out, scale_out, room, sems
):
    orb_ref, nu_ref = room["orb"], room["nu"]
    slots = list_ref.shape[1]
    here, size = lax.axis_index("orb"), lax.axis_size("orb")
    mine, count = lax.axis_index("aux"), lax.axis_size("aux")
    rank = nu_ref.shape[2]
    x_buf, parts, table, a_ref, e_ref, part = (
        room[name] for name in ("x", "parts", "table", "a", "e", "part")
    )
    work, even, odd = room["work"], room["even"], room["odd"]
    orb_rows, nu_rows = orb_ref.shape[0] * edge, nu_ref.shape[0] * edge
    first_base = mine * a_ref.shape[0]
    hop_send, hop_recv = sems["hop_send"], sems["hop_recv"]

    def load(slot):
        return pltpu.make_async_copy(x_hbm.at[slot], x_buf.at[slot], sems["x"].at[slot])

    def rows_of(ref, owner=mine):
        rows = ref.shape[0] // count
        return pl.ds(aligned(owner * rows, 8), rows)

    factor_loads = (
        pltpu.make_async_copy(nu_hbm, nu_ref, sems["factors"].at[0]),
        pltpu.make_async_copy(orb_hbm, orb_ref, sems["factors"].at[1]),
    )
    early, late = slots * 3 // 8, slots - slots // 4
    for copy in factor_loads:
        copy.start()
    for slot in range(early):
        load(slot).start()
    enter(("aux", "orb"))
    for slot in range(early, slots):
        load(slot).start()
    for copy in factor_loads:
        copy.wait()
    net = Net(sems["send"], sems["recv"])

    def part_rows(source, slot):
        return parts.at[pl.ds(aligned((source * slots + slot) * edge, edge), edge), :]

    def hop(way, distance, slot):
        rows = part_rows(here - way * distance, slot)
        lane = (1 - way) // 2
        return pltpu.make_async_remote_copy(
            src_ref=rows,
            dst_ref=rows,
            send_sem=hop_send.at[lane, distance, slot],
            recv_sem=hop_recv.at[lane, distance, slot],
            device_id={"orb": here + way},
            device_id_type=MESH,
        )

    def landed(way, distance, slot):
        rows = part_rows(here - way * distance, slot)
        lane = (1 - way) // 2
        return pltpu.make_async_remote_copy(
            src_ref=rows,
            dst_ref=rows,
            send_sem=hop_send.at[lane, distance - 1, slot],
            recv_sem=hop_recv.at[lane, distance - 1, slot],
            device_id={"orb": here - way},
            device_id_type=MESH,
        )

    def place(way):
        return (size - 1) * ((1 - way) // 2) + way * here

    def goes(way, distance):
        at = place(way)
        return (at + size - 1 - distance) // (size - 1) * ((2 * size - 3 - at) // (size - 1)) > 0

    def forward(distance, slot):
        for way in (1, -1):

            @pl.when(goes(way, distance))
            def _():
                landed(way, distance, slot).wait_recv()
                hop(way, distance, slot).start()

    def slot_step(slot, carry):
        load(slot).wait()
        nu_block = nu_ref[list_ref[2, slot]]
        orb_block = orb_ref[lax.rem(list_ref[1, slot], orb_ref.shape[0])]
        group = 4
        total = jnp.zeros((edge, rank), f32)
        for start in range(0, edge, group):
            x_high, x_low = split_two(x_buf[slot, :, start * edge:(start + group) * edge])
            stacked = jnp.concatenate([x_high, x_low], axis=0)
            product = jnp.concatenate(
                [nu_block * orb_block[j:j + 1, :] for j in range(start, start + group)], axis=0
            )
            high, low = split_two(product)
            main = jnp.dot(stacked, high, preferred_element_type=f32)
            rest = jnp.dot(x_high, low, preferred_element_type=f32)
            total += main[:edge] + (main[edge:] + rest)
        live = list_ref[3, slot].astype(f32)
        part_rows(here, slot)[...] = total * live
        for way in (1, -1):

            @pl.when(goes(way, 0))
            def _():
                hop(way, 0, slot).start()

        return carry

    lax.fori_loop(0, early, slot_step, 0)

    half, pieces = slots // 2, 4
    each = slots // pieces
    row = lax.broadcasted_iota(jnp.int32, table.shape[1:], 0)
    for piece in range(pieces):
        own_at = jnp.zeros(table.shape[1:], f32)
        for slot in range(each):
            value = (list_ref[0, piece * each + slot] - first_base).astype(f32)
            own_at = jnp.where(row == slot, value, own_at)
        table[pieces * here + piece] = own_at
    own_table = table.at[pl.ds(pieces * here, pieces)]
    table_copies = [
        net.copy(own_table, own_table, {"orb": (here + step) % size}) for step in range(1, size)
    ]
    orb_gram, orb_land, orb_sum = room["orb_gram"], room["orb_land"], room["orb_sum"]
    orb_gram[...] = gram_rows(orb_ref, even, odd)
    gram_copies = net.share("orb", orb_gram.at[rows_of(orb_gram), :], orb_land)
    room["s_nu"][...] = gram_rows(nu_ref, even, odd) / NU
    lax.fori_loop(early, late, slot_step, 0)
    arrive(gram_copies)
    orb_sum[rows_of(orb_sum), :] = total_of(orb_land)
    gram_copies = net.spread("aux", orb_sum, rank // count)
    lax.fori_loop(late, slots, slot_step, 0)

    arrive(gram_copies)
    ridge = jnp.where(eye_mask(rank), ridge_weight, 0.0)
    work[...] = orb_sum[...] / (orb_rows * size) * room["s_nu"][...] + ridge
    panels = rank // PANEL
    def beside_first(step):
        if size > 2:
            for at in range(-(-slots // panels)):
                slot = step * -(-slots // panels) + at

                @pl.when(slot < slots)
                def _():
                    forward(1, slot)

    sweep_inverse(work, beside_first)
    for at, piece in enumerate(split_three(-work[...])):
        room["inverse"][at] = piece
    arrive(table_copies)

    def add_rows(source, piece, clear):
        start = piece * each
        rows = parts[pl.ds(aligned((source * slots + start) * edge, edge), each * edge), :]
        inverse = tuple(room["inverse"][at] for at in range(3))
        room["q"][...] = dot_exact(split_three(rows), inverse)
        places = table[pieces * source + piece]

        def block_step(block, carry):
            name = jnp.full((1, rank), block, jnp.int32).astype(f32)
            total = jnp.zeros((edge, rank), f32) if clear else a_ref[block]
            for slot in range(each):
                weight = jnp.where(places[slot:slot + 1, :] == name, 1.0, 0.0)
                total += room["q"][slot * edge:(slot + 1) * edge, :] * weight
            a_ref[block] = total
            return carry

        lax.fori_loop(0, a_ref.shape[0], block_step, 0)

    for piece in range(pieces):
        add_rows(here, piece, piece == 0)
        if size > 3:
            forward(2, piece)

    def source_step(at, carry):
        if size > 3:

            @pl.when(at == 1)
            def _():
                for slot in range(pieces, (pieces + slots) // 2):
                    forward(2, slot)

            @pl.when(at == 2)
            def _():
                for slot in range((pieces + slots) // 2, slots):
                    forward(2, slot)
                for far in range(3, size - 1):
                    for slot in range(slots):
                        forward(far, slot)

        distance, way = at // 2 + 1, 1 - at % 2 * 2
        source = here - way * distance

        @pl.when((source + size) // size * ((2 * size - 1 - source) // size) > 0)
        def _():
            def piece_step(piece, carry):
                @pl.when(place(way) == size - 1)
                def _():
                    for slot in range(each):
                        landed(way, distance, piece * each + slot).wait_recv()

                add_rows(source, piece, False)
                return carry

            lax.fori_loop(0, pieces, piece_step, 0)

        return carry

    lax.fori_loop(0, 2 * (size - 1), source_step, 0)
    save_a = pltpu.make_async_copy(a_ref, a_out, sems["save"].at[0])
    save_a.start()

    gram_a, gram_land = room["gram_a"], room["gram_land"]
    room["gram"][...] = gram_rows(a_ref, even, odd)
    gram_copies = net.scatter("aux", room["gram"], gram_land)

    def second_step(slot, carry):
        nu_block = nu_ref[list_ref[2, slot]]
        a_high, a_low = split_two(a_ref[lax.rem(list_ref[0, slot], a_ref.shape[0])])
        weights = jnp.concatenate([a_high, a_high, a_low, a_low], axis=0)
        group = 8
        for start in range(0, edge, group):
            x_high, x_low = split_two(x_buf[slot, :, start * edge:(start + group) * edge])
            turned = jnp.concatenate([x_high, x_low], axis=0).T
            e = jnp.dot(
                jnp.concatenate([turned, turned], axis=1), weights, preferred_element_type=f32
            )
            e_ref[slot, start * edge:(start + group) * edge, :] = e
            part[slot, start:start + group, :] = jnp.sum(
                e.reshape(group, edge, rank) * nu_block[None], axis=1
            )
        return carry

    def gather_blocks(dimension, out_ref, columns=slice(None)):
        blocks = out_ref.shape[0] // edge
        places = [lax.rem(list_ref[dimension, slot], blocks) for slot in range(slots)]
        lives = [list_ref[3, slot].astype(f32) for slot in range(slots)]

        def block_step(block, carry):
            total = jnp.zeros((edge, out_ref.shape[1]), f32)
            for slot in range(slots):
                weight = (places[slot] == block).astype(f32) * lives[slot]
                total += part[slot, :, columns] * weight
            out_ref[pl.ds(aligned(block * edge, edge), edge), :] = total
            return carry

        lax.fori_loop(0, blocks, block_step, 0)

    lax.fori_loop(0, half, second_step, 0)
    arrive(gram_copies)
    gram_a[rows_of(gram_a), :] = total_of(gram_land)
    gram_copies = net.spread("aux", gram_a, rank // count)
    lax.fori_loop(half, slots, second_step, 0)
    gather_blocks(1, room["terms"])
    terms = room["terms"]
    terms_sum = PairScatter(
        net, "aux", lambda owner: terms.at[rows_of(terms, owner), :],
        room["terms_pair"], room["terms_stage"], room["terms_land"]
    )
    terms_sum.start()

    arrive(gram_copies)
    unit_a, scale_a = unit_gram(gram_a[...], P_SIZE)
    work[...] = unit_a * room["s_nu"][...] + ridge

    def beside_second(step):
        @pl.when(step == 1)
        def _():
            terms_sum.relay()

    sweep_inverse(work, beside_second)
    inverse = split_three(-work[...])
    b_full, b_blocks = room["b"], room["b_blocks"]
    b_full[rows_of(b_full), :] = dot_exact(
        split_three(terms_sum.total() / scale_a), inverse
    )
    even[...] = jnp.zeros_like(even)
    odd[...] = jnp.zeros_like(odd)

    def b_landed(owner):
        gram_add(b_full[rows_of(b_full, owner), :], even, odd)

    b_spread = PairSpread(net, "aux", lambda owner: b_full.at[rows_of(b_full, owner), :])
    b_spread.start()
    b_landed(mine)
    b_spread.relay(b_landed)
    b_spread.collect(b_landed)
    gram_b = room["gram_b"]
    cross = odd[...]
    gram_b[...] = even[...] + (cross + cross.T)
    z_copies = net.share("orb", gram_b.at[rows_of(gram_b), :], room["z_land"])
    save_b = pltpu.make_async_copy(b_full, b_out, sems["save"].at[1])
    save_b.start()
    b_blocks[...] = b_full[...].reshape(b_blocks.shape)

    gram_sum = room["gram_sum"]
    thirds, thirds_land, thirds_z, third_sums = (
        room[name] for name in ("thirds", "thirds_land", "thirds_z", "third_sums")
    )
    wide = rank // 2

    def third_half(side):
        columns = slice(side * wide, (side + 1) * wide)

        def third_step(slot, carry):
            b_block = b_blocks[lax.rem(list_ref[1, slot], b_blocks.shape[0])][:, columns]
            total = jnp.zeros((edge, wide), f32)
            for j in range(edge):
                total += e_ref[slot, j * edge:(j + 1) * edge, columns] * b_block[j:j + 1, :]
            part[slot, :, columns] = total
            return carry

        lax.fori_loop(0, slots, third_step, 0)
        gather_blocks(2, thirds.at[side], columns)

    def third_spread(side):
        full = third_sums.at[side]
        rows = nu_rows // count
        return PairSpread(
            net, "aux", lambda owner: full.at[pl.ds(aligned(owner * rows, 8), rows), :]
        )

    third_half(0)
    third_copies = [net.scatter("aux", thirds.at[0], thirds_land.at[0])]
    third_half(1)
    arrive(z_copies)
    gram_sum[rows_of(gram_sum), :] = total_of(room["z_land"])
    gram_spread = PairSpread(net, "aux", lambda owner: gram_sum.at[rows_of(gram_sum, owner), :])
    gram_spread.start()
    third_copies.append(net.scatter("aux", thirds.at[1], thirds_land.at[1]))
    shares, spreads = [], []
    for side in range(2):
        own = thirds_land.at[side, mine]
        shares.append(
            [
                net.plan(own, thirds_z.at[side, here], {"orb": (here + step) % size})
                for step in range(1, size)
            ]
        )
        spreads.append(third_spread(side))

    def third_landed(side):
        arrive(third_copies[side])
        total = total_of(thirds_land.at[side])
        thirds_land[side, mine] = total
        thirds_z[side, here] = total
        for copy in shares[side]:
            copy.start()

    def third_summed(side):
        arrive(shares[side])
        third_sums[side, pl.ds(aligned(mine * (nu_rows // count), 8), nu_rows // count), :] = (
            total_of(thirds_z.at[side])
        )
        spreads[side].start()

    gram_spread.relay()
    third_landed(0)
    gram_spread.collect()
    unit_b, scale_b = unit_gram(gram_sum[...], orb_rows * size)
    work[...] = unit_b * unit_gram(gram_a[...], P_SIZE)[0] + ridge

    def beside_third(step):
        for when, act, side in (
            (2, third_landed, 1), (panels - 3, third_summed, 0)
        ):

            @pl.when(step == when)
            def _():
                act(side)

    sweep_inverse(work, beside_third)
    inverse = split_three(-work[...])
    third_summed(1)
    for spread in spreads:
        spread.relay()
    for spread in spreads:
        spread.collect()
    third_all = jnp.concatenate([third_sums[0], third_sums[1]], axis=1)
    c_new = dot_exact(split_three(third_all / scale_a / scale_b), inverse)
    scale_c = jnp.sqrt(jnp.sum(c_new * c_new, axis=0, keepdims=True) / nu_rows + epsilon)
    c_out[...] = c_new
    scale_out[0:1, :] = scale_a
    scale_out[1:2, :] = scale_b
    scale_out[2:3, :] = scale_c

    def last(slot, carry):
        for way in (1, -1):
            for distance in range(size - 1):

                @pl.when(goes(way, distance))
                def _():
                    hop(way, distance, slot).wait_send()

        return carry

    lax.fori_loop(0, slots, last, 0)
    save_a.wait()
    save_b.wait()
    net.finish()


def scale_kernel(a_hbm, b_hbm, c_hbm, scale_ref, a_out, b_out, c_out, a, b, c, load_sem, save_sem):
    pieces = []
    for at, (source, target, buffer) in enumerate(
        ((a_hbm, a_out, a), (b_hbm, b_out, b), (c_hbm, c_out, c))
    ):
        step = min(512, buffer.shape[0])
        for start in range(0, buffer.shape[0], step):
            number = len(pieces)
            rows = pl.ds(start, step)
            pieces.append(
                (
                    at,
                    buffer,
                    rows,
                    pltpu.make_async_copy(
                        source.at[rows, :], buffer.at[rows, :], load_sem.at[number]
                    ),
                    pltpu.make_async_copy(
                        buffer.at[rows, :], target.at[rows, :], save_sem.at[number]
                    ),
                )
            )
    for piece in pieces:
        piece[3].start()
    for at, buffer, rows, load, save in pieces:
        load.wait()
        buffer[rows, :] = buffer[rows, :] / scale_ref[at:at + 1, :]
        save.start()
    for piece in pieces:
        piece[4].wait()


def per_device(tiles, tile_list, orb_factor, nu_factor):
    slots, edge, tile_width = tiles.shape
    rank = nu_factor.shape[1]
    aux_size, orb_size = lax.axis_size("aux"), lax.axis_size("orb")
    first_rows = P_SIZE // aux_size
    orb_rows, nu_rows = orb_factor.shape[0], nu_factor.shape[0]
    square = (rank, rank)
    shapes = {
        "x": (slots, edge, tile_width),
        "orb": (orb_rows // edge, edge, rank),
        "nu": (nu_rows // edge, edge, rank),
        "parts": (orb_size * slots * edge, rank),
        "table": (orb_size * 4, 8, rank),
        "a": (first_rows // edge, edge, rank),
        "e": (slots, tile_width, rank),
        "part": (slots, edge, rank),
        "q": (slots // 4 * edge, rank),
        "orb_land": (orb_size, rank // aux_size, rank),
        "gram_land": (aux_size, rank // aux_size, rank),
        "terms": (orb_rows, rank),
        "terms_pair": (aux_size // 2, orb_rows // aux_size, rank),
        "terms_stage": (aux_size // 2, orb_rows // aux_size, rank),
        "terms_land": (aux_size // 2, orb_rows // aux_size, rank),
        "b": (orb_rows, rank),
        "b_blocks": (orb_rows // edge, edge, rank),
        "z_land": (orb_size, rank // aux_size, rank),
        "thirds": (2, nu_rows, rank // 2),
        "thirds_land": (2, aux_size, nu_rows // aux_size, rank // 2),
        "thirds_z": (2, orb_size, nu_rows // aux_size, rank // 2),
        "third_sums": (2, nu_rows, rank // 2),
    }
    for name in ("work", "even", "odd", "orb_gram", "orb_sum", "s_nu", "gram", "gram_a", "gram_b", "gram_sum"):
        shapes[name] = square
    net_count = 10 * (aux_size - 1) + 5 * (orb_size - 1)
    dma = pltpu.SemaphoreType.DMA
    semaphores = {
        "x": dma((slots,)),
        "factors": dma((2,)),
        "send": dma((net_count,)),
        "recv": dma((net_count,)),
        "hop_send": dma((2, orb_size - 1, slots)),
        "hop_recv": dma((2, orb_size - 1, slots)),
        "save": dma((2,)),
    }
    room = {name: pltpu.VMEM(shape, f32) for name, shape in shapes.items()}
    room["inverse"] = pltpu.VMEM((3,) + square, bf16)
    vmem = pl.BlockSpec(memory_space=pltpu.VMEM)
    hbm = pl.BlockSpec(memory_space=pltpu.HBM)

    def kernel(list_ref, x_hbm, orb_hbm, nu_hbm, a_out, b_out, c_out, scale_out, *scratch):
        names = list(room)
        sweep_kernel(
            edge, list_ref, x_hbm, orb_hbm, nu_hbm, a_out, b_out, c_out, scale_out,
            dict(zip(names, scratch)), dict(zip(semaphores, scratch[len(names):]))
        )

    a_new, b_new, c_new, scales = pl.pallas_call(
        kernel,
        out_shape=(
            jax.ShapeDtypeStruct((first_rows // edge, edge, rank), f32),
            jax.ShapeDtypeStruct((orb_rows, rank), f32),
            jax.ShapeDtypeStruct((nu_rows, rank), f32),
            jax.ShapeDtypeStruct((8, rank), f32),
        ),
        in_specs=[pl.BlockSpec(memory_space=pltpu.SMEM), hbm, hbm, hbm],
        out_specs=(hbm, hbm, vmem, vmem),
        scratch_shapes=list(room.values()) + list(semaphores.values()),
        compiler_params=pltpu.CompilerParams(
            collective_id=5, has_side_effects=True, vmem_limit_bytes=62 << 20
        ),
        name="sweep",
    )(tile_list, tiles, orb_factor.reshape(-1, edge, rank), nu_factor.reshape(-1, edge, rank))
    rows = (first_rows, orb_rows, nu_rows)
    count = sum(-(-size // 512) for size in rows)
    return pl.pallas_call(
        scale_kernel,
        out_shape=tuple(jax.ShapeDtypeStruct((size, rank), f32) for size in rows),
        in_specs=[hbm, hbm, hbm, vmem],
        out_specs=(hbm, hbm, hbm),
        scratch_shapes=[pltpu.VMEM((size, rank), f32) for size in rows]
        + [dma((count,)), dma((count,))],
        compiler_params=pltpu.CompilerParams(vmem_limit_bytes=60 << 20),
        name="scale",
    )(a_new.reshape(first_rows, rank), b_new, c_new, scales)


def solution(mesh):
    return jax.shard_map(
        per_device,
        mesh=mesh,
        in_specs=(P(("aux", "orb"), None, None), P(None, ("aux", "orb")), P("orb", None), P()),
        out_specs=(P("aux", None), P("orb", None), P()),
        check_vma=False,
    )
```

```python
import functools

import jax
import jax.numpy as jnp
from jax import lax
from jax.experimental import pallas as pl
from jax.experimental.pallas import tpu as pltpu
from jax.sharding import PartitionSpec as P

P_SIZE = 16384
MU = 4096
NU = 512

ridge_weight = 0.5
epsilon = 1e-06
highest = lax.Precision.HIGHEST
f32 = jnp.float32
bf16 = jnp.bfloat16
PANEL = 32


MESH = pl.DeviceIdType.MESH


def split_two(x):
    high = x.astype(bf16)
    return high, (x - high.astype(f32)).astype(bf16)


def split_three(x):
    high = x.astype(bf16)
    rest = x - high.astype(f32)
    middle = rest.astype(bf16)
    return high, middle, (rest - middle.astype(f32)).astype(bf16)


def aligned(value, step):
    return pl.multiple_of(value, step)


def dot_t(left, right):
    return lax.dot_general(left, right, (((0,), (0,)), ((), ())), preferred_element_type=f32)


def dot_exact(left, right):
    l_high, l_middle, l_low = left
    r_high, r_middle, r_low = right
    dot = functools.partial(jnp.dot, preferred_element_type=f32)
    small = dot(l_low, r_high) + dot(l_high, r_low) + dot(l_middle, r_middle)
    return dot(l_high, r_high) + (dot(l_middle, r_high) + dot(l_high, r_middle) + small)


def gram_add(x, even_ref, odd_ref):
    high, middle, low = split_three(x)
    even_ref[...] += dot_t(high, high) + dot_t(middle, middle)
    odd_ref[...] += dot_t(high, middle) + dot_t(high, low)


def gram_rows(x_ref, even_ref, odd_ref):
    even_ref[...] = jnp.zeros_like(even_ref)
    odd_ref[...] = jnp.zeros_like(odd_ref)
    group = min(8, x_ref.shape[0])

    def step(at, carry):
        rows = x_ref[pl.ds(at * group, group)]
        gram_add(rows.reshape(-1, rows.shape[2]), even_ref, odd_ref)
        return carry

    lax.fori_loop(0, x_ref.shape[0] // group, step, 0)
    odd = odd_ref[...]
    return even_ref[...] + (odd + odd.T)


def enter(axes):
    barrier = pltpu.get_barrier_semaphore()
    count = 0
    for axis in axes:
        size, here = lax.axis_size(axis), lax.axis_index(axis)
        for step in range(1, size):
            pl.semaphore_signal(
                barrier, inc=1, device_id={axis: (here + step) % size}, device_id_type=MESH
            )
            count += 1
    pl.semaphore_wait(barrier, count)


class Net:
    def __init__(self, send, recv):
        self.send, self.recv, self.copies = send, recv, []

    def plan(self, src, dst, to):
        at = len(self.copies)
        copy = pltpu.make_async_remote_copy(
            src_ref=src,
            dst_ref=dst,
            send_sem=self.send.at[at],
            recv_sem=self.recv.at[at],
            device_id=to,
            device_id_type=MESH,
        )
        self.copies.append(copy)
        return copy

    def copy(self, src, dst, to):
        copy = self.plan(src, dst, to)
        copy.start()
        return copy

    def scatter(self, axis, src, land):
        size, here = lax.axis_size(axis), lax.axis_index(axis)
        rows = land.shape[1]
        land[here] = src[pl.ds(aligned(here * rows, 8), rows), :]
        copies = []
        for step in range(1, size):
            to = (here + step) % size
            block = src.at[pl.ds(aligned(to * rows, 8), rows), :]
            copies.append(self.copy(block, land.at[here], {axis: to}))
        return copies

    def share(self, axis, src, land):
        size, here = lax.axis_size(axis), lax.axis_index(axis)
        land[here] = src[...]
        return [
            self.copy(src, land.at[here], {axis: (here + step) % size}) for step in range(1, size)
        ]

    def spread(self, axis, full, rows):
        size, here = lax.axis_size(axis), lax.axis_index(axis)
        own = full.at[pl.ds(aligned(here * rows, 8), rows), :]
        return [self.copy(own, own, {axis: (here + step) % size}) for step in range(1, size)]

    def finish(self):
        for copy in self.copies:
            copy.wait_send()


class PairSpread:
    def __init__(self, net, axis, block):
        size, here = lax.axis_size(axis), lax.axis_index(axis)
        chips, chip, core = size // 2, here // 2, here % 2
        other = here + 1 - 2 * core
        self.own = here
        self.near_from = [chip * 2 + 1 - core]
        self.far_from, self.far, self.relays = [], [], []
        own = block(here)
        self.near = [net.plan(own, own, {axis: other})]
        for step in range(1, chips):
            target = (chip + step) % chips * 2 + core
            self.far.append(net.plan(own, own, {axis: target}))
            source = (chip + chips - step) % chips * 2
            self.far_from.append(source + core)
            self.near_from.append(source + 1 - core)
            passed = block(source + core)
            self.near.append(net.plan(passed, passed, {axis: other}))

    def start(self):
        for copy in self.far:
            copy.start()
        self.near[0].start()

    def relay(self, landed=None):
        for copy, near, owner in zip(self.far, self.near[1:], self.far_from):
            copy.wait_recv()
            near.start()
            if landed is not None:
                landed(owner)

    def collect(self, landed=None):
        for copy, owner in zip(self.near, self.near_from):
            copy.wait_recv()
            if landed is not None:
                landed(owner)


class PairScatter:
    def __init__(self, net, axis, block, pair, stage, land):
        size, here = lax.axis_size(axis), lax.axis_index(axis)
        chips, chip, core = size // 2, here // 2, here % 2
        other = here + 1 - 2 * core
        self.chip, self.land, self.pair, self.stage = chip, land, pair, stage
        self.first, self.second, self.targets = [], [], []
        for step in range(1, chips + 1):
            target = (chip + step) % chips
            self.targets.append((target, block(target * 2 + core)))
            away = block(target * 2 + 1 - core)
            self.first.append(net.plan(away, pair.at[target], {axis: other}))
            if step < chips:
                self.second.append(
                    net.plan(stage.at[target], land.at[chip], {axis: target * 2 + core})
                )

    def start(self):
        for copy in self.first:
            copy.start()

    def relay(self):
        for copy, send, (target, own) in zip(self.first, self.second, self.targets):
            copy.wait_recv()
            self.stage[target] = own[...] + self.pair[target]
            send.start()
        self.first[-1].wait_recv()
        target, own = self.targets[-1]
        self.land[self.chip] = own[...] + self.pair[target]

    def total(self):
        arrive(self.second)
        return total_of(self.land)


def arrive(copies):
    for copy in copies:
        copy.wait_recv()


def total_of(land):
    total = land[0]
    for at in range(1, land.shape[0]):
        total += land[at]
    return total


def eye_mask(n):
    return lax.broadcasted_iota(jnp.int32, (n, n), 0) == lax.broadcasted_iota(jnp.int32, (n, n), 1)


def unit_gram(gram, rows):
    diagonal = jnp.where(eye_mask(gram.shape[0]), gram, 0.0)
    along = jnp.sqrt(jnp.sum(diagonal, axis=0, keepdims=True) / rows + epsilon)
    down = jnp.sqrt(jnp.sum(diagonal, axis=1, keepdims=True) / rows + epsilon)
    return gram / down / along / rows, along


def pivot_panel(tiles, cols, lane, row):
    height = len(tiles[0])
    sub = tiles[0][0].shape[0]

    def columns(first):
        return [
            [jnp.broadcast_to(tile[:, k:k + 1], tile.shape) for tile in tiles[0]]
            for k in range(first, first + cols)
        ]

    def take(pieces, k):
        at = k % sub
        return pieces[k // sub][at:at + 1, :]

    def step(pieces, firsts, seconds, k, new_first, new_second, clear=None):
        out = []
        for g in range(height):
            base = pieces[g] if clear is None else jnp.where(clear, 0.0, pieces[g])
            value = base - firsts[g] * new_first - seconds[g] * new_second
            if g == k // sub:
                value = jnp.where(row == k % sub, new_first, value)
                value = jnp.where(row == k % sub + 1, new_second, value)
            out.append(value)
        return out

    now = columns(0)
    later = None
    for start in range(0, height * sub, cols):
        for j in range(0, cols, 2):
            k = start + j
            if j == cols - 2 and start + cols < height * sub:
                later = columns(start + cols)
            firsts, seconds = now[j], now[j + 1]
            a, b = take(firsts, k), take(seconds, k)
            c, d = take(firsts, k + 1), take(seconds, k + 1)
            scale = 1.0 / (a * d - b * c)
            a, b, c, d = d * scale, b * scale, c * scale, a * scale
            for i in range(j + 2, cols):
                up, down = take(now[i], k), take(now[i], k + 1)
                now[i] = step(now[i], firsts, seconds, k, a * up - b * down, d * down - c * up)
            if later is not None:
                for i in range(cols):
                    up, down = take(later[i], k), take(later[i], k + 1)
                    later[i] = step(
                        later[i], firsts, seconds, k, a * up - b * down, d * down - c * up
                    )
            for h, pieces in enumerate(tiles):
                up, down = take(pieces, k), take(pieces, k + 1)
                clear = None
                if h == 0:
                    at_up, at_down = lane == k, lane == k + 1
                    clear = at_up | at_down
                    up = jnp.where(at_up[:1], 1.0, jnp.where(at_down[:1], 0.0, up))
                    down = jnp.where(at_down[:1], 1.0, jnp.where(at_up[:1], 0.0, down))
                tiles[h] = step(
                    pieces, firsts, seconds, k, a * up - b * down, d * down - c * up, clear
                )
        now, later = later, None
    return tiles


def sweep_inverse(a_ref, beside=None, first=0, last=None):
    n = a_ref.shape[0]
    sub, wide = 8, 128
    lane = lax.broadcasted_iota(jnp.int32, (PANEL, n), 1)
    tile_lane = lax.broadcasted_iota(jnp.int32, (sub, wide), 1)
    tile_row = lax.broadcasted_iota(jnp.int32, (sub, wide), 0)

    def panel_step(step, carry):
        if beside is not None:
            beside(step)
        before = a_ref[:PANEL, :]
        tiles = [
            [before[g:g + sub, h:h + wide] for g in range(0, PANEL, sub)]
            for h in range(0, n, wide)
        ]
        tiles = pivot_panel(tiles, 8, tile_lane, tile_row)
        panel = jnp.concatenate([jnp.concatenate(pieces, axis=0) for pieces in tiles], axis=1)
        own = lane < PANEL
        update = jnp.where(own, -panel, panel)
        w_high, w_middle, w_low = split_three(before)
        z_high, z_middle, z_low = split_three(update)
        left = jnp.concatenate([w_low, w_middle, w_high, w_middle, w_high, w_high], axis=0)
        right = jnp.concatenate([z_high, z_middle, z_low, z_high, z_middle, z_high], axis=0)
        change = lax.dot_general(
            left, right, (((0,), (0,)), ((), ())), preferred_element_type=f32
        )
        others = jnp.where(own[:1], 0.0, a_ref[PANEL:, :]) - change[PANEL:, :]
        a_ref[:n - PANEL, :] = pltpu.roll(others, n - PANEL, 1)
        a_ref[n - PANEL:, :] = pltpu.roll(update, n - PANEL, 1)
        return carry

    lax.fori_loop(first, n // PANEL if last is None else last, panel_step, 0)


def sweep_kernel(
    edge, list_ref, x_hbm, orb_hbm, nu_hbm, a_out, b_out, c_out, scale_out, room, sems
):
    orb_ref, nu_ref = room["orb"], room["nu"]
    slots = list_ref.shape[1]
    here, size = lax.axis_index("orb"), lax.axis_size("orb")
    mine, count = lax.axis_index("aux"), lax.axis_size("aux")
    rank = nu_ref.shape[2]
    x_buf, parts, table, a_ref, e_ref, part = (
        room[name] for name in ("x", "parts", "table", "a", "e", "part")
    )
    work, even, odd = room["work"], room["even"], room["odd"]
    orb_rows, nu_rows = orb_ref.shape[0] * edge, nu_ref.shape[0] * edge
    first_base = mine * a_ref.shape[0]
    hop_send, hop_recv = sems["hop_send"], sems["hop_recv"]

    def load(slot):
        return pltpu.make_async_copy(x_hbm.at[slot], x_buf.at[slot], sems["x"].at[slot])

    def rows_of(ref, owner=mine):
        rows = ref.shape[0] // count
        return pl.ds(aligned(owner * rows, 8), rows)

    factor_loads = (
        pltpu.make_async_copy(nu_hbm, nu_ref, sems["factors"].at[0]),
        pltpu.make_async_copy(orb_hbm, orb_ref, sems["factors"].at[1]),
    )
    early, late = slots * 3 // 8, slots - 1
    for copy in factor_loads:
        copy.start()
    for slot in range(early):
        load(slot).start()
    enter(("aux", "orb"))
    for slot in range(early, slots):
        load(slot).start()
    for copy in factor_loads:
        copy.wait()
    net = Net(sems["send"], sems["recv"])

    def part_rows(source, slot):
        return parts.at[pl.ds(aligned((source * slots + slot) * edge, edge), edge), :]

    def hop(way, distance, slot):
        rows = part_rows(here - way * distance, slot)
        lane = (1 - way) // 2
        return pltpu.make_async_remote_copy(
            src_ref=rows,
            dst_ref=rows,
            send_sem=hop_send.at[lane, distance, slot],
            recv_sem=hop_recv.at[lane, distance, slot],
            device_id={"orb": here + way},
            device_id_type=MESH,
        )

    def landed(way, distance, slot):
        rows = part_rows(here - way * distance, slot)
        lane = (1 - way) // 2
        return pltpu.make_async_remote_copy(
            src_ref=rows,
            dst_ref=rows,
            send_sem=hop_send.at[lane, distance - 1, slot],
            recv_sem=hop_recv.at[lane, distance - 1, slot],
            device_id={"orb": here - way},
            device_id_type=MESH,
        )

    def place(way):
        return (size - 1) * ((1 - way) // 2) + way * here

    def goes(way, distance):
        at = place(way)
        return (at + size - 1 - distance) // (size - 1) * ((2 * size - 3 - at) // (size - 1)) > 0

    def forward(distance, slot):
        for way in (1, -1):

            @pl.when(goes(way, distance))
            def _():
                landed(way, distance, slot).wait_recv()
                hop(way, distance, slot).start()

    def slot_step(slot, carry):
        load(slot).wait()
        nu_block = nu_ref[list_ref[2, slot]]
        orb_block = orb_ref[lax.rem(list_ref[1, slot], orb_ref.shape[0])]
        group = 4
        total = jnp.zeros((edge, rank), f32)
        for start in range(0, edge, group):
            x_high, x_low = split_two(x_buf[slot, :, start * edge:(start + group) * edge])
            stacked = jnp.concatenate([x_high, x_low], axis=0)
            product = jnp.concatenate(
                [nu_block * orb_block[j:j + 1, :] for j in range(start, start + group)], axis=0
            )
            high, low = split_two(product)
            main = jnp.dot(stacked, high, preferred_element_type=f32)
            rest = jnp.dot(x_high, low, preferred_element_type=f32)
            total += main[:edge] + (main[edge:] + rest)
        live = list_ref[3, slot].astype(f32)
        part_rows(here, slot)[...] = total * live
        for way in (1, -1):

            @pl.when(goes(way, 0))
            def _():
                hop(way, 0, slot).start()

        return carry

    lax.fori_loop(0, early, slot_step, 0)

    half, pieces = slots // 2, 4
    each = slots // pieces
    row = lax.broadcasted_iota(jnp.int32, table.shape[1:], 0)
    for piece in range(pieces):
        own_at = jnp.zeros(table.shape[1:], f32)
        for slot in range(each):
            value = (list_ref[0, piece * each + slot] - first_base).astype(f32)
            own_at = jnp.where(row == slot, value, own_at)
        table[pieces * here + piece] = own_at
    own_table = table.at[pl.ds(pieces * here, pieces)]
    table_copies = [
        net.copy(own_table, own_table, {"orb": (here + step) % size}) for step in range(1, size)
    ]
    orb_gram, orb_land, orb_sum = room["orb_gram"], room["orb_land"], room["orb_sum"]
    orb_gram[...] = gram_rows(orb_ref, even, odd)
    gram_copies = net.share("orb", orb_gram.at[rows_of(orb_gram), :], orb_land)
    room["s_nu"][...] = gram_rows(nu_ref, even, odd) / NU
    lax.fori_loop(early, late, slot_step, 0)
    arrive(gram_copies)
    orb_sum[rows_of(orb_sum), :] = total_of(orb_land)
    gram_copies = net.spread("aux", orb_sum, rank // count)
    lax.fori_loop(late, slots, slot_step, 0)

    arrive(gram_copies)
    ridge = jnp.where(eye_mask(rank), ridge_weight, 0.0)
    work[...] = orb_sum[...] / (orb_rows * size) * room["s_nu"][...] + ridge
    panels = rank // PANEL
    def beside_first(step):
        if size > 2:
            for at in range(-(-slots // panels)):
                slot = step * -(-slots // panels) + at

                @pl.when(slot < slots)
                def _():
                    forward(1, slot)

    sweep_inverse(work, beside_first)
    for at, piece in enumerate(split_three(-work[...])):
        room["inverse"][at] = piece
    arrive(table_copies)

    def add_rows(source, piece, clear):
        start = piece * each
        rows = parts[pl.ds(aligned((source * slots + start) * edge, edge), each * edge), :]
        inverse = tuple(room["inverse"][at] for at in range(3))
        room["q"][...] = dot_exact(split_three(rows), inverse)
        places = table[pieces * source + piece]

        def block_step(block, carry):
            name = jnp.full((1, rank), block, jnp.int32).astype(f32)
            total = jnp.zeros((edge, rank), f32) if clear else a_ref[block]
            for slot in range(each):
                weight = jnp.where(places[slot:slot + 1, :] == name, 1.0, 0.0)
                total += room["q"][slot * edge:(slot + 1) * edge, :] * weight
            a_ref[block] = total
            return carry

        lax.fori_loop(0, a_ref.shape[0], block_step, 0)

    for piece in range(pieces):
        add_rows(here, piece, piece == 0)
        if size > 3:
            forward(2, piece)

    def source_step(at, carry):
        if size > 3:

            @pl.when(at == 1)
            def _():
                for slot in range(pieces, (pieces + slots) // 2):
                    forward(2, slot)

            @pl.when(at == 2)
            def _():
                for slot in range((pieces + slots) // 2, slots):
                    forward(2, slot)
                for far in range(3, size - 1):
                    for slot in range(slots):
                        forward(far, slot)

        distance, way = at // 2 + 1, 1 - at % 2 * 2
        source = here - way * distance

        @pl.when((source + size) // size * ((2 * size - 1 - source) // size) > 0)
        def _():
            def piece_step(piece, carry):
                @pl.when(place(way) == size - 1)
                def _():
                    for slot in range(each):
                        landed(way, distance, piece * each + slot).wait_recv()

                add_rows(source, piece, False)
                return carry

            lax.fori_loop(0, pieces, piece_step, 0)

        return carry

    lax.fori_loop(0, 2 * (size - 1), source_step, 0)
    save_a = pltpu.make_async_copy(a_ref, a_out, sems["save"].at[0])
    save_a.start()

    gram_a, gram_land = room["gram_a"], room["gram_land"]
    room["gram"][...] = gram_rows(a_ref, even, odd)
    gram_copies = net.scatter("aux", room["gram"], gram_land)

    def second_step(slot, carry):
        nu_block = nu_ref[list_ref[2, slot]]
        a_high, a_low = split_two(a_ref[lax.rem(list_ref[0, slot], a_ref.shape[0])])
        weights = jnp.concatenate([a_high, a_high, a_low, a_low], axis=0)
        group = 8
        for start in range(0, edge, group):
            x_high, x_low = split_two(x_buf[slot, :, start * edge:(start + group) * edge])
            turned = jnp.concatenate([x_high, x_low], axis=0).T
            e = jnp.dot(
                jnp.concatenate([turned, turned], axis=1), weights, preferred_element_type=f32
            )
            e_ref[slot, start * edge:(start + group) * edge, :] = e
            part[slot, start:start + group, :] = jnp.sum(
                e.reshape(group, edge, rank) * nu_block[None], axis=1
            )
        return carry

    def gather_blocks(dimension, out_ref, columns=slice(None)):
        blocks = out_ref.shape[0] // edge
        places = [lax.rem(list_ref[dimension, slot], blocks) for slot in range(slots)]
        lives = [list_ref[3, slot].astype(f32) for slot in range(slots)]

        def block_step(block, carry):
            total = jnp.zeros((edge, out_ref.shape[1]), f32)
            for slot in range(slots):
                weight = (places[slot] == block).astype(f32) * lives[slot]
                total += part[slot, :, columns] * weight
            out_ref[pl.ds(aligned(block * edge, edge), edge), :] = total
            return carry

        lax.fori_loop(0, blocks, block_step, 0)

    lax.fori_loop(0, half, second_step, 0)
    arrive(gram_copies)
    gram_a[rows_of(gram_a), :] = total_of(gram_land)
    gram_copies = net.spread("aux", gram_a, rank // count)
    lax.fori_loop(half, slots, second_step, 0)
    gather_blocks(1, room["terms"])
    terms = room["terms"]
    terms_sum = PairScatter(
        net, "aux", lambda owner: terms.at[rows_of(terms, owner), :],
        room["terms_pair"], room["terms_stage"], room["terms_land"]
    )
    terms_sum.start()

    arrive(gram_copies)
    unit_a, scale_a = unit_gram(gram_a[...], P_SIZE)
    work[...] = unit_a * room["s_nu"][...] + ridge

    def beside_second(step):
        @pl.when(step == 1)
        def _():
            terms_sum.relay()

    sweep_inverse(work, beside_second)
    inverse = split_three(-work[...])
    b_full, b_blocks = room["b"], room["b_blocks"]
    b_full[rows_of(b_full), :] = dot_exact(
        split_three(terms_sum.total() / scale_a), inverse
    )
    even[...] = jnp.zeros_like(even)
    odd[...] = jnp.zeros_like(odd)

    def b_landed(owner):
        gram_add(b_full[rows_of(b_full, owner), :], even, odd)

    b_spread = PairSpread(net, "aux", lambda owner: b_full.at[rows_of(b_full, owner), :])
    b_spread.start()
    b_landed(mine)
    b_spread.relay(b_landed)
    b_spread.collect(b_landed)
    gram_b = room["gram_b"]
    cross = odd[...]
    gram_b[...] = even[...] + (cross + cross.T)
    z_copies = net.share("orb", gram_b.at[rows_of(gram_b), :], room["z_land"])
    save_b = pltpu.make_async_copy(b_full, b_out, sems["save"].at[1])
    save_b.start()
    b_blocks[...] = b_full[...].reshape(b_blocks.shape)

    gram_sum = room["gram_sum"]
    thirds, thirds_land, thirds_z, third_sums = (
        room[name] for name in ("thirds", "thirds_land", "thirds_z", "third_sums")
    )
    wide = rank // 2

    def third_half(side):
        columns = slice(side * wide, (side + 1) * wide)

        def third_step(slot, carry):
            b_block = b_blocks[lax.rem(list_ref[1, slot], b_blocks.shape[0])][:, columns]
            total = jnp.zeros((edge, wide), f32)
            for j in range(edge):
                total += e_ref[slot, j * edge:(j + 1) * edge, columns] * b_block[j:j + 1, :]
            part[slot, :, columns] = total
            return carry

        lax.fori_loop(0, slots, third_step, 0)
        gather_blocks(2, thirds.at[side], columns)

    def third_spread(side):
        full = third_sums.at[side]
        rows = nu_rows // count
        return PairSpread(
            net, "aux", lambda owner: full.at[pl.ds(aligned(owner * rows, 8), rows), :]
        )

    third_half(0)
    third_copies = [net.scatter("aux", thirds.at[0], thirds_land.at[0])]
    third_half(1)
    arrive(z_copies)
    gram_sum[rows_of(gram_sum), :] = total_of(room["z_land"])
    gram_spread = PairSpread(net, "aux", lambda owner: gram_sum.at[rows_of(gram_sum, owner), :])
    gram_spread.start()
    third_copies.append(net.scatter("aux", thirds.at[1], thirds_land.at[1]))
    shares, spreads = [], []
    for side in range(2):
        own = thirds_land.at[side, mine]
        shares.append(
            [
                net.plan(own, thirds_z.at[side, here], {"orb": (here + step) % size})
                for step in range(1, size)
            ]
        )
        spreads.append(third_spread(side))

    def third_landed(side):
        arrive(third_copies[side])
        total = total_of(thirds_land.at[side])
        thirds_land[side, mine] = total
        thirds_z[side, here] = total
        for copy in shares[side]:
            copy.start()

    def third_summed(side):
        arrive(shares[side])
        third_sums[side, pl.ds(aligned(mine * (nu_rows // count), 8), nu_rows // count), :] = (
            total_of(thirds_z.at[side])
        )
        spreads[side].start()

    gram_spread.relay()
    third_landed(0)
    gram_spread.collect()
    unit_b, scale_b = unit_gram(gram_sum[...], orb_rows * size)
    work[...] = unit_b * unit_gram(gram_a[...], P_SIZE)[0] + ridge

    def beside_third(step):
        for when, act, side in (
            (2, third_landed, 1), (panels - 3, third_summed, 0), (panels - 1, third_summed, 1)
        ):

            @pl.when(step == when)
            def _():
                act(side)

    sweep_inverse(work, beside_third)
    inverse = split_three(-work[...])
    for spread in spreads:
        spread.relay()
    for spread in spreads:
        spread.collect()
    third_all = jnp.concatenate([third_sums[0], third_sums[1]], axis=1)
    c_new = dot_exact(split_three(third_all / scale_a / scale_b), inverse)
    scale_c = jnp.sqrt(jnp.sum(c_new * c_new, axis=0, keepdims=True) / nu_rows + epsilon)
    c_out[...] = c_new
    scale_out[0:1, :] = scale_a
    scale_out[1:2, :] = scale_b
    scale_out[2:3, :] = scale_c

    def last(slot, carry):
        for way in (1, -1):
            for distance in range(size - 1):

                @pl.when(goes(way, distance))
                def _():
                    hop(way, distance, slot).wait_send()

        return carry

    lax.fori_loop(0, slots, last, 0)
    save_a.wait()
    save_b.wait()
    net.finish()


def scale_kernel(a_hbm, b_hbm, c_hbm, scale_ref, a_out, b_out, c_out, a, b, c, load_sem, save_sem):
    pieces = []
    for at, (source, target, buffer) in enumerate(
        ((a_hbm, a_out, a), (b_hbm, b_out, b), (c_hbm, c_out, c))
    ):
        step = min(512, buffer.shape[0])
        for start in range(0, buffer.shape[0], step):
            number = len(pieces)
            rows = pl.ds(start, step)
            pieces.append(
                (
                    at,
                    buffer,
                    rows,
                    pltpu.make_async_copy(
                        source.at[rows, :], buffer.at[rows, :], load_sem.at[number]
                    ),
                    pltpu.make_async_copy(
                        buffer.at[rows, :], target.at[rows, :], save_sem.at[number]
                    ),
                )
            )
    for piece in pieces:
        piece[3].start()
    for at, buffer, rows, load, save in pieces:
        load.wait()
        buffer[rows, :] = buffer[rows, :] / scale_ref[at:at + 1, :]
        save.start()
    for piece in pieces:
        piece[4].wait()


def per_device(tiles, tile_list, orb_factor, nu_factor):
    slots, edge, tile_width = tiles.shape
    rank = nu_factor.shape[1]
    aux_size, orb_size = lax.axis_size("aux"), lax.axis_size("orb")
    first_rows = P_SIZE // aux_size
    orb_rows, nu_rows = orb_factor.shape[0], nu_factor.shape[0]
    square = (rank, rank)
    shapes = {
        "x": (slots, edge, tile_width),
        "orb": (orb_rows // edge, edge, rank),
        "nu": (nu_rows // edge, edge, rank),
        "parts": (orb_size * slots * edge, rank),
        "table": (orb_size * 4, 8, rank),
        "a": (first_rows // edge, edge, rank),
        "e": (slots, tile_width, rank),
        "part": (slots, edge, rank),
        "q": (slots // 4 * edge, rank),
        "orb_land": (orb_size, rank // aux_size, rank),
        "gram_land": (aux_size, rank // aux_size, rank),
        "terms": (orb_rows, rank),
        "terms_pair": (aux_size // 2, orb_rows // aux_size, rank),
        "terms_stage": (aux_size // 2, orb_rows // aux_size, rank),
        "terms_land": (aux_size // 2, orb_rows // aux_size, rank),
        "b": (orb_rows, rank),
        "b_blocks": (orb_rows // edge, edge, rank),
        "z_land": (orb_size, rank // aux_size, rank),
        "thirds": (2, nu_rows, rank // 2),
        "thirds_land": (2, aux_size, nu_rows // aux_size, rank // 2),
        "thirds_z": (2, orb_size, nu_rows // aux_size, rank // 2),
        "third_sums": (2, nu_rows, rank // 2),
    }
    for name in ("work", "even", "odd", "orb_gram", "orb_sum", "s_nu", "gram", "gram_a", "gram_b", "gram_sum"):
        shapes[name] = square
    net_count = 10 * (aux_size - 1) + 5 * (orb_size - 1)
    dma = pltpu.SemaphoreType.DMA
    semaphores = {
        "x": dma((slots,)),
        "factors": dma((2,)),
        "send": dma((net_count,)),
        "recv": dma((net_count,)),
        "hop_send": dma((2, orb_size - 1, slots)),
        "hop_recv": dma((2, orb_size - 1, slots)),
        "save": dma((2,)),
    }
    room = {name: pltpu.VMEM(shape, f32) for name, shape in shapes.items()}
    room["inverse"] = pltpu.VMEM((3,) + square, bf16)
    vmem = pl.BlockSpec(memory_space=pltpu.VMEM)
    hbm = pl.BlockSpec(memory_space=pltpu.HBM)

    def kernel(list_ref, x_hbm, orb_hbm, nu_hbm, a_out, b_out, c_out, scale_out, *scratch):
        names = list(room)
        sweep_kernel(
            edge, list_ref, x_hbm, orb_hbm, nu_hbm, a_out, b_out, c_out, scale_out,
            dict(zip(names, scratch)), dict(zip(semaphores, scratch[len(names):]))
        )

    a_new, b_new, c_new, scales = pl.pallas_call(
        kernel,
        out_shape=(
            jax.ShapeDtypeStruct((first_rows // edge, edge, rank), f32),
            jax.ShapeDtypeStruct((orb_rows, rank), f32),
            jax.ShapeDtypeStruct((nu_rows, rank), f32),
            jax.ShapeDtypeStruct((8, rank), f32),
        ),
        in_specs=[pl.BlockSpec(memory_space=pltpu.SMEM), hbm, hbm, hbm],
        out_specs=(hbm, hbm, vmem, vmem),
        scratch_shapes=list(room.values()) + list(semaphores.values()),
        compiler_params=pltpu.CompilerParams(
            collective_id=5, has_side_effects=True, vmem_limit_bytes=62 << 20
        ),
        name="sweep",
    )(tile_list, tiles, orb_factor.reshape(-1, edge, rank), nu_factor.reshape(-1, edge, rank))
    rows = (first_rows, orb_rows, nu_rows)
    count = sum(-(-size // 512) for size in rows)
    return pl.pallas_call(
        scale_kernel,
        out_shape=tuple(jax.ShapeDtypeStruct((size, rank), f32) for size in rows),
        in_specs=[hbm, hbm, hbm, vmem],
        out_specs=(hbm, hbm, hbm),
        scratch_shapes=[pltpu.VMEM((size, rank), f32) for size in rows]
        + [dma((count,)), dma((count,))],
        compiler_params=pltpu.CompilerParams(vmem_limit_bytes=60 << 20),
        name="scale",
    )(a_new.reshape(first_rows, rank), b_new, c_new, scales)


def solution(mesh):
    return jax.shard_map(
        per_device,
        mesh=mesh,
        in_specs=(P(("aux", "orb"), None, None), P(None, ("aux", "orb")), P("orb", None), P()),
        out_specs=(P("aux", None), P("orb", None), P()),
        check_vma=False,
    )
```

```python
import functools

import jax
import jax.numpy as jnp
from jax import lax
from jax.experimental import pallas as pl
from jax.experimental.pallas import tpu as pltpu
from jax.sharding import PartitionSpec as P

P_SIZE = 16384
MU = 4096
NU = 512

ridge_weight = 0.5
epsilon = 1e-06
highest = lax.Precision.HIGHEST
f32 = jnp.float32
bf16 = jnp.bfloat16
PANEL = 32


MESH = pl.DeviceIdType.MESH


def split_two(x):
    high = x.astype(bf16)
    return high, (x - high.astype(f32)).astype(bf16)


def split_three(x):
    high = x.astype(bf16)
    rest = x - high.astype(f32)
    middle = rest.astype(bf16)
    return high, middle, (rest - middle.astype(f32)).astype(bf16)


def aligned(value, step):
    return pl.multiple_of(value, step)


def dot_t(left, right):
    return lax.dot_general(left, right, (((0,), (0,)), ((), ())), preferred_element_type=f32)


def dot_exact(left, right):
    l_high, l_middle, l_low = left
    r_high, r_middle, r_low = right
    dot = functools.partial(jnp.dot, preferred_element_type=f32)
    small = dot(l_low, r_high) + dot(l_high, r_low) + dot(l_middle, r_middle)
    return dot(l_high, r_high) + (dot(l_middle, r_high) + dot(l_high, r_middle) + small)


def gram_add(x, even_ref, odd_ref):
    high, middle, low = split_three(x)
    even_ref[...] += dot_t(high, high) + dot_t(middle, middle)
    odd_ref[...] += dot_t(high, middle) + dot_t(high, low)


def gram_rows(x_ref, even_ref, odd_ref):
    even_ref[...] = jnp.zeros_like(even_ref)
    odd_ref[...] = jnp.zeros_like(odd_ref)
    group = min(8, x_ref.shape[0])

    def step(at, carry):
        rows = x_ref[pl.ds(at * group, group)]
        gram_add(rows.reshape(-1, rows.shape[2]), even_ref, odd_ref)
        return carry

    lax.fori_loop(0, x_ref.shape[0] // group, step, 0)
    odd = odd_ref[...]
    return even_ref[...] + (odd + odd.T)


def enter(axes):
    barrier = pltpu.get_barrier_semaphore()
    count = 0
    for axis in axes:
        size, here = lax.axis_size(axis), lax.axis_index(axis)
        for step in range(1, size):
            pl.semaphore_signal(
                barrier, inc=1, device_id={axis: (here + step) % size}, device_id_type=MESH
            )
            count += 1
    pl.semaphore_wait(barrier, count)


class Net:
    def __init__(self, send, recv):
        self.send, self.recv, self.copies = send, recv, []

    def plan(self, src, dst, to):
        at = len(self.copies)
        copy = pltpu.make_async_remote_copy(
            src_ref=src,
            dst_ref=dst,
            send_sem=self.send.at[at],
            recv_sem=self.recv.at[at],
            device_id=to,
            device_id_type=MESH,
        )
        self.copies.append(copy)
        return copy

    def copy(self, src, dst, to):
        copy = self.plan(src, dst, to)
        copy.start()
        return copy

    def scatter(self, axis, src, land):
        size, here = lax.axis_size(axis), lax.axis_index(axis)
        rows = land.shape[1]
        land[here] = src[pl.ds(aligned(here * rows, 8), rows), :]
        copies = []
        for step in range(1, size):
            to = (here + step) % size
            block = src.at[pl.ds(aligned(to * rows, 8), rows), :]
            copies.append(self.copy(block, land.at[here], {axis: to}))
        return copies

    def share(self, axis, src, land):
        size, here = lax.axis_size(axis), lax.axis_index(axis)
        land[here] = src[...]
        return [
            self.copy(src, land.at[here], {axis: (here + step) % size}) for step in range(1, size)
        ]

    def spread(self, axis, full, rows):
        size, here = lax.axis_size(axis), lax.axis_index(axis)
        own = full.at[pl.ds(aligned(here * rows, 8), rows), :]
        return [self.copy(own, own, {axis: (here + step) % size}) for step in range(1, size)]

    def finish(self):
        for copy in self.copies:
            copy.wait_send()


class PairSpread:
    def __init__(self, net, axis, block):
        size, here = lax.axis_size(axis), lax.axis_index(axis)
        chips, chip, core = size // 2, here // 2, here % 2
        other = here + 1 - 2 * core
        self.own = here
        self.near_from = [chip * 2 + 1 - core]
        self.far_from, self.far, self.relays = [], [], []
        own = block(here)
        self.near = [net.plan(own, own, {axis: other})]
        for step in range(1, chips):
            target = (chip + step) % chips * 2 + core
            self.far.append(net.plan(own, own, {axis: target}))
            source = (chip + chips - step) % chips * 2
            self.far_from.append(source + core)
            self.near_from.append(source + 1 - core)
            passed = block(source + core)
            self.near.append(net.plan(passed, passed, {axis: other}))

    def start(self):
        for copy in self.far:
            copy.start()
        self.near[0].start()

    def relay(self, landed=None):
        for copy, near, owner in zip(self.far, self.near[1:], self.far_from):
            copy.wait_recv()
            near.start()
            if landed is not None:
                landed(owner)

    def collect(self, landed=None):
        for copy, owner in zip(self.near, self.near_from):
            copy.wait_recv()
            if landed is not None:
                landed(owner)


class PairScatter:
    def __init__(self, net, axis, block, pair, stage, land):
        size, here = lax.axis_size(axis), lax.axis_index(axis)
        chips, chip, core = size // 2, here // 2, here % 2
        other = here + 1 - 2 * core
        self.chip, self.land, self.pair, self.stage = chip, land, pair, stage
        self.first, self.second, self.targets = [], [], []
        for step in range(1, chips + 1):
            target = (chip + step) % chips
            self.targets.append((target, block(target * 2 + core)))
            away = block(target * 2 + 1 - core)
            self.first.append(net.plan(away, pair.at[target], {axis: other}))
            if step < chips:
                self.second.append(
                    net.plan(stage.at[target], land.at[chip], {axis: target * 2 + core})
                )

    def start(self):
        for copy in self.first:
            copy.start()

    def relay(self):
        for copy, send, (target, own) in zip(self.first, self.second, self.targets):
            copy.wait_recv()
            self.stage[target] = own[...] + self.pair[target]
            send.start()
        self.first[-1].wait_recv()
        target, own = self.targets[-1]
        self.land[self.chip] = own[...] + self.pair[target]

    def total(self):
        arrive(self.second)
        return total_of(self.land)


def arrive(copies):
    for copy in copies:
        copy.wait_recv()


def total_of(land):
    total = land[0]
    for at in range(1, land.shape[0]):
        total += land[at]
    return total


def eye_mask(n):
    return lax.broadcasted_iota(jnp.int32, (n, n), 0) == lax.broadcasted_iota(jnp.int32, (n, n), 1)


def unit_gram(gram, rows):
    diagonal = jnp.where(eye_mask(gram.shape[0]), gram, 0.0)
    along = jnp.sqrt(jnp.sum(diagonal, axis=0, keepdims=True) / rows + epsilon)
    down = jnp.sqrt(jnp.sum(diagonal, axis=1, keepdims=True) / rows + epsilon)
    return gram / down / along / rows, along


def pivot_panel(tiles, cols, lane, row):
    height = len(tiles[0])
    sub = tiles[0][0].shape[0]

    def columns(first):
        return [
            [jnp.broadcast_to(tile[:, k:k + 1], tile.shape) for tile in tiles[0]]
            for k in range(first, first + cols)
        ]

    def take(pieces, k):
        at = k % sub
        return pieces[k // sub][at:at + 1, :]

    def step(pieces, firsts, seconds, k, new_first, new_second, clear=None):
        out = []
        for g in range(height):
            base = pieces[g] if clear is None else jnp.where(clear, 0.0, pieces[g])
            value = base - firsts[g] * new_first - seconds[g] * new_second
            if g == k // sub:
                value = jnp.where(row == k % sub, new_first, value)
                value = jnp.where(row == k % sub + 1, new_second, value)
            out.append(value)
        return out

    now = columns(0)
    later = None
    for start in range(0, height * sub, cols):
        for j in range(0, cols, 2):
            k = start + j
            if j == cols - 2 and start + cols < height * sub:
                later = columns(start + cols)
            firsts, seconds = now[j], now[j + 1]
            a, b = take(firsts, k), take(seconds, k)
            c, d = take(firsts, k + 1), take(seconds, k + 1)
            scale = 1.0 / (a * d - b * c)
            a, b, c, d = d * scale, b * scale, c * scale, a * scale
            for i in range(j + 2, cols):
                up, down = take(now[i], k), take(now[i], k + 1)
                now[i] = step(now[i], firsts, seconds, k, a * up - b * down, d * down - c * up)
            if later is not None:
                for i in range(cols):
                    up, down = take(later[i], k), take(later[i], k + 1)
                    later[i] = step(
                        later[i], firsts, seconds, k, a * up - b * down, d * down - c * up
                    )
            for h, pieces in enumerate(tiles):
                up, down = take(pieces, k), take(pieces, k + 1)
                clear = None
                if h == 0:
                    at_up, at_down = lane == k, lane == k + 1
                    clear = at_up | at_down
                    up = jnp.where(at_up[:1], 1.0, jnp.where(at_down[:1], 0.0, up))
                    down = jnp.where(at_down[:1], 1.0, jnp.where(at_up[:1], 0.0, down))
                tiles[h] = step(
                    pieces, firsts, seconds, k, a * up - b * down, d * down - c * up, clear
                )
        now, later = later, None
    return tiles


def sweep_inverse(a_ref, beside=None, first=0, last=None):
    n = a_ref.shape[0]
    sub, wide = 8, 128
    lane = lax.broadcasted_iota(jnp.int32, (PANEL, n), 1)
    tile_lane = lax.broadcasted_iota(jnp.int32, (sub, wide), 1)
    tile_row = lax.broadcasted_iota(jnp.int32, (sub, wide), 0)

    def panel_step(step, carry):
        if beside is not None:
            beside(step)
        before = a_ref[:PANEL, :]
        tiles = [
            [before[g:g + sub, h:h + wide] for g in range(0, PANEL, sub)]
            for h in range(0, n, wide)
        ]
        tiles = pivot_panel(tiles, 8, tile_lane, tile_row)
        panel = jnp.concatenate([jnp.concatenate(pieces, axis=0) for pieces in tiles], axis=1)
        own = lane < PANEL
        update = jnp.where(own, -panel, panel)
        w_high, w_middle, w_low = split_three(before)
        z_high, z_middle, z_low = split_three(update)
        left = jnp.concatenate([w_low, w_middle, w_high, w_middle, w_high, w_high], axis=0)
        right = jnp.concatenate([z_high, z_middle, z_low, z_high, z_middle, z_high], axis=0)
        change = lax.dot_general(
            left, right, (((0,), (0,)), ((), ())), preferred_element_type=f32
        )
        others = jnp.where(own[:1], 0.0, a_ref[PANEL:, :]) - change[PANEL:, :]
        a_ref[:n - PANEL, :] = pltpu.roll(others, n - PANEL, 1)
        a_ref[n - PANEL:, :] = pltpu.roll(update, n - PANEL, 1)
        return carry

    lax.fori_loop(first, n // PANEL if last is None else last, panel_step, 0)


def sweep_kernel(
    edge, list_ref, x_hbm, orb_hbm, nu_hbm, a_out, b_out, c_out, scale_out, room, sems
):
    orb_ref, nu_ref = room["orb"], room["nu"]
    slots = list_ref.shape[1]
    here, size = lax.axis_index("orb"), lax.axis_size("orb")
    mine, count = lax.axis_index("aux"), lax.axis_size("aux")
    rank = nu_ref.shape[2]
    x_buf, parts, table, a_ref, e_ref, part = (
        room[name] for name in ("x", "parts", "table", "a", "e", "part")
    )
    work, even, odd = room["work"], room["even"], room["odd"]
    orb_rows, nu_rows = orb_ref.shape[0] * edge, nu_ref.shape[0] * edge
    first_base = mine * a_ref.shape[0]
    hop_send, hop_recv = sems["hop_send"], sems["hop_recv"]

    def load(slot):
        return pltpu.make_async_copy(x_hbm.at[slot], x_buf.at[slot], sems["x"].at[slot])

    def rows_of(ref, owner=mine):
        rows = ref.shape[0] // count
        return pl.ds(aligned(owner * rows, 8), rows)

    factor_loads = (
        pltpu.make_async_copy(nu_hbm, nu_ref, sems["factors"].at[0]),
        pltpu.make_async_copy(orb_hbm, orb_ref, sems["factors"].at[1]),
    )
    early, late = slots * 3 // 8, slots - 1
    for copy in factor_loads:
        copy.start()
    for slot in range(early):
        load(slot).start()
    enter(("aux", "orb"))
    for slot in range(early, slots):
        load(slot).start()
    for copy in factor_loads:
        copy.wait()
    net = Net(sems["send"], sems["recv"])

    def part_rows(source, slot):
        return parts.at[pl.ds(aligned((source * slots + slot) * edge, edge), edge), :]

    def hop(way, distance, slot):
        rows = part_rows(here - way * distance, slot)
        lane = (1 - way) // 2
        return pltpu.make_async_remote_copy(
            src_ref=rows,
            dst_ref=rows,
            send_sem=hop_send.at[lane, distance, slot],
            recv_sem=hop_recv.at[lane, distance, slot],
            device_id={"orb": here + way},
            device_id_type=MESH,
        )

    def landed(way, distance, slot):
        rows = part_rows(here - way * distance, slot)
        lane = (1 - way) // 2
        return pltpu.make_async_remote_copy(
            src_ref=rows,
            dst_ref=rows,
            send_sem=hop_send.at[lane, distance - 1, slot],
            recv_sem=hop_recv.at[lane, distance - 1, slot],
            device_id={"orb": here - way},
            device_id_type=MESH,
        )

    def place(way):
        return (size - 1) * ((1 - way) // 2) + way * here

    def goes(way, distance):
        at = place(way)
        return (at + size - 1 - distance) // (size - 1) * ((2 * size - 3 - at) // (size - 1)) > 0

    def forward(distance, slot):
        for way in (1, -1):

            @pl.when(goes(way, distance))
            def _():
                landed(way, distance, slot).wait_recv()
                hop(way, distance, slot).start()

    def slot_step(slot, carry):
        load(slot).wait()
        nu_block = nu_ref[list_ref[2, slot]]
        orb_block = orb_ref[lax.rem(list_ref[1, slot], orb_ref.shape[0])]
        group = 4
        total = jnp.zeros((edge, rank), f32)
        for start in range(0, edge, group):
            x_high, x_low = split_two(x_buf[slot, :, start * edge:(start + group) * edge])
            stacked = jnp.concatenate([x_high, x_low], axis=0)
            product = jnp.concatenate(
                [nu_block * orb_block[j:j + 1, :] for j in range(start, start + group)], axis=0
            )
            high, low = split_two(product)
            main = jnp.dot(stacked, high, preferred_element_type=f32)
            rest = jnp.dot(x_high, low, preferred_element_type=f32)
            total += main[:edge] + (main[edge:] + rest)
        live = list_ref[3, slot].astype(f32)
        part_rows(here, slot)[...] = total * live
        for way in (1, -1):

            @pl.when(goes(way, 0))
            def _():
                hop(way, 0, slot).start()

        return carry

    lax.fori_loop(0, early, slot_step, 0)

    half, pieces = slots // 2, 4
    each = slots // pieces
    row = lax.broadcasted_iota(jnp.int32, table.shape[1:], 0)
    for piece in range(pieces):
        own_at = jnp.zeros(table.shape[1:], f32)
        for slot in range(each):
            value = (list_ref[0, piece * each + slot] - first_base).astype(f32)
            own_at = jnp.where(row == slot, value, own_at)
        table[pieces * here + piece] = own_at
    own_table = table.at[pl.ds(pieces * here, pieces)]
    table_copies = [
        net.copy(own_table, own_table, {"orb": (here + step) % size}) for step in range(1, size)
    ]
    orb_gram, orb_land, orb_sum = room["orb_gram"], room["orb_land"], room["orb_sum"]
    orb_gram[...] = gram_rows(orb_ref, even, odd)
    gram_copies = net.share("orb", orb_gram.at[rows_of(orb_gram), :], orb_land)
    room["s_nu"][...] = gram_rows(nu_ref, even, odd) / NU
    lax.fori_loop(early, late, slot_step, 0)
    arrive(gram_copies)
    orb_sum[rows_of(orb_sum), :] = total_of(orb_land)
    gram_copies = net.spread("aux", orb_sum, rank // count)
    lax.fori_loop(late, slots, slot_step, 0)

    if size > 2:

        def pass_near(slot, carry):
            forward(1, slot)
            return carry

        lax.fori_loop(0, half, pass_near, 0)
    arrive(gram_copies)
    ridge = jnp.where(eye_mask(rank), ridge_weight, 0.0)
    work[...] = orb_sum[...] / (orb_rows * size) * room["s_nu"][...] + ridge
    panels = rank // PANEL
    def beside_first(step):
        if size > 2:
            for at in range(-(-half // panels)):
                slot = half + step * -(-half // panels) + at

                @pl.when(slot < slots)
                def _():
                    forward(1, slot)

    sweep_inverse(work, beside_first)
    for at, piece in enumerate(split_three(-work[...])):
        room["inverse"][at] = piece
    arrive(table_copies)

    def add_rows(source, piece, clear):
        start = piece * each
        rows = parts[pl.ds(aligned((source * slots + start) * edge, edge), each * edge), :]
        inverse = tuple(room["inverse"][at] for at in range(3))
        room["q"][...] = dot_exact(split_three(rows), inverse)
        places = table[pieces * source + piece]

        def block_step(block, carry):
            name = jnp.full((1, rank), block, jnp.int32).astype(f32)
            total = jnp.zeros((edge, rank), f32) if clear else a_ref[block]
            for slot in range(each):
                weight = jnp.where(places[slot:slot + 1, :] == name, 1.0, 0.0)
                total += room["q"][slot * edge:(slot + 1) * edge, :] * weight
            a_ref[block] = total
            return carry

        lax.fori_loop(0, a_ref.shape[0], block_step, 0)

    for piece in range(pieces):
        if size > 3:
            forward(2, piece)
        add_rows(here, piece, piece == 0)

    def source_step(at, carry):
        if size > 3:

            @pl.when(at == 0)
            def _():
                for slot in range(pieces, (pieces + slots) // 2):
                    forward(2, slot)

            @pl.when(at == 1)
            def _():
                for slot in range((pieces + slots) // 2, slots):
                    forward(2, slot)
                for far in range(3, size - 1):
                    for slot in range(slots):
                        forward(far, slot)

        distance, way = at // 2 + 1, 1 - at % 2 * 2
        source = here - way * distance

        @pl.when((source + size) // size * ((2 * size - 1 - source) // size) > 0)
        def _():
            def piece_step(piece, carry):
                @pl.when(place(way) == size - 1)
                def _():
                    for slot in range(each):
                        landed(way, distance, piece * each + slot).wait_recv()

                add_rows(source, piece, False)
                return carry

            lax.fori_loop(0, pieces, piece_step, 0)

        return carry

    lax.fori_loop(0, 2 * (size - 1), source_step, 0)
    save_a = pltpu.make_async_copy(a_ref, a_out, sems["save"].at[0])
    save_a.start()

    gram_a, gram_land = room["gram_a"], room["gram_land"]
    room["gram"][...] = gram_rows(a_ref, even, odd)
    gram_copies = net.scatter("aux", room["gram"], gram_land)

    def second_step(slot, carry):
        nu_block = nu_ref[list_ref[2, slot]]
        a_high, a_low = split_two(a_ref[lax.rem(list_ref[0, slot], a_ref.shape[0])])
        weights = jnp.concatenate([a_high, a_high, a_low, a_low], axis=0)
        group = 8
        for start in range(0, edge, group):
            x_high, x_low = split_two(x_buf[slot, :, start * edge:(start + group) * edge])
            turned = jnp.concatenate([x_high, x_low], axis=0).T
            e = jnp.dot(
                jnp.concatenate([turned, turned], axis=1), weights, preferred_element_type=f32
            )
            e_ref[slot, start * edge:(start + group) * edge, :] = e
            part[slot, start:start + group, :] = jnp.sum(
                e.reshape(group, edge, rank) * nu_block[None], axis=1
            )
        return carry

    def gather_blocks(dimension, out_ref, columns=slice(None)):
        blocks = out_ref.shape[0] // edge
        places = [lax.rem(list_ref[dimension, slot], blocks) for slot in range(slots)]
        lives = [list_ref[3, slot].astype(f32) for slot in range(slots)]

        def block_step(block, carry):
            total = jnp.zeros((edge, out_ref.shape[1]), f32)
            for slot in range(slots):
                weight = (places[slot] == block).astype(f32) * lives[slot]
                total += part[slot, :, columns] * weight
            out_ref[pl.ds(aligned(block * edge, edge), edge), :] = total
            return carry

        lax.fori_loop(0, blocks, block_step, 0)

    lax.fori_loop(0, half, second_step, 0)
    arrive(gram_copies)
    gram_a[rows_of(gram_a), :] = total_of(gram_land)
    gram_copies = net.spread("aux", gram_a, rank // count)
    lax.fori_loop(half, slots, second_step, 0)
    gather_blocks(1, room["terms"])
    terms = room["terms"]
    terms_sum = PairScatter(
        net, "aux", lambda owner: terms.at[rows_of(terms, owner), :],
        room["terms_pair"], room["terms_stage"], room["terms_land"]
    )
    terms_sum.start()

    arrive(gram_copies)
    unit_a, scale_a = unit_gram(gram_a[...], P_SIZE)
    work[...] = unit_a * room["s_nu"][...] + ridge

    def beside_second(step):
        @pl.when(step == 1)
        def _():
            terms_sum.relay()

    sweep_inverse(work, beside_second)
    inverse = split_three(-work[...])
    b_full, b_blocks = room["b"], room["b_blocks"]
    b_full[rows_of(b_full), :] = dot_exact(
        split_three(terms_sum.total() / scale_a), inverse
    )
    even[...] = jnp.zeros_like(even)
    odd[...] = jnp.zeros_like(odd)

    def b_landed(owner):
        gram_add(b_full[rows_of(b_full, owner), :], even, odd)

    b_spread = PairSpread(net, "aux", lambda owner: b_full.at[rows_of(b_full, owner), :])
    b_spread.start()
    b_landed(mine)
    b_spread.relay(b_landed)
    b_spread.collect(b_landed)
    gram_b = room["gram_b"]
    cross = odd[...]
    gram_b[...] = even[...] + (cross + cross.T)
    z_copies = net.share("orb", gram_b.at[rows_of(gram_b), :], room["z_land"])
    save_b = pltpu.make_async_copy(b_full, b_out, sems["save"].at[1])
    save_b.start()
    b_blocks[...] = b_full[...].reshape(b_blocks.shape)

    gram_sum = room["gram_sum"]
    thirds, thirds_land, thirds_z, third_sums = (
        room[name] for name in ("thirds", "thirds_land", "thirds_z", "third_sums")
    )
    wide = rank // 2

    def third_half(side):
        columns = slice(side * wide, (side + 1) * wide)

        def third_step(slot, carry):
            b_block = b_blocks[lax.rem(list_ref[1, slot], b_blocks.shape[0])][:, columns]
            total = jnp.zeros((edge, wide), f32)
            for j in range(edge):
                total += e_ref[slot, j * edge:(j + 1) * edge, columns] * b_block[j:j + 1, :]
            part[slot, :, columns] = total
            return carry

        lax.fori_loop(0, slots, third_step, 0)
        gather_blocks(2, thirds.at[side], columns)

    def third_spread(side):
        full = third_sums.at[side]
        rows = nu_rows // count
        return PairSpread(
            net, "aux", lambda owner: full.at[pl.ds(aligned(owner * rows, 8), rows), :]
        )

    third_half(0)
    third_copies = [net.scatter("aux", thirds.at[0], thirds_land.at[0])]
    third_half(1)
    arrive(z_copies)
    gram_sum[rows_of(gram_sum), :] = total_of(room["z_land"])
    gram_spread = PairSpread(net, "aux", lambda owner: gram_sum.at[rows_of(gram_sum, owner), :])
    gram_spread.start()
    third_copies.append(net.scatter("aux", thirds.at[1], thirds_land.at[1]))
    shares, spreads = [], []
    for side in range(2):
        own = thirds_land.at[side, mine]
        shares.append(
            [
                net.plan(own, thirds_z.at[side, here], {"orb": (here + step) % size})
                for step in range(1, size)
            ]
        )
        spreads.append(third_spread(side))

    def third_landed(side):
        arrive(third_copies[side])
        total = total_of(thirds_land.at[side])
        thirds_land[side, mine] = total
        thirds_z[side, here] = total
        for copy in shares[side]:
            copy.start()

    def third_summed(side):
        arrive(shares[side])
        third_sums[side, pl.ds(aligned(mine * (nu_rows // count), 8), nu_rows // count), :] = (
            total_of(thirds_z.at[side])
        )
        spreads[side].start()

    gram_spread.relay()
    third_landed(0)
    gram_spread.collect()
    unit_b, scale_b = unit_gram(gram_sum[...], orb_rows * size)
    work[...] = unit_b * unit_gram(gram_a[...], P_SIZE)[0] + ridge

    def beside_third(step):
        for when, act, side in (
            (2, third_landed, 1), (panels - 3, third_summed, 0), (panels - 1, third_summed, 1)
        ):

            @pl.when(step == when)
            def _():
                act(side)

    sweep_inverse(work, beside_third)
    inverse = split_three(-work[...])
    for spread in spreads:
        spread.relay()
    for spread in spreads:
        spread.collect()
    third_all = jnp.concatenate([third_sums[0], third_sums[1]], axis=1)
    c_new = dot_exact(split_three(third_all / scale_a / scale_b), inverse)
    scale_c = jnp.sqrt(jnp.sum(c_new * c_new, axis=0, keepdims=True) / nu_rows + epsilon)
    c_out[...] = c_new
    scale_out[0:1, :] = scale_a
    scale_out[1:2, :] = scale_b
    scale_out[2:3, :] = scale_c

    def last(slot, carry):
        for way in (1, -1):
            for distance in range(size - 1):

                @pl.when(goes(way, distance))
                def _():
                    hop(way, distance, slot).wait_send()

        return carry

    lax.fori_loop(0, slots, last, 0)
    save_a.wait()
    save_b.wait()
    net.finish()


def scale_kernel(a_hbm, b_hbm, c_hbm, scale_ref, a_out, b_out, c_out, a, b, c, load_sem, save_sem):
    pieces = []
    for at, (source, target, buffer) in enumerate(
        ((a_hbm, a_out, a), (b_hbm, b_out, b), (c_hbm, c_out, c))
    ):
        step = min(512, buffer.shape[0])
        for start in range(0, buffer.shape[0], step):
            number = len(pieces)
            rows = pl.ds(start, step)
            pieces.append(
                (
                    at,
                    buffer,
                    rows,
                    pltpu.make_async_copy(
                        source.at[rows, :], buffer.at[rows, :], load_sem.at[number]
                    ),
                    pltpu.make_async_copy(
                        buffer.at[rows, :], target.at[rows, :], save_sem.at[number]
                    ),
                )
            )
    for piece in pieces:
        piece[3].start()
    for at, buffer, rows, load, save in pieces:
        load.wait()
        buffer[rows, :] = buffer[rows, :] / scale_ref[at:at + 1, :]
        save.start()
    for piece in pieces:
        piece[4].wait()


def per_device(tiles, tile_list, orb_factor, nu_factor):
    slots, edge, tile_width = tiles.shape
    rank = nu_factor.shape[1]
    aux_size, orb_size = lax.axis_size("aux"), lax.axis_size("orb")
    first_rows = P_SIZE // aux_size
    orb_rows, nu_rows = orb_factor.shape[0], nu_factor.shape[0]
    square = (rank, rank)
    shapes = {
        "x": (slots, edge, tile_width),
        "orb": (orb_rows // edge, edge, rank),
        "nu": (nu_rows // edge, edge, rank),
        "parts": (orb_size * slots * edge, rank),
        "table": (orb_size * 4, 8, rank),
        "a": (first_rows // edge, edge, rank),
        "e": (slots, tile_width, rank),
        "part": (slots, edge, rank),
        "q": (slots // 4 * edge, rank),
        "orb_land": (orb_size, rank // aux_size, rank),
        "gram_land": (aux_size, rank // aux_size, rank),
        "terms": (orb_rows, rank),
        "terms_pair": (aux_size // 2, orb_rows // aux_size, rank),
        "terms_stage": (aux_size // 2, orb_rows // aux_size, rank),
        "terms_land": (aux_size // 2, orb_rows // aux_size, rank),
        "b": (orb_rows, rank),
        "b_blocks": (orb_rows // edge, edge, rank),
        "z_land": (orb_size, rank // aux_size, rank),
        "thirds": (2, nu_rows, rank // 2),
        "thirds_land": (2, aux_size, nu_rows // aux_size, rank // 2),
        "thirds_z": (2, orb_size, nu_rows // aux_size, rank // 2),
        "third_sums": (2, nu_rows, rank // 2),
    }
    for name in ("work", "even", "odd", "orb_gram", "orb_sum", "s_nu", "gram", "gram_a", "gram_b", "gram_sum"):
        shapes[name] = square
    net_count = 10 * (aux_size - 1) + 5 * (orb_size - 1)
    dma = pltpu.SemaphoreType.DMA
    semaphores = {
        "x": dma((slots,)),
        "factors": dma((2,)),
        "send": dma((net_count,)),
        "recv": dma((net_count,)),
        "hop_send": dma((2, orb_size - 1, slots)),
        "hop_recv": dma((2, orb_size - 1, slots)),
        "save": dma((2,)),
    }
    room = {name: pltpu.VMEM(shape, f32) for name, shape in shapes.items()}
    room["inverse"] = pltpu.VMEM((3,) + square, bf16)
    vmem = pl.BlockSpec(memory_space=pltpu.VMEM)
    hbm = pl.BlockSpec(memory_space=pltpu.HBM)

    def kernel(list_ref, x_hbm, orb_hbm, nu_hbm, a_out, b_out, c_out, scale_out, *scratch):
        names = list(room)
        sweep_kernel(
            edge, list_ref, x_hbm, orb_hbm, nu_hbm, a_out, b_out, c_out, scale_out,
            dict(zip(names, scratch)), dict(zip(semaphores, scratch[len(names):]))
        )

    a_new, b_new, c_new, scales = pl.pallas_call(
        kernel,
        out_shape=(
            jax.ShapeDtypeStruct((first_rows // edge, edge, rank), f32),
            jax.ShapeDtypeStruct((orb_rows, rank), f32),
            jax.ShapeDtypeStruct((nu_rows, rank), f32),
            jax.ShapeDtypeStruct((8, rank), f32),
        ),
        in_specs=[pl.BlockSpec(memory_space=pltpu.SMEM), hbm, hbm, hbm],
        out_specs=(hbm, hbm, vmem, vmem),
        scratch_shapes=list(room.values()) + list(semaphores.values()),
        compiler_params=pltpu.CompilerParams(
            collective_id=5, has_side_effects=True, vmem_limit_bytes=62 << 20
        ),
        name="sweep",
    )(tile_list, tiles, orb_factor.reshape(-1, edge, rank), nu_factor.reshape(-1, edge, rank))
    rows = (first_rows, orb_rows, nu_rows)
    count = sum(-(-size // 512) for size in rows)
    return pl.pallas_call(
        scale_kernel,
        out_shape=tuple(jax.ShapeDtypeStruct((size, rank), f32) for size in rows),
        in_specs=[hbm, hbm, hbm, vmem],
        out_specs=(hbm, hbm, hbm),
        scratch_shapes=[pltpu.VMEM((size, rank), f32) for size in rows]
        + [dma((count,)), dma((count,))],
        compiler_params=pltpu.CompilerParams(vmem_limit_bytes=60 << 20),
        name="scale",
    )(a_new.reshape(first_rows, rank), b_new, c_new, scales)


def solution(mesh):
    return jax.shard_map(
        per_device,
        mesh=mesh,
        in_specs=(P(("aux", "orb"), None, None), P(None, ("aux", "orb")), P("orb", None), P()),
        out_specs=(P("aux", None), P("orb", None), P()),
        check_vma=False,
    )
```
